32 devices in a mesh: orbit: 4 (over x, core), group: 8 (over z, y).
Axes of the slice: x: 2, y: 2, z: 4, core: 2. Of those that a mesh axis runs over, the one named last changes fastest.
Arguments:
- along_jac: bfloat16 [8, 64, 2, 128, 256], P('group', 'orbit'), may hold values from -0.375 to 0.375
- along_res: float32 [8, 64, 2, 128], P('group', 'orbit'), may hold values from -6 to 6
- along_e: float32 [8, 64, 2, 128], P('group', 'orbit'), may hold values from -6 to 6
- along_count: int32 [8, 64], P('group', 'orbit'), may hold values from 32 to 128, as said below
- damping: float32 [8, 64], P('group', 'orbit'), may hold values from 0.05 to 1
- cross_jac: bfloat16 [8, 256, 2, 128, 256], P('group', 'orbit'), may hold values from -0.375 to 0.375
- cross_res: float32 [8, 256, 2, 128], P('group', 'orbit'), may hold values from -6 to 6
- cross_e: float32 [8, 256, 2, 128], P('group', 'orbit'), may hold values from -6 to 6
- cross_own: int32 [8, 256], P('group', 'orbit'), may hold values from 0 to 15
- cross_group: int32 [8, 256, 1], P('group', 'orbit'), may hold values from 0 to 7; in each aligned block of 64 rows (0 to 63, 64 to 127, ..., all dimensions but the last counted through in order) at most 16 rows name the same one
- cross_other: int32 [8, 256], P('group', 'orbit'), may hold values from 0 to 15
Outputs:
- solution: float32 [8, 64, 256], P('group', 'orbit')
- residual: float32 [8, 64, 256], P('group', 'orbit')
The draws below stay inside these ranges and needn't reach their ends.
Inputs may be any that keep to these rules, and one draw needn't show every extreme that they name: along_count of some scene equals 128 in every draw, and every count is at least 32. `cross_group`: among the 64 crossover blocks of one device no partner group is named more than 16 times, a bound that some block reaches.
All inputs are finite; a program needn't handle non-finite values.
Results may differ from the reference program's by a relative error of at most 0.015.
Values may be sent and summed in bfloat16 or wider, within the bound.
No kernel may reach another device: no remote copies, remote signals or barrier semaphores. Data moves between devices by JAX's collectives and lax.ppermute only.
A program may use at most 64 MiB of HBM per device.

```python
import math
import jax
import jax.numpy as jnp
import numpy as np
from jax import lax

P_SIZE = 256
TIE = 128
SC = 16
XC = 64
ITERS = 4
GROUPS = 8
ALONG = 64
CROSS = 256
CAP = 16


def draw_along_count(key, part):
    first, second = jax.random.split(key)
    counts = jax.random.randint(first, (GROUPS * ALONG,), TIE // 4, TIE + 1)
    where_full = jax.random.randint(second, (), 0, GROUPS * ALONG)
    counts = counts.at[where_full].set(TIE)
    return counts.reshape(GROUPS, ALONG).astype(jnp.int32)


def with_ends(values, stream_key, low, largest):
    extent = values.shape
    spot = [jax.random.randint(jax.random.fold_in(stream_key, axis), (), 0, extent[axis]) for axis in range(len(extent))]
    values = values.at[tuple(spot)].set(low)
    longest = extent.index(max(extent))
    spot[longest] = (spot[longest] + 1) % extent[longest]
    return values.at[tuple(spot)].set(largest)


def shard_levels(stream_key, shape, shards, least, high):
    gain = 1.0
    for dim, shards_of in shards:
        steps = jax.random.uniform(jax.random.fold_in(jax.random.fold_in(stream_key, 6), dim), (shards_of,), jnp.float32, least / len(shards), high / len(shards))
        gain = gain * jnp.repeat(jnp.exp(steps), shape[dim] // shards_of).reshape((-1,) + (1,) * (len(shape) - 1 - dim))
    return gain


def deal_out(own_key, own, number, rows, number_of, top, bound, skew):
    sequence = jax.random.permutation(own_key, number_of)
    heavy_load, ordinary = load_shares(number_of, rows * top, bound, skew, True), load_shares(number_of, rows * top, bound, skew, False)
    places = jnp.arange(number_of)

    def named(tallies, rotation):
        used = int((tallies > 0).sum())
        fixed = max(1, used // 4)
        shifted = fixed + (places - fixed + rotation * (used - fixed)) % max(1, number_of - fixed)
        return jnp.zeros((number_of,), jnp.int32).at[sequence[jnp.where(places < fixed, places, shifted)]].set(jnp.asarray(tallies, jnp.int32))

    tallies = jnp.where(number % 4 == 0, named(heavy_load, number // 4), named(ordinary, number - number // 4 - 1))
    mixed = jax.random.permutation(jax.random.fold_in(own, 3), number_of)
    source_of, sink = mixed[0:number_of // 2 * 2:2], mixed[1:number_of // 2 * 2:2]
    margin = jnp.minimum(tallies[source_of] - 1, bound - tallies[sink]) // 2
    margin = jnp.where((source_of == sequence[0]) | (sink == sequence[0]) | (tallies[sink] == 0), 0, jnp.maximum(margin, 0))
    shifted = jax.random.randint(jax.random.fold_in(own, 4), (number_of // 2,), 0, 1 << 20) % (margin + 1)
    tallies = tallies.at[source_of].add(-shifted).at[sink].add(shifted)
    items = jnp.searchsorted(jnp.cumsum(tallies), jnp.arange(rows * top), side="right").astype(jnp.int32)
    table = items.reshape(top, rows).T
    table = table[jax.random.permutation(jax.random.fold_in(own, 1), rows)]
    rotation = jax.random.randint(jax.random.fold_in(own, 2), (rows, 1), 0, top)
    return jnp.take_along_axis(table, (jnp.arange(top)[None, :] + rotation) % top, axis=1)


def load_shares(number_of, total, most, lean, full):
    weights = [(1 << 20) // math.isqrt(standing ** lean) + 1 for standing in range(1, number_of + 1)]
    largest = most if full else min(most, max(-(-total // number_of), total * weights[0] // sum(weights)))
    least = 1 if total - largest >= number_of - 1 else 0
    given, rest = [largest] + [least] * (number_of - 1), total - largest - least * (number_of - 1)
    while rest > 0:
        candidates = [i for i in range(1, number_of) if given[i] < largest] or [i for i in range(1, number_of) if given[i] < most]
        whole, remaining = sum([weights[i] for i in candidates]), rest
        for i in candidates:
            extra = min(most - given[i], max(1, remaining * weights[i] // whole), rest)
            given[i] = given[i] + extra
            rest = rest - extra
    return np.array(given)


def gaussian(key, shape, width, most, shards=(), held_as=jnp.bfloat16):
    factor_of = shard_levels(key, shape, shards, -0.22, 0.18) if shards else 1.0
    result = jax.random.normal(key, shape, jnp.float32) * width * factor_of
    return jnp.minimum(jnp.maximum(result, -most), most).astype(held_as)


def setup_inputs(seed: int = 0) -> dict:
    arg_keys = jax.random.split(jax.random.key(seed), 12)
    along_jac = gaussian(arg_keys[0], (GROUPS, ALONG, 2, TIE, P_SIZE), P_SIZE ** -0.5, 0.375, ((0, 8), (1, 4)))
    along_res = gaussian(arg_keys[1], (GROUPS, ALONG, 2, TIE), 1.0, 6.0, ((0, 8), (1, 4)), jnp.float32)
    along_e = gaussian(arg_keys[2], (GROUPS, ALONG, 2, TIE), 1.0, 6.0, ((0, 8), (1, 4)), jnp.float32)
    along_count = draw_along_count(jax.random.fold_in(arg_keys[11], 71), 0)
    damping = jnp.clip(jnp.exp(math.log(1.0) - 2.9957323 * jax.random.uniform(arg_keys[4], (GROUPS, ALONG), jnp.float32) ** shard_levels(arg_keys[4], (GROUPS, ALONG), ((0, 8), (1, 4)), -0.2, 0.2)), 0.05, 1.0)
    cross_jac = gaussian(arg_keys[5], (GROUPS, CROSS, 2, TIE, P_SIZE), P_SIZE ** -0.5, 0.375, ((0, 8), (1, 4)))
    cross_res = gaussian(arg_keys[6], (GROUPS, CROSS, 2, TIE), 1.0, 6.0, ((0, 8), (1, 4)), jnp.float32)
    cross_e = gaussian(arg_keys[7], (GROUPS, CROSS, 2, TIE), 1.0, 6.0, ((0, 8), (1, 4)), jnp.float32)
    cross_own = with_ends(jax.random.randint(arg_keys[8], (GROUPS, CROSS), 0, SC), jax.random.fold_in(arg_keys[8], 1), 0, SC - 1).astype(jnp.int32)
    cross_group_keys = jax.random.split(jax.random.fold_in(arg_keys[9], 1), GROUPS * CROSS // XC)
    cross_group_turns = jax.random.permutation(jax.random.fold_in(arg_keys[9], 3), GROUPS * CROSS // XC)
    cross_group = jax.vmap(lambda own, number: deal_out(jax.random.fold_in(arg_keys[9], 2), own, number, XC, GROUPS, 1, CAP, 2))(cross_group_keys, cross_group_turns).reshape((GROUPS, CROSS, 1))
    cross_other = with_ends(jax.random.randint(arg_keys[10], (GROUPS, CROSS), 0, SC), jax.random.fold_in(arg_keys[10], 1), 0, SC - 1).astype(jnp.int32)
    return {"along_jac": along_jac, "along_res": along_res, "along_e": along_e, "along_count": along_count, "damping": damping, "cross_jac": cross_jac, "cross_res": cross_res, "cross_e": cross_e, "cross_own": cross_own, "cross_group": cross_group, "cross_other": cross_other}


def project(item):
    jac, va, vb = item
    jf = jac.astype(jnp.float32)
    r1 = jnp.einsum('btp,bp->bt', jf[:, 0], va)
    r2 = jnp.einsum('btp,bp->bt', jf[:, 1], vb)
    return r1, r2


def settle(item):
    jac, e, r1, r2 = item
    e1 = e[:, 0]
    e2 = e[:, 1]
    z = (e1 * r1 + e2 * r2) / (1.0 + e1 * e1 + e2 * e2)
    q1 = lax.optimization_barrier((r1 - e1 * z).astype(jnp.bfloat16)).astype(jnp.float32)
    q2 = lax.optimization_barrier((r2 - e2 * z).astype(jnp.bfloat16)).astype(jnp.float32)
    jf = jac.astype(jnp.float32)
    t1 = jnp.einsum('btp,bt->bp', jf[:, 0], q1)
    t2 = jnp.einsum('btp,bt->bp', jf[:, 1], q2)
    return t1, t2


def reference(along_jac, along_res, along_e, along_count, damping, cross_jac, cross_res, cross_e, cross_own, cross_group, cross_other):
    live = (jnp.arange(TIE)[None, None, :] < along_count[:, :, None]).astype(jnp.float32)
    orbit_of = (jnp.arange(CROSS) // XC).astype(jnp.int32)
    own_k = orbit_of[None, :] * SC + cross_own
    other_k = orbit_of[None, :] * SC + cross_other
    partner = cross_group[:, :, 0]
    group_of = jnp.broadcast_to(jnp.arange(GROUPS, dtype=jnp.int32)[:, None], (GROUPS, CROSS))

    def backward(a1, a2, c1, c2):
        t1, t2 = lax.map(settle, (along_jac, along_e, a1, a2))
        out = t1 + jnp.roll(t2, 1, axis=1)
        u1, u2 = lax.map(settle, (cross_jac, cross_e, c1, c2))
        out = out.at[group_of, own_k].add(u1)
        out = out.at[partner, other_k].add(u2)
        return out

    def operate(direction):
        vb = lax.optimization_barrier(direction.astype(jnp.bfloat16)).astype(jnp.float32)
        nxt = jnp.roll(vb, -1, axis=1)
        a1, a2 = lax.map(project, (along_jac, vb, nxt))
        va = vb[group_of, own_k]
        vp = vb[partner, other_k]
        c1, c2 = lax.map(project, (cross_jac, va, vp))
        return damping[:, :, None] * direction + backward(a1 * live, a2 * live, c1, c2)

    rhs = -backward(along_res[:, :, 0] * live, along_res[:, :, 1] * live, cross_res[:, :, 0], cross_res[:, :, 1])
    solution = jnp.zeros_like(rhs)
    residual = rhs
    direction = rhs
    norm_now = jnp.sum(residual * residual)
    for step in range(ITERS):
        image = operate(direction)
        alpha = norm_now / jnp.sum(direction * image)
        solution = solution + alpha * direction
        residual = residual - alpha * image
        norm_next = jnp.sum(residual * residual)
        direction = residual + (norm_next / norm_now) * direction
        norm_now = norm_next
    return solution, residual
```

```python
import functools

import jax
import jax.numpy as jnp
from jax import lax
from jax.experimental import pallas as pl
from jax.experimental.pallas import tpu as pltpu
from jax.sharding import PartitionSpec as P

ITERS = 4
F32, BF16 = jnp.float32, jnp.bfloat16
OCTET = 8


def dot(a, b):
    return lax.dot_general(a, b, (((1,), (0,)), ((), ())), preferred_element_type=F32)


def dot_t(a, b):
    return lax.dot_general(a, b, (((1,), (1,)), ((), ())), preferred_element_type=F32)


def halves(x):
    high = x.astype(BF16)
    return high, (x - high.astype(F32)).astype(BF16)


def row_of(shape):
    return lax.broadcasted_iota(jnp.int32, shape, 0)


def octets(refs, body):
    slot = 0
    for ref in refs:
        blocks = ref.shape[0]
        if blocks <= OCTET:
            body(ref, 0, slot, blocks)
        else:

            @pl.loop(0, blocks // OCTET)
            def _(i, ref=ref, slot=slot):
                at = pl.multiple_of(i * OCTET, OCTET)
                body(ref, at, pl.multiple_of(slot + at, OCTET), OCTET)

        slot += -(-blocks // OCTET) * OCTET


def project_kernel(field_ref, pick1_ref, pick2_ref, cjac_ref, ajac_ref, ejac_ref, out_ref, l1_ref, l2_ref):
    ties = out_ref.shape[1] // 2
    high, low = halves(field_ref[...])
    for pick_ref, left_ref in ((pick1_ref, l1_ref), (pick2_ref, l2_ref)):
        left_ref[0] = dot(pick_ref[...], high)
        left_ref[1] = dot(pick_ref[...], low)

    def body(ref, at, slot, count):
        rows = pl.ds(slot, OCTET)
        left = jnp.concatenate([l1_ref[0, rows], l2_ref[0, rows], l1_ref[1, rows], l2_ref[1, rows]])
        left = left.astype(BF16)
        total = jnp.zeros((OCTET, 2 * ties), F32)
        for j in range(count):
            got = dot_t(left, ref[at + j])
            one = got[0:8, :ties] + got[16:24, :ties]
            two = got[8:16, ties:] + got[24:32, ties:]
            got = jnp.concatenate([one, two], axis=1)
            total = jnp.where(row_of(total.shape) == j, got, total)
        out_ref[rows] = total

    octets((cjac_ref, ajac_ref, ejac_ref), body)


def backward(q1_ref, q2_ref, put1_ref, put2_ref, cjac_ref, ajac_ref, ejac_ref, t1_ref, t2_ref):
    ties = q1_ref.shape[1]
    width = t1_ref.shape[1]

    def body(ref, at, slot, count):
        rows = pl.ds(slot, OCTET)
        zero = jnp.zeros((OCTET, ties), F32)
        q1, q2 = q1_ref[rows], q2_ref[rows]
        total = jnp.zeros((2 * OCTET, width), F32)
        for j in range(count):
            chosen = row_of(q1.shape) == j
            top = jnp.concatenate([jnp.where(chosen, q1, 0.0), zero], axis=1)
            low = jnp.concatenate([zero, jnp.where(chosen, q2, 0.0)], axis=1)
            total = total + dot(jnp.concatenate([top, low]).astype(BF16), ref[at + j])
        t1_ref[rows] = total[:OCTET]
        t2_ref[rows] = total[OCTET:]

    octets((cjac_ref, ajac_ref, ejac_ref), body)
    out = None
    for t_ref, put_ref in ((t1_ref, put1_ref), (t2_ref, put2_ref)):
        for part in halves(t_ref[...]):
            term = dot(put_ref[...], part)
            out = term if out is None else out + term
    return out


def rhs_kernel(res_ref, coef_ref, put1_ref, put2_ref, cjac_ref, ajac_ref, ejac_ref, out_ref, q1_ref, q2_ref, t1_ref, t2_ref):
    ties = q1_ref.shape[1]
    r1, r2 = res_ref[:, :ties], res_ref[:, ties:]
    q1_ref[...] = coef_ref[0] * r1 - coef_ref[1] * r2
    q2_ref[...] = coef_ref[2] * r2 - coef_ref[1] * r1
    out = backward(q1_ref, q2_ref, put1_ref, put2_ref, cjac_ref, ajac_ref, ejac_ref, t1_ref, t2_ref)
    out_ref[...] = out.astype(BF16)


def gather_kernel(scenes, start, mine_ref, got_ref, *refs):
    first = pl.multiple_of(lax.axis_index("group") * scenes, scenes)
    field = mine_ref[...].astype(F32) + got_ref[...].astype(F32)
    if start:
        out_ref, packet_ref = refs
        field = -field
    else:
        res_ref, out_ref, packet_ref = refs
    out_ref[...] = field
    packet_ref[...] = jnp.zeros_like(packet_ref)
    if not start:
        res = res_ref[...]
        half = packet_ref.shape[1] // 2
        packet_ref[0:1, :half] = jnp.full((1, half), jnp.sum(res * res), F32)
        packet_ref[0:1, half:] = jnp.full((1, half), jnp.sum(res * field), F32)
    packet_ref[1:2, :] = out_ref[pl.ds(first, OCTET), :][0:1]
    packet_ref[2:3, :] = out_ref[pl.ds(pl.multiple_of(first + scenes - OCTET, OCTET), OCTET), :][OCTET - 1 :]


def outside(packet_refs, ajac_ref, ejac_ref, part_ref, slot):
    _, one, _, three = packet_refs
    ties = part_ref.shape[1] // 2
    last = ajac_ref.shape[0] - 1
    even = lax.axis_index("orbit") % 2 == 0
    after = jnp.where(even, one[1:2, :], three[1:2, :])
    ahead = jnp.where(even, three[2:3, :], one[2:3, :])
    sub = row_of((OCTET, after.shape[1]))
    both = jnp.where(sub == last % OCTET, after, jnp.where(sub == 0, ahead, 0.0))
    high = both.astype(BF16).astype(F32)
    left = jnp.concatenate([high, both - high]).astype(BF16)
    got = dot_t(left, ajac_ref[last])
    got = got[:OCTET] + got[OCTET:]
    tail = pl.ds(slot + last - last % OCTET, OCTET)
    keep = row_of((OCTET, ties)) == last % OCTET
    part_ref[tail, ties:] = part_ref[tail, ties:] + jnp.where(keep, got[:, ties:], 0.0)
    got = dot_t(left, ejac_ref[0])
    got = got[:OCTET] + got[OCTET:]
    tail = pl.ds(slot + last + 1, OCTET)
    keep = row_of((OCTET, ties)) == 0
    part_ref[tail, :ties] = part_ref[tail, :ties] + jnp.where(keep, got[:, :ties], 0.0)


def scalars(packet_refs, scal_ref, step):
    mine, one, two, three = (ref[0:1, :] for ref in packet_refs)
    sums = (mine + one) + (two + three)
    half = sums.shape[1] // 2
    now, along = sums[:, :half], sums[:, half:]
    if step == 0:
        beta = jnp.zeros_like(now)
        alpha = now / along
    else:
        before, last = scal_ref[0:1, :], scal_ref[1:2, :]
        beta = now / before
        alpha = now / (along - beta * now / last)
    return now, alpha, beta


def wide(x):
    return jnp.concatenate([x, x], axis=1)


def step_kernel(step, scenes, *refs):
    refs = list(refs)
    take = lambda n: [refs.pop(0) for _ in range(n)]
    (part_ref,) = take(1)
    packet_refs = take(4)
    coef_ref, put1_ref, put2_ref, damp_ref, cjac_ref, ajac_ref, ejac_ref = take(7)
    (res_ref,) = take(1)
    if step >= 1:
        field_ref, obs_ref, x_ref = take(3)
    if step >= 2:
        image_ref, shadow_ref, dir_ref, scal_ref = take(4)
    (sent_ref, out_obs_ref) = take(2)
    if step >= 1:
        out_res_ref, out_image_ref, out_shadow_ref, out_dir_ref, out_x_ref, out_scal_ref = take(6)
    part_scr, q1_ref, q2_ref, t1_ref, t2_ref, c_ref = take(6)
    ties = q1_ref.shape[1]
    first = pl.multiple_of(lax.axis_index("group") * scenes, scenes)
    own = pl.ds(first, scenes)

    part_scr[...] = part_ref[...]
    outside(packet_refs, ajac_ref, ejac_ref, part_scr, cjac_ref.shape[0])
    if step == 0:
        out_obs_ref[...] = part_scr[...]
        now_res_ref = res_ref
    else:
        now, alpha, beta = scalars(packet_refs, None if step == 1 else scal_ref, step - 1)
        out_scal_ref[...] = jnp.zeros_like(out_scal_ref)
        out_scal_ref[0:1, :] = now
        out_scal_ref[1:2, :] = alpha
        alpha, beta = wide(alpha), wide(beta)
        image, shadow, direction = field_ref[...], part_scr[...], res_ref[own]
        if step >= 2:
            image = image + beta * image_ref[...]
            shadow = shadow + beta * shadow_ref[...]
            direction = direction + beta * dir_ref[...]
            out_x_ref[...] = x_ref[...] + alpha * direction
        else:
            out_x_ref[...] = alpha * direction
        out_image_ref[...] = image
        out_shadow_ref[...] = shadow
        out_dir_ref[...] = direction
        out_res_ref[...] = res_ref[...] - alpha * image
        out_obs_ref[...] = obs_ref[...] - alpha * shadow
        now_res_ref = out_res_ref
    r1, r2 = out_obs_ref[:, :ties], out_obs_ref[:, ties:]
    q1_ref[...] = coef_ref[0] * r1 - coef_ref[1] * r2
    q2_ref[...] = coef_ref[2] * r2 - coef_ref[1] * r1
    c_ref[...] = backward(q1_ref, q2_ref, put1_ref, put2_ref, cjac_ref, ajac_ref, ejac_ref, t1_ref, t2_ref)
    c_ref[own] = c_ref[own] + damp_ref[...] * now_res_ref[own]
    sent_ref[...] = c_ref[...].astype(BF16)


def final_kernel(step, scenes, *refs):
    field_ref, m, a, b, c, res_ref, image_ref, dir_ref, x_ref, scal_ref, out_x_ref, out_res_ref = refs
    own = pl.ds(pl.multiple_of(lax.axis_index("group") * scenes, scenes), scenes)
    now, alpha, beta = scalars((m, a, b, c), scal_ref, step)
    alpha, beta = wide(alpha), wide(beta)
    res = res_ref[own]
    out_x_ref[...] = x_ref[...] + alpha * (res + beta * dir_ref[...])
    out_res_ref[...] = res - alpha * (field_ref[own] + beta * image_ref[own])


def call(kernel, outs, scratch, name, args, flops=0):
    whole = pl.BlockSpec(memory_space=pltpu.VMEM)
    moved = sum(a.size * a.dtype.itemsize for a in args)
    return pl.pallas_call(
        kernel,
        out_shape=[jax.ShapeDtypeStruct(*o) for o in outs],
        in_specs=[whole] * len(args),
        out_specs=[whole] * len(outs),
        scratch_shapes=[pltpu.VMEM(*s) for s in scratch],
        cost_estimate=pl.CostEstimate(flops=flops, bytes_accessed=moved, transcendentals=0),
        compiler_params=pltpu.CompilerParams(vmem_limit_bytes=VMEM_LIMIT),
        name=name,
    )(*args)


VMEM_LIMIT = 16 << 20


def group_sum_but_last(sent):
    n, g = lax.axis_size("orbit"), lax.axis_size("group")
    stages = g.bit_length() - 1
    for stage in range(stages):
        route = []
        for o in range(n):
            mask = 1 << ((stage + o % 2) % stages)
            route += [(o * g + i, o * g + (i ^ mask)) for i in range(g)]
        got = lax.ppermute(sent, ("orbit", "group"), route)
        if stage == stages - 1:
            return sent, got
        sent = lax.optimization_barrier((sent.astype(F32) + got.astype(F32)).astype(BF16))


def orbit_packets(packet):
    n = lax.axis_size("orbit")
    return [packet] + [lax.ppermute(packet, "orbit", [(i, i ^ mask) for i in range(n)]) for mask in range(1, n)]


def on_device(
    along_jac,
    along_res,
    along_e,
    along_count,
    damping,
    cross_jac,
    cross_res,
    cross_e,
    cross_own,
    cross_group,
    cross_other,
):
    scenes, _, ties, width = along_jac.shape[1:]
    links = cross_jac.shape[1]
    groups = lax.axis_size("group")
    rows = groups * scenes
    first = lax.axis_index("group") * scenes
    ajac = along_jac[0].reshape(scenes, 2 * ties, width)
    cjac = cross_jac[0].reshape(links, 2 * ties, width)
    slots = links + scenes + OCTET

    def pass_on(block):
        n = lax.axis_size("orbit")
        return lax.ppermute(block, "orbit", [(i, (i + 1) % n) for i in range(n)])

    live = (jnp.arange(ties)[None, :] < along_count[0][:, None]).astype(F32)
    ejac = pass_on(ajac[-1:])
    small = pass_on(jnp.concatenate([along_e[0, -1], along_res[0, -1], live[-1:], live[-1:] * 0, live[-1:] * 0, live[-1:] * 0], axis=0))

    fill = lambda a: jnp.pad(a, ((0, OCTET - 1), (0, 0)))
    stacked = lambda c, a, e: jnp.concatenate([c, a, fill(e)], axis=0)
    e1 = stacked(cross_e[0, :, 0], along_e[0, :, 0], small[0:1])
    e2 = stacked(cross_e[0, :, 1], along_e[0, :, 1], small[1:2])
    res1 = stacked(cross_res[0, :, 0], along_res[0, :, 0], small[2:3])
    res2 = stacked(cross_res[0, :, 1], along_res[0, :, 1], small[3:4])
    keep = stacked(jnp.ones((links, ties), F32), live, small[4:5])
    over = keep / (1.0 + e1 * e1 + e2 * e2)
    coef = jnp.stack([(1.0 + e2 * e2) * over, e1 * e2 * over, (1.0 + e1 * e1) * over])
    observed = jnp.concatenate([res1, res2], axis=1)
    here = first + jnp.arange(scenes)
    none = jnp.full((OCTET,), -1)
    one = jnp.concatenate([first + cross_own[0], here, none])
    two = jnp.concatenate([cross_group[0, :, 0] * scenes + cross_other[0], here[1:], none[:1], first[None], none[1:]])
    numbers = jnp.arange(rows)
    pick1, pick2 = ((v[:, None] == numbers[None, :]).astype(BF16) for v in (one, two))
    put1, put2 = ((v[None, :] == numbers[:, None]).astype(BF16) for v in (one, two))
    damp = jnp.broadcast_to(damping[0][:, None], (scenes, width))

    jacs = (cjac, ajac, ejac)
    work = 2 * (links + scenes + 1) * 32 * 2 * ties * width
    tie = (slots, ties)
    pair = (slots, 2 * ties)
    full = (rows, width)
    own = (scenes, width)
    terms = [(tie, F32), (tie, F32), ((slots, width), F32), ((slots, width), F32)]

    def project(field):
        scratch = [((2, slots, width), F32)] * 2
        return call(project_kernel, [(pair, F32)], scratch, "project", (field, pick1, pick2) + jacs, work)[0]

    def finish(sums, res=None):
        args = sums if res is None else sums + (res,)
        kernel = functools.partial(gather_kernel, scenes, res is None)
        field, packet = call(kernel, [(full, F32), ((OCTET, width), F32)], [], "finish", args)
        return field, orbit_packets(packet)

    (sent,) = call(rhs_kernel, [(full, BF16)], terms, "rhs", (observed, coef, put1, put2) + jacs, work)
    res, packets = finish(group_sum_but_last(sent))
    part = project(res)
    fixed = (coef, put1, put2, damp) + jacs
    scratch = [(pair, F32)] + terms + [(full, F32)]
    sent, obs = call(
        functools.partial(step_kernel, 0, scenes),
        [(full, BF16), (pair, F32)],
        scratch,
        "step",
        (part, *packets) + fixed + (res,),
        work,
    )
    state = ()
    x = jnp.zeros(own, F32)
    for step in range(1, ITERS):
        field, packets = finish(group_sum_but_last(sent), res)
        part = project(field)
        sent, obs, res, image, shadow, direction, x, scal = call(
            functools.partial(step_kernel, step, scenes),
            [(full, BF16), (pair, F32), (full, F32), (full, F32), (pair, F32), (own, F32), (own, F32), ((OCTET, width // 2), F32)],
            scratch,
            "step",
            (part, *packets) + fixed + (res, field, obs, x) + state,
            work,
        )
        state = (image, shadow, direction, scal)
    field, packets = finish(group_sum_but_last(sent), res)
    x, res = call(
        functools.partial(final_kernel, ITERS - 1, scenes),
        [(own, F32), (own, F32)],
        [],
        "final",
        (field, *packets, res, image, direction, x, scal),
    )
    return x[None], res[None]


def solution(mesh):
    placed = (
        P("group", "orbit", None, None, None),
        P("group", "orbit", None, None),
        P("group", "orbit", None, None),
        P("group", "orbit"),
        P("group", "orbit"),
        P("group", "orbit", None, None, None),
        P("group", "orbit", None, None),
        P("group", "orbit", None, None),
        P("group", "orbit"),
        P("group", "orbit", None),
        P("group", "orbit"),
    )
    return jax.shard_map(
        on_device,
        mesh=mesh,
        in_specs=placed,
        out_specs=(P("group", "orbit", None), P("group", "orbit", None)),
        check_vma=False,
    )
```

```python
import functools

import jax
import jax.numpy as jnp
from jax import lax
from jax.experimental import pallas as pl
from jax.experimental.pallas import tpu as pltpu
from jax.sharding import PartitionSpec as P

ITERS = 4
F32, BF16 = jnp.float32, jnp.bfloat16
OCTET = 8


def dot(a, b):
    return lax.dot_general(a, b, (((1,), (0,)), ((), ())), preferred_element_type=F32)


def dot_t(a, b):
    return lax.dot_general(a, b, (((1,), (1,)), ((), ())), preferred_element_type=F32)


def halves(x):
    high = x.astype(BF16)
    return high, (x - high.astype(F32)).astype(BF16)


def row_of(shape):
    return lax.broadcasted_iota(jnp.int32, shape, 0)


def octets(refs, body):
    slot = 0
    for ref in refs:
        blocks = ref.shape[0]
        if blocks <= OCTET:
            body(ref, 0, slot, blocks)
        else:

            @pl.loop(0, blocks // OCTET)
            def _(i, ref=ref, slot=slot):
                at = pl.multiple_of(i * OCTET, OCTET)
                body(ref, at, pl.multiple_of(slot + at, OCTET), OCTET)

        slot += -(-blocks // OCTET) * OCTET


def project_kernel(field_ref, pick1_ref, pick2_ref, cjac_ref, ajac_ref, ejac_ref, out_ref, l1_ref, l2_ref):
    ties = out_ref.shape[1] // 2
    high, low = halves(field_ref[...])
    for pick_ref, left_ref in ((pick1_ref, l1_ref), (pick2_ref, l2_ref)):
        left_ref[0] = dot(pick_ref[...], high)
        left_ref[1] = dot(pick_ref[...], low)

    def body(ref, at, slot, count):
        rows = pl.ds(slot, OCTET)
        left = jnp.concatenate([l1_ref[0, rows], l2_ref[0, rows], l1_ref[1, rows], l2_ref[1, rows]])
        left = left.astype(BF16)
        total = jnp.zeros((OCTET, 2 * ties), F32)
        for j in range(count):
            got = dot(left, ref[at + j])
            one = got[0:8, :ties] + got[16:24, :ties]
            two = got[8:16, ties:] + got[24:32, ties:]
            got = jnp.concatenate([one, two], axis=1)
            total = jnp.where(row_of(total.shape) == j, got, total)
        out_ref[rows] = total

    octets((cjac_ref, ajac_ref, ejac_ref), body)


def turn_kernel(*refs):
    half = len(refs) // 2
    for ref, out_ref in zip(refs[:half], refs[half:]):

        @pl.loop(0, ref.shape[0])
        def _(i, ref=ref, out_ref=out_ref):
            out_ref[i] = ref[i].T


def backward(q1_ref, q2_ref, put1_ref, put2_ref, cjac_ref, ajac_ref, ejac_ref, t1_ref, t2_ref):
    ties = q1_ref.shape[1]
    width = t1_ref.shape[1]

    def body(ref, at, slot, count):
        rows = pl.ds(slot, OCTET)
        zero = jnp.zeros((OCTET, ties), F32)
        q1, q2 = q1_ref[rows], q2_ref[rows]
        total = jnp.zeros((2 * OCTET, width), F32)
        for j in range(count):
            chosen = row_of(q1.shape) == j
            top = jnp.concatenate([jnp.where(chosen, q1, 0.0), zero], axis=1)
            low = jnp.concatenate([zero, jnp.where(chosen, q2, 0.0)], axis=1)
            total = total + dot(jnp.concatenate([top, low]).astype(BF16), ref[at + j])
        t1_ref[rows] = total[:OCTET]
        t2_ref[rows] = total[OCTET:]

    octets((cjac_ref, ajac_ref, ejac_ref), body)
    out = None
    for t_ref, put_ref in ((t1_ref, put1_ref), (t2_ref, put2_ref)):
        for part in halves(t_ref[...]):
            term = dot(put_ref[...], part)
            out = term if out is None else out + term
    return out


def rhs_kernel(res_ref, coef_ref, put1_ref, put2_ref, cjac_ref, ajac_ref, ejac_ref, out_ref, q1_ref, q2_ref, t1_ref, t2_ref):
    ties = q1_ref.shape[1]
    r1, r2 = res_ref[:, :ties], res_ref[:, ties:]
    q1_ref[...] = coef_ref[0] * r1 - coef_ref[1] * r2
    q2_ref[...] = coef_ref[2] * r2 - coef_ref[1] * r1
    out = backward(q1_ref, q2_ref, put1_ref, put2_ref, cjac_ref, ajac_ref, ejac_ref, t1_ref, t2_ref)
    out_ref[...] = out.astype(BF16)


def gather_kernel(scenes, start, parts, *refs):
    first = pl.multiple_of(lax.axis_index("group") * scenes, scenes)
    field = refs[0][...].astype(F32)
    for ref in refs[1:parts]:
        field = field + ref[...].astype(F32)
    refs = refs[parts:]
    if start:
        out_ref, packet_ref = refs
        field = -field
    else:
        res_ref, out_ref, packet_ref = refs
    out_ref[...] = field
    packet_ref[...] = jnp.zeros_like(packet_ref)
    if not start:
        res = res_ref[...]
        half = packet_ref.shape[1] // 2
        packet_ref[0:1, :half] = jnp.full((1, half), jnp.sum(res * res), F32)
        packet_ref[0:1, half:] = jnp.full((1, half), jnp.sum(res * field), F32)
    packet_ref[1:2, :] = out_ref[pl.ds(first, OCTET), :][0:1]
    packet_ref[2:3, :] = out_ref[pl.ds(pl.multiple_of(first + scenes - OCTET, OCTET), OCTET), :][OCTET - 1 :]


def outside(packet_refs, ajac_ref, ejac_ref, part_ref, slot):
    _, one, _, three = packet_refs
    ties = part_ref.shape[1] // 2
    last = ajac_ref.shape[0] - 1
    even = lax.axis_index("orbit") % 2 == 0
    after = jnp.where(even, one[1:2, :], three[1:2, :])
    ahead = jnp.where(even, three[2:3, :], one[2:3, :])
    sub = row_of((OCTET, after.shape[1]))
    both = jnp.where(sub == last % OCTET, after, jnp.where(sub == 0, ahead, 0.0))
    high = both.astype(BF16).astype(F32)
    left = jnp.concatenate([high, both - high]).astype(BF16)
    got = dot_t(left, ajac_ref[last])
    got = got[:OCTET] + got[OCTET:]
    tail = pl.ds(slot + last - last % OCTET, OCTET)
    keep = row_of((OCTET, ties)) == last % OCTET
    part_ref[tail, ties:] = part_ref[tail, ties:] + jnp.where(keep, got[:, ties:], 0.0)
    got = dot_t(left, ejac_ref[0])
    got = got[:OCTET] + got[OCTET:]
    tail = pl.ds(slot + last + 1, OCTET)
    keep = row_of((OCTET, ties)) == 0
    part_ref[tail, :ties] = part_ref[tail, :ties] + jnp.where(keep, got[:, :ties], 0.0)


def scalars(packet_refs, scal_ref, step):
    mine, one, two, three = (ref[0:1, :] for ref in packet_refs)
    sums = (mine + one) + (two + three)
    half = sums.shape[1] // 2
    now, along = sums[:, :half], sums[:, half:]
    if step == 0:
        beta = jnp.zeros_like(now)
        alpha = now / along
    else:
        before, last = scal_ref[0:1, :], scal_ref[1:2, :]
        beta = now / before
        alpha = now / (along - beta * now / last)
    return now, alpha, beta


def wide(x):
    return jnp.concatenate([x, x], axis=1)


def step_kernel(step, scenes, *refs):
    refs = list(refs)
    take = lambda n: [refs.pop(0) for _ in range(n)]
    (part_ref,) = take(1)
    packet_refs = take(4)
    coef_ref, put1_ref, put2_ref, damp_ref, cjac_ref, ajac_ref, ejac_ref = take(7)
    (res_ref,) = take(1)
    if step >= 1:
        field_ref, obs_ref, x_ref = take(3)
    if step >= 2:
        image_ref, shadow_ref, dir_ref, scal_ref = take(4)
    (sent_ref, out_obs_ref) = take(2)
    if step >= 1:
        out_res_ref, out_image_ref, out_shadow_ref, out_dir_ref, out_x_ref, out_scal_ref = take(6)
    part_scr, q1_ref, q2_ref, t1_ref, t2_ref, c_ref = take(6)
    ties = q1_ref.shape[1]
    first = pl.multiple_of(lax.axis_index("group") * scenes, scenes)
    own = pl.ds(first, scenes)

    part_scr[...] = part_ref[...]
    outside(packet_refs, ajac_ref, ejac_ref, part_scr, cjac_ref.shape[0])
    if step == 0:
        out_obs_ref[...] = part_scr[...]
        now_res_ref = res_ref
    else:
        now, alpha, beta = scalars(packet_refs, None if step == 1 else scal_ref, step - 1)
        out_scal_ref[...] = jnp.zeros_like(out_scal_ref)
        out_scal_ref[0:1, :] = now
        out_scal_ref[1:2, :] = alpha
        alpha, beta = wide(alpha), wide(beta)
        image, shadow, direction = field_ref[...], part_scr[...], res_ref[own]
        if step >= 2:
            image = image + beta * image_ref[...]
            shadow = shadow + beta * shadow_ref[...]
            direction = direction + beta * dir_ref[...]
            out_x_ref[...] = x_ref[...] + alpha * direction
        else:
            out_x_ref[...] = alpha * direction
        out_image_ref[...] = image
        out_shadow_ref[...] = shadow
        out_dir_ref[...] = direction
        out_res_ref[...] = res_ref[...] - alpha * image
        out_obs_ref[...] = obs_ref[...] - alpha * shadow
        now_res_ref = out_res_ref
    r1, r2 = out_obs_ref[:, :ties], out_obs_ref[:, ties:]
    q1_ref[...] = coef_ref[0] * r1 - coef_ref[1] * r2
    q2_ref[...] = coef_ref[2] * r2 - coef_ref[1] * r1
    c_ref[...] = backward(q1_ref, q2_ref, put1_ref, put2_ref, cjac_ref, ajac_ref, ejac_ref, t1_ref, t2_ref)
    c_ref[own] = c_ref[own] + damp_ref[...] * now_res_ref[own]
    sent_ref[...] = c_ref[...].astype(BF16)


def final_kernel(step, scenes, *refs):
    field_ref, m, a, b, c, res_ref, image_ref, dir_ref, x_ref, scal_ref, out_x_ref, out_res_ref = refs
    own = pl.ds(pl.multiple_of(lax.axis_index("group") * scenes, scenes), scenes)
    now, alpha, beta = scalars((m, a, b, c), scal_ref, step)
    alpha, beta = wide(alpha), wide(beta)
    res = res_ref[own]
    out_x_ref[...] = x_ref[...] + alpha * (res + beta * dir_ref[...])
    out_res_ref[...] = res - alpha * (field_ref[own] + beta * image_ref[own])


def call(kernel, outs, scratch, name, args, flops=0):
    whole = pl.BlockSpec(memory_space=pltpu.VMEM)
    moved = sum(a.size * a.dtype.itemsize for a in args)
    return pl.pallas_call(
        kernel,
        out_shape=[jax.ShapeDtypeStruct(*o) for o in outs],
        in_specs=[whole] * len(args),
        out_specs=[whole] * len(outs),
        scratch_shapes=[pltpu.VMEM(*s) for s in scratch],
        cost_estimate=pl.CostEstimate(flops=flops, bytes_accessed=moved, transcendentals=0),
        compiler_params=pltpu.CompilerParams(vmem_limit_bytes=VMEM_LIMIT),
        name=name,
    )(*args)


VMEM_LIMIT = 16 << 20


def group_sum_but_last(sent):
    size = lax.axis_size("group")
    stride, pairs = 1, None
    while stride < size:
        masks = (1, 2, 3) if 4 * stride <= size else (1,)
        got = [swap(sent, "group", mask * stride) for mask in masks]
        stride *= len(masks) + 1
        pairs = [sent] + got
        if stride < size or len(pairs) > 2:
            low = [p.astype(F32) for p in pairs]
            total = low[0] + low[1]
            if len(low) > 2:
                total = total + (low[2] + low[3])
            if stride < size:
                sent = lax.optimization_barrier(total.astype(BF16))
            else:
                pairs = [total]
    return pairs


def swap(block, axis, mask):
    return lax.ppermute(block, axis, [(i, i ^ mask) for i in range(lax.axis_size(axis))])


def orbit_packets(packet):
    n = lax.axis_size("orbit")
    return [packet] + [lax.ppermute(packet, "orbit", [(i, i ^ mask) for i in range(n)]) for mask in range(1, n)]


def on_device(
    along_jac,
    along_res,
    along_e,
    along_count,
    damping,
    cross_jac,
    cross_res,
    cross_e,
    cross_own,
    cross_group,
    cross_other,
):
    scenes, _, ties, width = along_jac.shape[1:]
    links = cross_jac.shape[1]
    groups = lax.axis_size("group")
    rows = groups * scenes
    first = lax.axis_index("group") * scenes
    ajac = along_jac[0].reshape(scenes, 2 * ties, width)
    cjac = cross_jac[0].reshape(links, 2 * ties, width)
    slots = links + scenes + OCTET

    def pass_on(block):
        n = lax.axis_size("orbit")
        return lax.ppermute(block, "orbit", [(i, (i + 1) % n) for i in range(n)])

    live = (jnp.arange(ties)[None, :] < along_count[0][:, None]).astype(F32)
    ejac = pass_on(ajac[-1:])
    small = pass_on(jnp.concatenate([along_e[0, -1], along_res[0, -1], live[-1:], live[-1:] * 0, live[-1:] * 0, live[-1:] * 0], axis=0))

    fill = lambda a: jnp.pad(a, ((0, OCTET - 1), (0, 0)))
    stacked = lambda c, a, e: jnp.concatenate([c, a, fill(e)], axis=0)
    e1 = stacked(cross_e[0, :, 0], along_e[0, :, 0], small[0:1])
    e2 = stacked(cross_e[0, :, 1], along_e[0, :, 1], small[1:2])
    res1 = stacked(cross_res[0, :, 0], along_res[0, :, 0], small[2:3])
    res2 = stacked(cross_res[0, :, 1], along_res[0, :, 1], small[3:4])
    keep = stacked(jnp.ones((links, ties), F32), live, small[4:5])
    over = keep / (1.0 + e1 * e1 + e2 * e2)
    coef = jnp.stack([(1.0 + e2 * e2) * over, e1 * e2 * over, (1.0 + e1 * e1) * over])
    observed = jnp.concatenate([res1, res2], axis=1)
    here = first + jnp.arange(scenes)
    none = jnp.full((OCTET,), -1)
    one = jnp.concatenate([first + cross_own[0], here, none])
    two = jnp.concatenate([cross_group[0, :, 0] * scenes + cross_other[0], here[1:], none[:1], first[None], none[1:]])
    numbers = jnp.arange(rows)
    pick1, pick2 = ((v[:, None] == numbers[None, :]).astype(BF16) for v in (one, two))
    put1, put2 = ((v[None, :] == numbers[:, None]).astype(BF16) for v in (one, two))
    damp = jnp.broadcast_to(damping[0][:, None], (scenes, width))

    jacs = (cjac, ajac, ejac)
    work = 2 * (links + scenes + 1) * 32 * 2 * ties * width
    tie = (slots, ties)
    pair = (slots, 2 * ties)
    full = (rows, width)
    own = (scenes, width)
    terms = [(tie, F32), (tie, F32), ((slots, width), F32), ((slots, width), F32)]

    def project(field):
        scratch = [((2, slots, width), F32)] * 2
        return call(project_kernel, [(pair, F32)], scratch, "project", (field, pick1, pick2) + turned, work)[0]

    def finish(sums, res=None):
        args = sums if res is None else sums + [res]
        kernel = functools.partial(gather_kernel, scenes, res is None, len(sums))
        field, packet = call(kernel, [(full, F32), ((OCTET, width), F32)], [], "finish", args)
        return field, orbit_packets(packet)

    (sent,) = call(rhs_kernel, [(full, BF16)], terms, "rhs", (observed, coef, put1, put2) + jacs, work)
    turned = tuple(call(turn_kernel, [(j.shape, BF16) for j in jacs], [], "turn", jacs, work))
    res, packets = finish(group_sum_but_last(sent))
    part = project(res)
    fixed = (coef, put1, put2, damp) + jacs
    scratch = [(pair, F32)] + terms + [(full, F32)]
    sent, obs = call(
        functools.partial(step_kernel, 0, scenes),
        [(full, BF16), (pair, F32)],
        scratch,
        "step",
        (part, *packets) + fixed + (res,),
        work,
    )
    state = ()
    x = jnp.zeros(own, F32)
    for step in range(1, ITERS):
        field, packets = finish(group_sum_but_last(sent), res)
        part = project(field)
        sent, obs, res, image, shadow, direction, x, scal = call(
            functools.partial(step_kernel, step, scenes),
            [(full, BF16), (pair, F32), (full, F32), (full, F32), (pair, F32), (own, F32), (own, F32), ((OCTET, width // 2), F32)],
            scratch,
            "step",
            (part, *packets) + fixed + (res, field, obs, x) + state,
            work,
        )
        state = (image, shadow, direction, scal)
    field, packets = finish(group_sum_but_last(sent), res)
    x, res = call(
        functools.partial(final_kernel, ITERS - 1, scenes),
        [(own, F32), (own, F32)],
        [],
        "final",
        (field, *packets, res, image, direction, x, scal),
    )
    return x[None], res[None]


def solution(mesh):
    placed = (
        P("group", "orbit", None, None, None),
        P("group", "orbit", None, None),
        P("group", "orbit", None, None),
        P("group", "orbit"),
        P("group", "orbit"),
        P("group", "orbit", None, None, None),
        P("group", "orbit", None, None),
        P("group", "orbit", None, None),
        P("group", "orbit"),
        P("group", "orbit", None),
        P("group", "orbit"),
    )
    return jax.shard_map(
        on_device,
        mesh=mesh,
        in_specs=placed,
        out_specs=(P("group", "orbit", None), P("group", "orbit", None)),
        check_vma=False,
    )
```

```python
import functools

import jax
import jax.numpy as jnp
from jax import lax
from jax.experimental import pallas as pl
from jax.experimental.pallas import tpu as pltpu
from jax.sharding import PartitionSpec as P

ITERS = 4
F32, BF16 = jnp.float32, jnp.bfloat16
OCTET = 8


def dot(a, b):
    return lax.dot_general(a, b, (((1,), (0,)), ((), ())), preferred_element_type=F32)


def dot_t(a, b):
    return lax.dot_general(a, b, (((1,), (1,)), ((), ())), preferred_element_type=F32)


def halves(x):
    high = x.astype(BF16)
    return high, (x - high.astype(F32)).astype(BF16)


def row_of(shape):
    return lax.broadcasted_iota(jnp.int32, shape, 0)


def octets(refs, body):
    slot = 0
    for number, ref in enumerate(refs):
        blocks = ref.shape[0]
        if blocks <= OCTET:
            body(number, ref, 0, slot, blocks)
        else:

            @pl.loop(0, blocks // OCTET)
            def _(i, number=number, ref=ref, slot=slot):
                at = pl.multiple_of(i * OCTET, OCTET)
                body(number, ref, at, pl.multiple_of(slot + at, OCTET), OCTET)

        slot += -(-blocks // OCTET) * OCTET


def project_kernel(turned, field_ref, pick1_ref, pick2_ref, *refs):
    *jac_refs, out_ref, l1_ref, l2_ref = refs
    product = [dot if is_turned else dot_t for is_turned in turned]
    ties = out_ref.shape[1] // 2
    high, low = halves(field_ref[...])
    for pick_ref, left_ref in ((pick1_ref, l1_ref), (pick2_ref, l2_ref)):
        left_ref[0] = dot(pick_ref[...], high)
        left_ref[1] = dot(pick_ref[...], low)

    def body(number, ref, at, slot, count):
        rows = pl.ds(slot, OCTET)
        left = jnp.concatenate([l1_ref[0, rows], l2_ref[0, rows], l1_ref[1, rows], l2_ref[1, rows]])
        left = left.astype(BF16)
        total = jnp.zeros((OCTET, 2 * ties), F32)
        for j in range(count):
            got = product[number](left, ref[at + j])
            one = got[0:8, :ties] + got[16:24, :ties]
            two = got[8:16, ties:] + got[24:32, ties:]
            got = jnp.concatenate([one, two], axis=1)
            total = jnp.where(row_of(total.shape) == j, got, total)
        out_ref[rows] = total

    octets(jac_refs, body)


def turn_kernel(start, after_ref, *refs):
    half = len(refs) // 2
    for ref, out_ref in zip(refs[:half], refs[half:]):

        @pl.loop(0, out_ref.shape[0])
        def _(i, ref=ref, out_ref=out_ref):
            out_ref[i] = ref[start + i].T


def terms(q1, q2, ref, at, count):
    zero = jnp.zeros_like(q1)
    total = jnp.zeros((2 * OCTET, ref.shape[2]), F32)
    for j in range(count):
        chosen = row_of(q1.shape) == j
        top = jnp.concatenate([jnp.where(chosen, q1, 0.0), zero], axis=1)
        low = jnp.concatenate([zero, jnp.where(chosen, q2, 0.0)], axis=1)
        total = total + dot(jnp.concatenate([top, low]).astype(BF16), ref[at + j])
    return total[:OCTET], total[OCTET:]


def scatter(t1_ref, t2_ref, put1_ref, put2_ref):
    out = None
    for t_ref, put_ref in ((t1_ref, put1_ref), (t2_ref, put2_ref)):
        for part in halves(t_ref[...]):
            term = dot(put_ref[...], part)
            out = term if out is None else out + term
    return out


def backward(q1_ref, q2_ref, put1_ref, put2_ref, cjac_ref, ajac_ref, ejac_ref, t1_ref, t2_ref):
    def body(number, ref, at, slot, count):
        rows = pl.ds(slot, OCTET)
        t1_ref[rows], t2_ref[rows] = terms(q1_ref[rows], q2_ref[rows], ref, at, count)

    octets((cjac_ref, ajac_ref, ejac_ref), body)
    return scatter(t1_ref, t2_ref, put1_ref, put2_ref)


def elimination(e1, e2, live):
    over = live / (1.0 + e1 * e1 + e2 * e2)
    return (1.0 + e2 * e2) * over, e1 * e2 * over, (1.0 + e1 * e1) * over


def settled(c11, c12, c22, r1, r2):
    return c11 * r1 - c12 * r2, c22 * r2 - c12 * r1


def live_rows(count_ref, out_ref):
    lane = lax.broadcasted_iota(jnp.int32, (1, out_ref.shape[1]), 1)
    for i in range(out_ref.shape[0]):
        out_ref[i : i + 1, :] = jnp.where(lane < count_ref[0, i], 1.0, 0.0)


def fetch(pairs, sems):
    copies = [pltpu.make_async_copy(a, b, sems.at[i]) for i, (a, b) in enumerate(pairs)]
    for copy in copies:
        copy.start()
    return copies


def pack_kernel(jac_ref, e_ref, res_ref, count_ref, out_jac_ref, out_ref, pair_ref, tally_ref, sems):
    last = jac_ref.shape[0] - 1
    block = pl.ds(last, 1)
    copies = fetch(
        [
            (jac_ref.at[block], out_jac_ref),
            (e_ref.at[block], pair_ref.at[0:1]),
            (res_ref.at[block], pair_ref.at[1:2]),
            (count_ref, tally_ref),
        ],
        sems,
    )
    for copy in copies[1:]:
        copy.wait()
    lane = lax.broadcasted_iota(jnp.int32, (1, out_ref.shape[1]), 1)
    out_ref[...] = jnp.zeros_like(out_ref)
    out_ref[0:2, :] = pair_ref[0]
    out_ref[2:4, :] = pair_ref[1]
    out_ref[4:5, :] = jnp.where(lane < tally_ref[0, last], 1.0, 0.0)
    copies[0].wait()


def setup_kernel(cjac_ref, ajac_ref, *refs):
    far_refs, refs = refs[:8], refs[8:]
    (out_cjac_ref, out_ajac_ref, coef_ref, put1_ref, put2_ref, pick1_ref, pick2_ref, t1_ref, t2_ref) = refs[:9]
    live_ref, q1_ref, q2_ref, index_ref, sems = refs[9:14]
    near_refs, near_sems = refs[14:22], refs[22]
    near = fetch(list(zip(far_refs, near_refs)), near_sems)
    ce_ref, cres_ref, ae_ref, ares_ref, count_ref, own_ref, group_ref, other_ref = near_refs
    copies = []
    for ref, out_ref in ((cjac_ref, out_cjac_ref), (ajac_ref, out_ajac_ref)):
        for at in range(0, ref.shape[0], OCTET):
            part = pl.ds(at, OCTET)
            copies.append(pltpu.make_async_copy(ref.at[part], out_ref.at[part], sems.at[len(copies)]))
            copies[-1].start()
    links, scenes = cjac_ref.shape[0], ajac_ref.shape[0]
    blocks = links + scenes
    for copy in near:
        copy.wait()
    live_ref[0:links] = jnp.ones((links, live_ref.shape[1]), F32)
    live_rows(count_ref, live_ref.at[links:blocks])
    for rows, e_ref, res_ref in ((slice(0, links), ce_ref, cres_ref), (slice(links, blocks), ae_ref, ares_ref)):
        c = elimination(e_ref[:, 0, :], e_ref[:, 1, :], live_ref[rows])
        for i in range(3):
            coef_ref[i, rows] = c[i]
        q1_ref[rows], q2_ref[rows] = settled(*c, res_ref[:, 0, :], res_ref[:, 1, :])

    first = lax.axis_index("group") * scenes
    slots = put1_ref.shape[1]
    index_ref[...] = jnp.zeros_like(index_ref)
    index_ref[0:1, :links] = own_ref[...] + first
    index_ref[1:2, :links] = group_ref[...] * scenes + other_ref[...]
    lane = lax.broadcasted_iota(jnp.int32, (1, index_ref.shape[1]), 1)
    one = jnp.where(lane < links, index_ref[0:1, :], jnp.where(lane < blocks, first + lane - links, -1))
    two = jnp.where(lane < blocks - 1, first + lane - links + 1, jnp.where(lane == blocks, first, -1))
    two = jnp.where(lane < links, index_ref[1:2, :], two)
    for index, put_ref, pick_ref in ((one, put1_ref, pick1_ref), (two, put2_ref, pick2_ref)):
        shape = (put_ref.shape[0], index.shape[1])
        table = jnp.where(row_of(shape) == index, 1.0, 0.0)
        put_ref[...] = table[:, :slots].astype(BF16)
        pick_ref[...] = table.T[:slots].astype(BF16)

    octet = 0
    for ref in (out_cjac_ref, out_ajac_ref):
        for at in range(0, ref.shape[0], OCTET):
            copies[octet].wait()
            rows = pl.ds(octet * OCTET, OCTET)
            t1_ref[rows], t2_ref[rows] = terms(q1_ref[rows], q2_ref[rows], ref, at, OCTET)
            octet += 1


def rhs_kernel(coef_ref, t1_ref, t2_ref, small_ref, ejac_ref, put1_ref, put2_ref, out_ref, out_coef_ref, all1_ref, all2_ref):
    blocks = t1_ref.shape[0]
    rows = pl.ds(blocks, OCTET)
    e1, e2, r1, r2, live = (small_ref[i : i + 1, :] for i in range(5))
    c = elimination(e1, e2, live)
    fill = lambda x: jnp.where(row_of((OCTET, x.shape[1])) == 0, x, 0.0)
    for i in range(3):
        out_coef_ref[i, :blocks] = coef_ref[i]
        out_coef_ref[i, rows] = fill(c[i])
    q1, q2 = settled(*c, r1, r2)
    all1_ref[:blocks] = t1_ref[...]
    all2_ref[:blocks] = t2_ref[...]
    all1_ref[rows], all2_ref[rows] = terms(fill(q1), fill(q2), ejac_ref, 0, 1)
    out_ref[...] = scatter(all1_ref, all2_ref, put1_ref, put2_ref).astype(BF16)


def gather_kernel(scenes, start, parts, *refs):
    first = pl.multiple_of(lax.axis_index("group") * scenes, scenes)
    field = refs[0][...].astype(F32)
    for ref in refs[1:parts]:
        field = field + ref[...].astype(F32)
    refs = refs[parts:]
    if start:
        out_ref, packet_ref = refs
        field = -field
    else:
        res_ref, out_ref, packet_ref = refs
    out_ref[...] = field
    packet_ref[...] = jnp.zeros_like(packet_ref)
    if not start:
        res = res_ref[...]
        half = packet_ref.shape[1] // 2
        packet_ref[0:1, :half] = jnp.full((1, half), jnp.sum(res * res), F32)
        packet_ref[0:1, half:] = jnp.full((1, half), jnp.sum(res * field), F32)
    packet_ref[1:2, :] = out_ref[pl.ds(first, OCTET), :][0:1]
    packet_ref[2:3, :] = out_ref[pl.ds(pl.multiple_of(first + scenes - OCTET, OCTET), OCTET), :][OCTET - 1 :]


def outside(packet_refs, ajac_ref, ejac_ref, part_ref, slot):
    _, one, _, three = packet_refs
    ties = part_ref.shape[1] // 2
    last = ajac_ref.shape[0] - 1
    even = lax.axis_index("orbit") % 2 == 0
    after = jnp.where(even, one[1:2, :], three[1:2, :])
    ahead = jnp.where(even, three[2:3, :], one[2:3, :])
    sub = row_of((OCTET, after.shape[1]))
    both = jnp.where(sub == last % OCTET, after, jnp.where(sub == 0, ahead, 0.0))
    high = both.astype(BF16).astype(F32)
    left = jnp.concatenate([high, both - high]).astype(BF16)
    got = dot_t(left, ajac_ref[last])
    got = got[:OCTET] + got[OCTET:]
    tail = pl.ds(slot + last - last % OCTET, OCTET)
    keep = row_of((OCTET, ties)) == last % OCTET
    part_ref[tail, ties:] = part_ref[tail, ties:] + jnp.where(keep, got[:, ties:], 0.0)
    got = dot_t(left, ejac_ref[0])
    got = got[:OCTET] + got[OCTET:]
    tail = pl.ds(slot + last + 1, OCTET)
    keep = row_of((OCTET, ties)) == 0
    part_ref[tail, :ties] = part_ref[tail, :ties] + jnp.where(keep, got[:, :ties], 0.0)


def scalars(packet_refs, scal_ref, step):
    mine, one, two, three = (ref[0:1, :] for ref in packet_refs)
    sums = (mine + one) + (two + three)
    half = sums.shape[1] // 2
    now, along = sums[:, :half], sums[:, half:]
    if step == 0:
        beta = jnp.zeros_like(now)
        alpha = now / along
    else:
        before, last = scal_ref[0:1, :], scal_ref[1:2, :]
        beta = now / before
        alpha = now / (along - beta * now / last)
    return now, alpha, beta


def wide(x):
    return jnp.concatenate([x, x], axis=1)


def step_kernel(step, scenes, *refs):
    refs = list(refs)
    take = lambda n: [refs.pop(0) for _ in range(n)]
    (part_ref,) = take(1)
    packet_refs = take(4)
    coef_ref, put1_ref, put2_ref, damp_ref, cjac_ref, ajac_ref, ejac_ref = take(7)
    (res_ref,) = take(1)
    if step >= 1:
        field_ref, obs_ref, x_ref = take(3)
    if step >= 2:
        image_ref, shadow_ref, dir_ref, scal_ref = take(4)
    (sent_ref, out_obs_ref) = take(2)
    if step >= 1:
        out_res_ref, out_image_ref, out_shadow_ref, out_dir_ref, out_x_ref, out_scal_ref = take(6)
    part_scr, q1_ref, q2_ref, t1_ref, t2_ref, c_ref = take(6)
    ties = q1_ref.shape[1]
    first = pl.multiple_of(lax.axis_index("group") * scenes, scenes)
    own = pl.ds(first, scenes)

    part_scr[...] = part_ref[...]
    outside(packet_refs, ajac_ref, ejac_ref, part_scr, cjac_ref.shape[0])
    if step == 0:
        out_obs_ref[...] = part_scr[...]
        now_res_ref = res_ref
    else:
        now, alpha, beta = scalars(packet_refs, None if step == 1 else scal_ref, step - 1)
        out_scal_ref[...] = jnp.zeros_like(out_scal_ref)
        out_scal_ref[0:1, :] = now
        out_scal_ref[1:2, :] = alpha
        alpha, beta = wide(alpha), wide(beta)
        image, shadow, direction = field_ref[...], part_scr[...], res_ref[own]
        if step >= 2:
            image = image + beta * image_ref[...]
            shadow = shadow + beta * shadow_ref[...]
            direction = direction + beta * dir_ref[...]
            out_x_ref[...] = x_ref[...] + alpha * direction
        else:
            out_x_ref[...] = alpha * direction
        out_image_ref[...] = image
        out_shadow_ref[...] = shadow
        out_dir_ref[...] = direction
        out_res_ref[...] = res_ref[...] - alpha * image
        out_obs_ref[...] = obs_ref[...] - alpha * shadow
        now_res_ref = out_res_ref
    r1, r2 = out_obs_ref[:, :ties], out_obs_ref[:, ties:]
    q1_ref[...], q2_ref[...] = settled(coef_ref[0], coef_ref[1], coef_ref[2], r1, r2)
    c_ref[...] = backward(q1_ref, q2_ref, put1_ref, put2_ref, cjac_ref, ajac_ref, ejac_ref, t1_ref, t2_ref)
    inside = now_res_ref[own]
    damped = jnp.zeros_like(inside)
    for i in range(scenes):
        damped = jnp.where(row_of(inside.shape) == i, damp_ref[0, i] * inside, damped)
    c_ref[own] = c_ref[own] + damped
    sent_ref[...] = c_ref[...].astype(BF16)


def final_kernel(step, scenes, *refs):
    field_ref, m, a, b, c, res_ref, image_ref, dir_ref, x_ref, scal_ref, out_x_ref, out_res_ref = refs
    own = pl.ds(pl.multiple_of(lax.axis_index("group") * scenes, scenes), scenes)
    now, alpha, beta = scalars((m, a, b, c), scal_ref, step)
    alpha, beta = wide(alpha), wide(beta)
    res = res_ref[own]
    out_x_ref[...] = x_ref[...] + alpha * (res + beta * dir_ref[...])
    out_res_ref[...] = res - alpha * (field_ref[own] + beta * image_ref[own])


def call(kernel, outs, scratch, name, args, flops=0, spaces={}, limit=None):
    args = [
        pltpu.with_memory_space_constraint(a, pltpu.HBM) if spaces.get(i) == pltpu.HBM else a
        for i, a in enumerate(args)
    ]
    at = lambda i: pl.BlockSpec(memory_space=spaces.get(i, pltpu.VMEM))
    moved = sum(a.size * a.dtype.itemsize for a in args)
    return pl.pallas_call(
        kernel,
        out_shape=[jax.ShapeDtypeStruct(*o) for o in outs],
        in_specs=[at(i) for i in range(len(args))],
        out_specs=[pl.BlockSpec(memory_space=pltpu.VMEM)] * len(outs),
        scratch_shapes=[pltpu.VMEM(*s) if isinstance(s, tuple) else s for s in scratch],
        cost_estimate=pl.CostEstimate(flops=flops, bytes_accessed=moved, transcendentals=0),
        compiler_params=pltpu.CompilerParams(vmem_limit_bytes=limit or VMEM_LIMIT),
        name=name,
    )(*args)


VMEM_LIMIT = 16 << 20


def group_sum_but_last(sent, first=(), between=None):
    size = lax.axis_size("group")
    stride, pairs = 1, None
    while stride < size:
        masks = (1, 2, 3) if 4 * stride <= size else (1,)
        got = [swap(sent, "group", mask * stride) for mask in masks]
        stride *= len(masks) + 1
        pairs = [sent] + got
        if stride < size or len(pairs) > 2:
            low = [p.astype(F32) for p in pairs]
            total = low[0] + low[1]
            if len(low) > 2:
                total = total + (low[2] + low[3])
            if stride < size:
                sent, first = lax.optimization_barrier((total.astype(BF16), first))
                if between is not None:
                    between(sent, first)
                    first, between = (), None
            else:
                pairs = [total]
    return pairs


def swap(block, axis, mask):
    return lax.ppermute(block, axis, [(i, i ^ mask) for i in range(lax.axis_size(axis))])


def orbit_packets(packet):
    n = lax.axis_size("orbit")
    return [packet] + [lax.ppermute(packet, "orbit", [(i, i ^ mask) for i in range(n)]) for mask in range(1, n)]


def on_device(
    along_jac,
    along_res,
    along_e,
    along_count,
    damping,
    cross_jac,
    cross_res,
    cross_e,
    cross_own,
    cross_group,
    cross_other,
):
    scenes, _, ties, width = along_jac.shape[1:]
    links = cross_jac.shape[1]
    groups = lax.axis_size("group")
    rows = groups * scenes
    ajac = along_jac[0].reshape(scenes, 2 * ties, width)
    cjac = cross_jac[0].reshape(links, 2 * ties, width)
    slots = links + scenes + OCTET

    def pass_on(block):
        n = lax.axis_size("orbit")
        return lax.ppermute(block, "orbit", [(i, (i + 1) % n) for i in range(n)])

    work = 2 * (links + scenes + 1) * 32 * 2 * ties * width
    tie = (slots, ties)
    pair = (slots, 2 * ties)
    full = (rows, width)
    own = (scenes, width)
    lanes = -(-slots // 128) * 128
    term_space = [((slots, width), F32)] * 2
    sems = pltpu.SemaphoreType.DMA
    pack_args = (ajac, along_e[0], along_res[0], along_count)
    packed = call(
        pack_kernel,
        [((1, 2 * ties, width), BF16), ((OCTET, ties), F32)],
        [((2, 2, ties), F32), pltpu.SMEM((1, scenes), jnp.int32), sems((4,))],
        "pack",
        pack_args,
        spaces={i: pltpu.HBM for i in range(4)},
    )
    ejac, small = pass_on(packed[0]), pass_on(packed[1])
    blocks = links + scenes
    part_tie = (blocks, ties)
    put = ((rows, slots), BF16)
    pick = ((slots, rows), BF16)
    cjac, ajac, coef, put1, put2, pick1, pick2, t1, t2 = call(
        setup_kernel,
        [
            (cjac.shape, BF16),
            (ajac.shape, BF16),
            ((3,) + part_tie, F32),
            put,
            put,
            pick,
            pick,
            ((blocks, width), F32),
            ((blocks, width), F32),
        ],
        [(part_tie, F32)] * 3
        + [((OCTET, lanes), jnp.int32), sems((blocks // OCTET,))]
        + [((links, 2, ties), F32)] * 2
        + [((scenes, 2, ties), F32)] * 2
        + [pltpu.SMEM((1, scenes), jnp.int32)]
        + [((1, links), jnp.int32)] * 3
        + [sems((8,))],
        "setup",
        (cjac, ajac, cross_e[0], cross_res[0], along_e[0], along_res[0], along_count)
        + (cross_own, cross_group[:, :, 0], cross_other),
        work,
        {i: pltpu.HBM for i in range(10)},
    )
    jacs = (cjac, ajac, ejac)

    def turn(start, count, refs, after):
        outs = [((min(count, j.shape[0]),) + j.shape[1:], BF16) for j in refs]
        share = work * sum(o[0][0] for o in outs) // blocks
        return call(functools.partial(turn_kernel, start), outs, [], "turn", (after,) + refs, share)

    def project(field, turned, refs):
        scratch = [((2, slots, width), F32)] * 2
        kernel = functools.partial(project_kernel, turned)
        return call(kernel, [(pair, F32)], scratch, "project", (field, pick1, pick2) + tuple(refs), work)[0]

    def finish(sums, res=None):
        args = sums if res is None else sums + [res]
        kernel = functools.partial(gather_kernel, scenes, res is None, len(sums))
        field, packet = call(kernel, [(full, F32), ((OCTET, width), F32)], [], "finish", args)
        return field, orbit_packets(packet)

    sent, coef = call(
        rhs_kernel,
        [(full, BF16), ((3,) + tie, F32)],
        term_space,
        "rhs",
        (coef, t1, t2, small, ejac, put1, put2),
        work // blocks,
    )
    half = links // 2
    turned = []

    def more(after, done):
        turned.extend([*done, *turn(half, links - half, (cjac,), after)])

    sums = group_sum_but_last(sent, turn(0, half, (cjac,), sent), more)
    res, packets = finish(sums)
    part = project(res, (True, True, False, False), turned + [ajac, ejac])
    fixed = (coef, put1, put2, damping) + jacs
    damp_at = {8: pltpu.SMEM}
    scratch = [(pair, F32), (tie, F32), (tie, F32)] + term_space + [(full, F32)]
    sent, obs = call(
        functools.partial(step_kernel, 0, scenes),
        [(full, BF16), (pair, F32)],
        scratch,
        "step",
        (part, *packets) + fixed + (res,),
        work,
        damp_at,
    )
    turned += turn(0, scenes, (ajac, ejac), sent)
    state = ()
    x = jnp.zeros(own, F32)
    for step in range(1, ITERS):
        field, packets = finish(group_sum_but_last(sent), res)
        part = project(field, (True,) * 4, turned)
        sent, obs, res, image, shadow, direction, x, scal = call(
            functools.partial(step_kernel, step, scenes),
            [(full, BF16), (pair, F32), (full, F32), (full, F32), (pair, F32), (own, F32), (own, F32), ((OCTET, width // 2), F32)],
            scratch,
            "step",
            (part, *packets) + fixed + (res, field, obs, x) + state,
            work,
            damp_at,
        )
        state = (image, shadow, direction, scal)
    field, packets = finish(group_sum_but_last(sent), res)
    x, res = call(
        functools.partial(final_kernel, ITERS - 1, scenes),
        [(own, F32), (own, F32)],
        [],
        "final",
        (field, *packets, res, image, direction, x, scal),
    )
    return x[None], res[None]


def solution(mesh):
    placed = (
        P("group", "orbit", None, None, None),
        P("group", "orbit", None, None),
        P("group", "orbit", None, None),
        P("group", "orbit"),
        P("group", "orbit"),
        P("group", "orbit", None, None, None),
        P("group", "orbit", None, None),
        P("group", "orbit", None, None),
        P("group", "orbit"),
        P("group", "orbit", None),
        P("group", "orbit"),
    )
    return jax.shard_map(
        on_device,
        mesh=mesh,
        in_specs=placed,
        out_specs=(P("group", "orbit", None), P("group", "orbit", None)),
        check_vma=False,
    )
```

```python
import functools

import jax
import jax.numpy as jnp
from jax import lax
from jax.experimental import pallas as pl
from jax.experimental.pallas import tpu as pltpu
from jax.sharding import PartitionSpec as P

ITERS = 4
F32, BF16 = jnp.float32, jnp.bfloat16
OCTET = 8


def dot(a, b):
    return lax.dot_general(a, b, (((1,), (0,)), ((), ())), preferred_element_type=F32)


def dot_t(a, b):
    return lax.dot_general(a, b, (((1,), (1,)), ((), ())), preferred_element_type=F32)


def halves(x):
    high = x.astype(BF16)
    return high, (x - high.astype(F32)).astype(BF16)


def row_of(shape):
    return lax.broadcasted_iota(jnp.int32, shape, 0)


def octets(refs, body):
    slot = 0
    for number, ref in enumerate(refs):
        blocks = ref.shape[0]
        for at in range(0, blocks, OCTET):
            body(number, ref, at, slot + at, min(OCTET, blocks - at))
        slot += -(-blocks // OCTET) * OCTET


def project_kernel(turned, field_ref, pick1_ref, pick2_ref, *refs):
    *jac_refs, out_ref, l1_ref, l2_ref = refs
    product = [dot if is_turned else dot_t for is_turned in turned]
    ties = out_ref.shape[1] // 2
    high, low = halves(field_ref[...])
    for pick_ref, left_ref in ((pick1_ref, l1_ref), (pick2_ref, l2_ref)):
        left_ref[0] = dot(pick_ref[...], high)
        left_ref[1] = dot(pick_ref[...], low)

    def body(number, ref, at, slot, count):
        rows = pl.ds(slot, OCTET)
        left = jnp.concatenate([l1_ref[0, rows], l2_ref[0, rows], l1_ref[1, rows], l2_ref[1, rows]])
        left = left.astype(BF16)
        total = jnp.zeros((OCTET, 2 * ties), F32)
        for j in range(count):
            got = product[number](left, ref[at + j])
            one = got[0:8, :ties] + got[16:24, :ties]
            two = got[8:16, ties:] + got[24:32, ties:]
            got = jnp.concatenate([one, two], axis=1)
            total = jnp.where(row_of(total.shape) == j, got, total)
        out_ref[rows] = total

    octets(jac_refs, body)


def turn_kernel(start, after_ref, *refs):
    half = len(refs) // 2
    for ref, out_ref in zip(refs[:half], refs[half:]):

        @pl.loop(0, out_ref.shape[0])
        def _(i, ref=ref, out_ref=out_ref):
            out_ref[i] = ref[start + i].T


def terms(q1, q2, ref, at, count):
    zero = jnp.zeros_like(q1)
    total = jnp.zeros((2 * OCTET, ref.shape[2]), F32)
    for j in range(count):
        chosen = row_of(q1.shape) == j
        top = jnp.concatenate([jnp.where(chosen, q1, 0.0), zero], axis=1)
        low = jnp.concatenate([zero, jnp.where(chosen, q2, 0.0)], axis=1)
        total = total + dot(jnp.concatenate([top, low]).astype(BF16), ref[at + j])
    return total[:OCTET], total[OCTET:]


def scatter(t1_ref, t2_ref, put1_ref, put2_ref):
    out = None
    for t_ref, put_ref in ((t1_ref, put1_ref), (t2_ref, put2_ref)):
        for part in halves(t_ref[...]):
            term = dot(put_ref[...], part)
            out = term if out is None else out + term
    return out


def backward(q1_ref, q2_ref, put1_ref, put2_ref, cjac_ref, ajac_ref, ejac_ref, t1_ref, t2_ref):
    def body(number, ref, at, slot, count):
        rows = pl.ds(slot, OCTET)
        t1_ref[rows], t2_ref[rows] = terms(q1_ref[rows], q2_ref[rows], ref, at, count)

    octets((cjac_ref, ajac_ref, ejac_ref), body)
    return scatter(t1_ref, t2_ref, put1_ref, put2_ref)


def elimination(e1, e2, live):
    over = live / (1.0 + e1 * e1 + e2 * e2)
    return (1.0 + e2 * e2) * over, e1 * e2 * over, (1.0 + e1 * e1) * over


def settled(c11, c12, c22, r1, r2):
    return c11 * r1 - c12 * r2, c22 * r2 - c12 * r1


def live_rows(count_ref, out_ref):
    lane = lax.broadcasted_iota(jnp.int32, (1, out_ref.shape[1]), 1)
    for i in range(out_ref.shape[0]):
        out_ref[i : i + 1, :] = jnp.where(lane < count_ref[0, i], 1.0, 0.0)


def fetch(pairs, sems):
    copies = [pltpu.make_async_copy(a, b, sems.at[i]) for i, (a, b) in enumerate(pairs)]
    for copy in copies:
        copy.start()
    return copies


def pack_kernel(jac_ref, e_ref, res_ref, count_ref, out_jac_ref, out_ref, pair_ref, tally_ref, sems):
    last = jac_ref.shape[0] - 1
    block = pl.ds(last, 1)
    copies = fetch(
        [
            (jac_ref.at[block], out_jac_ref),
            (e_ref.at[block], pair_ref.at[0:1]),
            (res_ref.at[block], pair_ref.at[1:2]),
            (count_ref, tally_ref),
        ],
        sems,
    )
    for copy in copies[1:]:
        copy.wait()
    lane = lax.broadcasted_iota(jnp.int32, (1, out_ref.shape[1]), 1)
    out_ref[...] = jnp.zeros_like(out_ref)
    out_ref[0:2, :] = pair_ref[0]
    out_ref[2:4, :] = pair_ref[1]
    out_ref[4:5, :] = jnp.where(lane < tally_ref[0, last], 1.0, 0.0)
    copies[0].wait()


def setup_kernel(cjac_ref, ajac_ref, *refs):
    far_refs, refs = refs[:9], refs[9:]
    (out_cjac_ref, out_ajac_ref, coef_ref, put1_ref, put2_ref, pick1_ref, pick2_ref, t1_ref, t2_ref, damp_ref) = refs[:10]
    live_ref, q1_ref, q2_ref, index_ref, sems = refs[10:15]
    near_refs, near_sems = refs[15:24], refs[24]
    near = fetch(list(zip(far_refs, near_refs)), near_sems)
    ce_ref, cres_ref, ae_ref, ares_ref, count_ref, own_ref, group_ref, other_ref, scale_ref = near_refs
    copies = []
    for ref, out_ref in ((cjac_ref, out_cjac_ref), (ajac_ref, out_ajac_ref)):
        for at in range(0, ref.shape[0], OCTET):
            part = pl.ds(at, OCTET)
            copies.append(pltpu.make_async_copy(ref.at[part], out_ref.at[part], sems.at[len(copies)]))
            copies[-1].start()
    links, scenes = cjac_ref.shape[0], ajac_ref.shape[0]
    blocks = links + scenes
    for copy in near:
        copy.wait()
    live_ref[0:links] = jnp.ones((links, live_ref.shape[1]), F32)
    live_rows(count_ref, live_ref.at[links:blocks])
    for i in range(scenes):
        damp_ref[i : i + 1, :] = jnp.full((1, damp_ref.shape[1]), scale_ref[0, i], F32)
    for rows, e_ref, res_ref in ((slice(0, links), ce_ref, cres_ref), (slice(links, blocks), ae_ref, ares_ref)):
        c = elimination(e_ref[:, 0, :], e_ref[:, 1, :], live_ref[rows])
        for i in range(3):
            coef_ref[i, rows] = c[i]
        q1_ref[rows], q2_ref[rows] = settled(*c, res_ref[:, 0, :], res_ref[:, 1, :])

    first = lax.axis_index("group") * scenes
    slots = put1_ref.shape[1]
    index_ref[...] = jnp.zeros_like(index_ref)
    index_ref[0:1, :links] = own_ref[...] + first
    index_ref[1:2, :links] = group_ref[...] * scenes + other_ref[...]
    lane = lax.broadcasted_iota(jnp.int32, (1, index_ref.shape[1]), 1)
    one = jnp.where(lane < links, index_ref[0:1, :], jnp.where(lane < blocks, first + lane - links, -1))
    two = jnp.where(lane < blocks - 1, first + lane - links + 1, jnp.where(lane == blocks, first, -1))
    two = jnp.where(lane < links, index_ref[1:2, :], two)
    for index, put_ref, pick_ref in ((one, put1_ref, pick1_ref), (two, put2_ref, pick2_ref)):
        shape = (put_ref.shape[0], index.shape[1])
        table = jnp.where(row_of(shape) == index, 1.0, 0.0)
        put_ref[...] = table[:, :slots].astype(BF16)
        pick_ref[...] = table.T[:slots].astype(BF16)

    octet = 0
    for ref in (out_cjac_ref, out_ajac_ref):
        for at in range(0, ref.shape[0], OCTET):
            copies[octet].wait()
            rows = pl.ds(octet * OCTET, OCTET)
            t1_ref[rows], t2_ref[rows] = terms(q1_ref[rows], q2_ref[rows], ref, at, OCTET)
            octet += 1


def rhs_kernel(coef_ref, t1_ref, t2_ref, small_ref, ejac_ref, put1_ref, put2_ref, out_ref, out_coef_ref, all1_ref, all2_ref):
    blocks = t1_ref.shape[0]
    rows = pl.ds(blocks, OCTET)
    e1, e2, r1, r2, live = (small_ref[i : i + 1, :] for i in range(5))
    c = elimination(e1, e2, live)
    fill = lambda x: jnp.where(row_of((OCTET, x.shape[1])) == 0, x, 0.0)
    for i in range(3):
        out_coef_ref[i, :blocks] = coef_ref[i]
        out_coef_ref[i, rows] = fill(c[i])
    q1, q2 = settled(*c, r1, r2)
    all1_ref[:blocks] = t1_ref[...]
    all2_ref[:blocks] = t2_ref[...]
    all1_ref[rows], all2_ref[rows] = terms(fill(q1), fill(q2), ejac_ref, 0, 1)
    out_ref[...] = scatter(all1_ref, all2_ref, put1_ref, put2_ref).astype(BF16)


def gather_kernel(scenes, start, parts, *refs):
    first = pl.multiple_of(lax.axis_index("group") * scenes, scenes)
    field = refs[0][...].astype(F32)
    for ref in refs[1:parts]:
        field = field + ref[...].astype(F32)
    refs = refs[parts:]
    if start:
        out_ref, packet_ref = refs
        field = -field
    else:
        res_ref, out_ref, packet_ref = refs
    out_ref[...] = field
    packet_ref[...] = jnp.zeros_like(packet_ref)
    if not start:
        res = res_ref[...]
        half = packet_ref.shape[1] // 2
        packet_ref[0:1, :half] = jnp.full((1, half), jnp.sum(res * res), F32)
        packet_ref[0:1, half:] = jnp.full((1, half), jnp.sum(res * field), F32)
    packet_ref[1:2, :] = out_ref[pl.ds(first, OCTET), :][0:1]
    packet_ref[2:3, :] = out_ref[pl.ds(pl.multiple_of(first + scenes - OCTET, OCTET), OCTET), :][OCTET - 1 :]


def outside(packet_refs, ajac_ref, ejac_ref, part_ref, slot):
    _, one, _, three = packet_refs
    ties = part_ref.shape[1] // 2
    last = ajac_ref.shape[0] - 1
    even = lax.axis_index("orbit") % 2 == 0
    after = jnp.where(even, one[1:2, :], three[1:2, :])
    ahead = jnp.where(even, three[2:3, :], one[2:3, :])
    sub = row_of((OCTET, after.shape[1]))
    both = jnp.where(sub == last % OCTET, after, jnp.where(sub == 0, ahead, 0.0))
    high = both.astype(BF16).astype(F32)
    left = jnp.concatenate([high, both - high]).astype(BF16)
    got = dot_t(left, ajac_ref[last])
    got = got[:OCTET] + got[OCTET:]
    tail = pl.ds(slot + last - last % OCTET, OCTET)
    keep = row_of((OCTET, ties)) == last % OCTET
    part_ref[tail, ties:] = part_ref[tail, ties:] + jnp.where(keep, got[:, ties:], 0.0)
    got = dot_t(left, ejac_ref[0])
    got = got[:OCTET] + got[OCTET:]
    tail = pl.ds(slot + last + 1, OCTET)
    keep = row_of((OCTET, ties)) == 0
    part_ref[tail, :ties] = part_ref[tail, :ties] + jnp.where(keep, got[:, :ties], 0.0)


def scalars(packet_refs, scal_ref, step):
    mine, one, two, three = (ref[0:1, :] for ref in packet_refs)
    sums = (mine + one) + (two + three)
    half = sums.shape[1] // 2
    now, along = sums[:, :half], sums[:, half:]
    if step == 0:
        beta = jnp.zeros_like(now)
        alpha = now / along
    else:
        before, last = scal_ref[0:1, :], scal_ref[1:2, :]
        beta = now / before
        alpha = now / (along - beta * now / last)
    return now, alpha, beta


def wide(x):
    return jnp.concatenate([x, x], axis=1)


def step_kernel(step, scenes, *refs):
    refs = list(refs)
    take = lambda n: [refs.pop(0) for _ in range(n)]
    (part_ref,) = take(1)
    packet_refs = take(4)
    coef_ref, put1_ref, put2_ref, damp_ref, cjac_ref, ajac_ref, ejac_ref = take(7)
    (res_ref,) = take(1)
    if step >= 1:
        field_ref, obs_ref, x_ref = take(3)
    if step >= 2:
        image_ref, shadow_ref, dir_ref, scal_ref = take(4)
    (sent_ref, out_obs_ref) = take(2)
    if step >= 1:
        out_res_ref, out_image_ref, out_shadow_ref, out_dir_ref, out_x_ref, out_scal_ref = take(6)
    part_scr, q1_ref, q2_ref, t1_ref, t2_ref, c_ref = take(6)
    ties = q1_ref.shape[1]
    first = pl.multiple_of(lax.axis_index("group") * scenes, scenes)
    own = pl.ds(first, scenes)

    part_scr[...] = part_ref[...]
    outside(packet_refs, ajac_ref, ejac_ref, part_scr, cjac_ref.shape[0])
    if step == 0:
        out_obs_ref[...] = part_scr[...]
        now_res_ref = res_ref
    else:
        now, alpha, beta = scalars(packet_refs, None if step == 1 else scal_ref, step - 1)
        out_scal_ref[...] = jnp.zeros_like(out_scal_ref)
        out_scal_ref[0:1, :] = now
        out_scal_ref[1:2, :] = alpha
        alpha, beta = wide(alpha), wide(beta)
        image, shadow, direction = field_ref[...], part_scr[...], res_ref[own]
        if step >= 2:
            image = image + beta * image_ref[...]
            shadow = shadow + beta * shadow_ref[...]
            direction = direction + beta * dir_ref[...]
            out_x_ref[...] = x_ref[...] + alpha * direction
        else:
            out_x_ref[...] = alpha * direction
        out_image_ref[...] = image
        out_shadow_ref[...] = shadow
        out_dir_ref[...] = direction
        out_res_ref[...] = res_ref[...] - alpha * image
        out_obs_ref[...] = obs_ref[...] - alpha * shadow
        now_res_ref = out_res_ref
    r1, r2 = out_obs_ref[:, :ties], out_obs_ref[:, ties:]
    q1_ref[...], q2_ref[...] = settled(coef_ref[0], coef_ref[1], coef_ref[2], r1, r2)
    c_ref[...] = backward(q1_ref, q2_ref, put1_ref, put2_ref, cjac_ref, ajac_ref, ejac_ref, t1_ref, t2_ref)
    c_ref[own] = c_ref[own] + damp_ref[...] * now_res_ref[own]
    sent_ref[...] = c_ref[...].astype(BF16)


def final_kernel(step, scenes, *refs):
    field_ref, m, a, b, c, res_ref, image_ref, dir_ref, x_ref, scal_ref, out_x_ref, out_res_ref = refs
    own = pl.ds(pl.multiple_of(lax.axis_index("group") * scenes, scenes), scenes)
    now, alpha, beta = scalars((m, a, b, c), scal_ref, step)
    alpha, beta = wide(alpha), wide(beta)
    res = res_ref[own]
    out_x_ref[...] = x_ref[...] + alpha * (res + beta * dir_ref[...])
    out_res_ref[...] = res - alpha * (field_ref[own] + beta * image_ref[own])


def call(kernel, outs, scratch, name, args, flops=0, spaces={}, limit=None):
    args = [
        pltpu.with_memory_space_constraint(a, pltpu.HBM) if spaces.get(i) == pltpu.HBM else a
        for i, a in enumerate(args)
    ]
    at = lambda i: pl.BlockSpec(memory_space=spaces.get(i, pltpu.VMEM))
    moved = sum(a.size * a.dtype.itemsize for a in args)
    return pl.pallas_call(
        kernel,
        out_shape=[jax.ShapeDtypeStruct(*o) for o in outs],
        in_specs=[at(i) for i in range(len(args))],
        out_specs=[pl.BlockSpec(memory_space=pltpu.VMEM)] * len(outs),
        scratch_shapes=[pltpu.VMEM(*s) if isinstance(s, tuple) else s for s in scratch],
        cost_estimate=pl.CostEstimate(flops=flops, bytes_accessed=moved, transcendentals=0),
        compiler_params=pltpu.CompilerParams(vmem_limit_bytes=limit or VMEM_LIMIT),
        name=name,
    )(*args)


VMEM_LIMIT = 16 << 20


def group_sum_but_last(sent, first=(), between=None):
    size = lax.axis_size("group")
    stride, pairs = 1, None
    while stride < size:
        masks = (1, 2, 3) if 4 * stride <= size else (1,)
        got = [swap(sent, "group", mask * stride) for mask in masks]
        stride *= len(masks) + 1
        pairs = [sent] + got
        if stride < size or len(pairs) > 2:
            low = [p.astype(F32) for p in pairs]
            total = low[0] + low[1]
            if len(low) > 2:
                total = total + (low[2] + low[3])
            if stride < size:
                sent, first = lax.optimization_barrier((total.astype(BF16), first))
                if between is not None:
                    between(sent, first)
                    first, between = (), None
            else:
                pairs = [total]
    return pairs


def swap(block, axis, mask):
    return lax.ppermute(block, axis, [(i, i ^ mask) for i in range(lax.axis_size(axis))])


def orbit_packets(packet):
    n = lax.axis_size("orbit")
    return [packet] + [lax.ppermute(packet, "orbit", [(i, i ^ mask) for i in range(n)]) for mask in range(1, n)]


def on_device(
    along_jac,
    along_res,
    along_e,
    along_count,
    damping,
    cross_jac,
    cross_res,
    cross_e,
    cross_own,
    cross_group,
    cross_other,
):
    scenes, _, ties, width = along_jac.shape[1:]
    links = cross_jac.shape[1]
    groups = lax.axis_size("group")
    rows = groups * scenes
    ajac = along_jac[0].reshape(scenes, 2 * ties, width)
    cjac = cross_jac[0].reshape(links, 2 * ties, width)
    slots = links + scenes + OCTET

    def pass_on(block):
        n = lax.axis_size("orbit")
        return lax.ppermute(block, "orbit", [(i, (i + 1) % n) for i in range(n)])

    work = 2 * (links + scenes + 1) * 32 * 2 * ties * width
    tie = (slots, ties)
    pair = (slots, 2 * ties)
    full = (rows, width)
    own = (scenes, width)
    lanes = -(-slots // 128) * 128
    term_space = [((slots, width), F32)] * 2
    sems = pltpu.SemaphoreType.DMA
    pack_args = (ajac, along_e[0], along_res[0], along_count)
    packed = call(
        pack_kernel,
        [((1, 2 * ties, width), BF16), ((OCTET, ties), F32)],
        [((2, 2, ties), F32), pltpu.SMEM((1, scenes), jnp.int32), sems((4,))],
        "pack",
        pack_args,
        spaces={i: pltpu.HBM for i in range(4)},
    )
    ejac, small = pass_on(packed[0]), pass_on(packed[1])
    blocks = links + scenes
    part_tie = (blocks, ties)
    put = ((rows, slots), BF16)
    pick = ((slots, rows), BF16)
    cjac, ajac, coef, put1, put2, pick1, pick2, t1, t2, damp = call(
        setup_kernel,
        [
            (cjac.shape, BF16),
            (ajac.shape, BF16),
            ((3,) + part_tie, F32),
            put,
            put,
            pick,
            pick,
            ((blocks, width), F32),
            ((blocks, width), F32),
            (own, F32),
        ],
        [(part_tie, F32)] * 3
        + [((OCTET, lanes), jnp.int32), sems((blocks // OCTET,))]
        + [((links, 2, ties), F32)] * 2
        + [((scenes, 2, ties), F32)] * 2
        + [pltpu.SMEM((1, scenes), jnp.int32)]
        + [((1, links), jnp.int32)] * 3
        + [pltpu.SMEM((1, scenes), F32), sems((9,))],
        "setup",
        (cjac, ajac, cross_e[0], cross_res[0], along_e[0], along_res[0], along_count)
        + (cross_own, cross_group[:, :, 0], cross_other, damping),
        work,
        {i: pltpu.HBM for i in range(11)},
    )
    jacs = (cjac, ajac, ejac)

    def turn(start, count, refs, after):
        outs = [((min(count, j.shape[0]),) + j.shape[1:], BF16) for j in refs]
        share = work * sum(o[0][0] for o in outs) // blocks
        return call(functools.partial(turn_kernel, start), outs, [], "turn", (after,) + refs, share)

    def project(field, turned, refs):
        scratch = [((2, slots, width), F32)] * 2
        kernel = functools.partial(project_kernel, turned)
        return call(kernel, [(pair, F32)], scratch, "project", (field, pick1, pick2) + tuple(refs), work)[0]

    def finish(sums, res=None):
        args = sums if res is None else sums + [res]
        kernel = functools.partial(gather_kernel, scenes, res is None, len(sums))
        field, packet = call(kernel, [(full, F32), ((OCTET, width), F32)], [], "finish", args)
        return field, orbit_packets(packet)

    sent, coef = call(
        rhs_kernel,
        [(full, BF16), ((3,) + tie, F32)],
        term_space,
        "rhs",
        (coef, t1, t2, small, ejac, put1, put2),
        work // blocks,
    )
    half = links // 2
    turned = []

    def more(after, done):
        turned.extend([*done, *turn(half, links - half, (cjac,), after)])

    sums = group_sum_but_last(sent, turn(0, half, (cjac,), sent), more)
    res, packets = finish(sums)
    part = project(res, (True, True, False, False), turned + [ajac, ejac])
    fixed = (coef, put1, put2, damp) + jacs
    scratch = [(pair, F32), (tie, F32), (tie, F32)] + term_space + [(full, F32)]
    sent, obs = call(
        functools.partial(step_kernel, 0, scenes),
        [(full, BF16), (pair, F32)],
        scratch,
        "step",
        (part, *packets) + fixed + (res,),
        work,
    )
    turned += turn(0, scenes, (ajac, ejac), sent)
    state = ()
    x = jnp.zeros(own, F32)
    for step in range(1, ITERS):
        field, packets = finish(group_sum_but_last(sent), res)
        part = project(field, (True,) * 4, turned)
        sent, obs, res, image, shadow, direction, x, scal = call(
            functools.partial(step_kernel, step, scenes),
            [(full, BF16), (pair, F32), (full, F32), (full, F32), (pair, F32), (own, F32), (own, F32), ((OCTET, width // 2), F32)],
            scratch,
            "step",
            (part, *packets) + fixed + (res, field, obs, x) + state,
            work,
        )
        state = (image, shadow, direction, scal)
    field, packets = finish(group_sum_but_last(sent), res)
    x, res = call(
        functools.partial(final_kernel, ITERS - 1, scenes),
        [(own, F32), (own, F32)],
        [],
        "final",
        (field, *packets, res, image, direction, x, scal),
    )
    return x[None], res[None]


def solution(mesh):
    placed = (
        P("group", "orbit", None, None, None),
        P("group", "orbit", None, None),
        P("group", "orbit", None, None),
        P("group", "orbit"),
        P("group", "orbit"),
        P("group", "orbit", None, None, None),
        P("group", "orbit", None, None),
        P("group", "orbit", None, None),
        P("group", "orbit"),
        P("group", "orbit", None),
        P("group", "orbit"),
    )
    return jax.shard_map(
        on_device,
        mesh=mesh,
        in_specs=placed,
        out_specs=(P("group", "orbit", None), P("group", "orbit", None)),
        check_vma=False,
    )
```

```python
import functools

import jax
import jax.numpy as jnp
from jax import lax
from jax.experimental import pallas as pl
from jax.experimental.pallas import tpu as pltpu
from jax.sharding import PartitionSpec as P

ITERS = 4
F32, BF16 = jnp.float32, jnp.bfloat16
OCTET = 8


def dot(a, b):
    return lax.dot_general(a, b, (((1,), (0,)), ((), ())), preferred_element_type=F32)


def dot_t(a, b):
    return lax.dot_general(a, b, (((1,), (1,)), ((), ())), preferred_element_type=F32)


def halves(x):
    high = x.astype(BF16)
    return high, (x - high.astype(F32)).astype(BF16)


def row_of(shape):
    return lax.broadcasted_iota(jnp.int32, shape, 0)


def octets(refs, body):
    slot = 0
    for number, ref in enumerate(refs):
        blocks = ref.shape[0]
        for at in range(0, blocks, OCTET):
            body(number, ref, at, slot + at, min(OCTET, blocks - at))
        slot += -(-blocks // OCTET) * OCTET


def project_kernel(turned, field_ref, pick1_ref, pick2_ref, *refs):
    *jac_refs, out_ref, l1_ref, l2_ref = refs
    product = [dot if is_turned else dot_t for is_turned in turned]
    ties = out_ref.shape[1] // 2
    high, low = halves(field_ref[...])
    for pick_ref, left_ref in ((pick1_ref, l1_ref), (pick2_ref, l2_ref)):
        left_ref[0] = dot(pick_ref[...], high)
        left_ref[1] = dot(pick_ref[...], low)

    def body(number, ref, at, slot, count):
        rows = pl.ds(slot, OCTET)
        left = jnp.concatenate([l1_ref[0, rows], l2_ref[0, rows], l1_ref[1, rows], l2_ref[1, rows]])
        left = left.astype(BF16)
        total = jnp.zeros((OCTET, 2 * ties), F32)
        for j in range(count):
            got = product[number](left, ref[at + j])
            one = got[0:8, :ties] + got[16:24, :ties]
            two = got[8:16, ties:] + got[24:32, ties:]
            got = jnp.concatenate([one, two], axis=1)
            total = jnp.where(row_of(total.shape) == j, got, total)
        out_ref[rows] = total

    octets(jac_refs, body)


def turn_kernel(start, after_ref, *refs):
    half = len(refs) // 2
    for ref, out_ref in zip(refs[:half], refs[half:]):

        @pl.loop(0, out_ref.shape[0])
        def _(i, ref=ref, out_ref=out_ref):
            out_ref[i] = ref[start + i].T


def terms(q1, q2, ref, at, count):
    zero = jnp.zeros_like(q1)
    total = jnp.zeros((2 * OCTET, ref.shape[2]), F32)
    for j in range(count):
        chosen = row_of(q1.shape) == j
        top = jnp.concatenate([jnp.where(chosen, q1, 0.0), zero], axis=1)
        low = jnp.concatenate([zero, jnp.where(chosen, q2, 0.0)], axis=1)
        total = total + dot(jnp.concatenate([top, low]).astype(BF16), ref[at + j])
    return total[:OCTET], total[OCTET:]


def scatter(t1_ref, t2_ref, put1_ref, put2_ref):
    out = None
    for t_ref, put_ref in ((t1_ref, put1_ref), (t2_ref, put2_ref)):
        for part in halves(t_ref[...]):
            term = dot(put_ref[...], part)
            out = term if out is None else out + term
    return out


def backward(q1_ref, q2_ref, put1_ref, put2_ref, cjac_ref, ajac_ref, ejac_ref, t1_ref, t2_ref):
    def body(number, ref, at, slot, count):
        rows = pl.ds(slot, OCTET)
        t1_ref[rows], t2_ref[rows] = terms(q1_ref[rows], q2_ref[rows], ref, at, count)

    octets((cjac_ref, ajac_ref, ejac_ref), body)
    return scatter(t1_ref, t2_ref, put1_ref, put2_ref)


def elimination(e1, e2, live):
    over = live / (1.0 + e1 * e1 + e2 * e2)
    return (1.0 + e2 * e2) * over, e1 * e2 * over, (1.0 + e1 * e1) * over


def settled(c11, c12, c22, r1, r2):
    return c11 * r1 - c12 * r2, c22 * r2 - c12 * r1


def live_rows(count_ref, out_ref):
    lane = lax.broadcasted_iota(jnp.int32, (1, out_ref.shape[1]), 1)
    for i in range(out_ref.shape[0]):
        out_ref[i : i + 1, :] = jnp.where(lane < count_ref[0, i], 1.0, 0.0)


def fetch(pairs, sems):
    copies = [pltpu.make_async_copy(a, b, sems.at[i]) for i, (a, b) in enumerate(pairs)]
    for copy in copies:
        copy.start()
    return copies


def pack_kernel(jac_ref, e_ref, res_ref, count_ref, out_ref, pair_ref, tally_ref, wide_ref, sems):
    last = jac_ref.shape[0] - 1
    block = pl.ds(last, 1)
    height = jac_ref.shape[1]
    copies = fetch(
        [
            (jac_ref.at[block], out_ref.at[:, :height]),
            (e_ref.at[block], pair_ref.at[0:1]),
            (res_ref.at[block], pair_ref.at[1:2]),
            (count_ref, tally_ref),
        ],
        sems,
    )
    for copy in copies[1:]:
        copy.wait()
    ties = pair_ref.shape[2]
    lane = lax.broadcasted_iota(jnp.int32, (1, ties), 1)
    wide_ref[...] = jnp.zeros_like(wide_ref)
    for i in range(2):
        rest = pair_ref[i]
        for j in range(3):
            part = rest.astype(BF16).astype(F32)
            rest = rest - part
            wide_ref[4 * j + 2 * i : 4 * j + 2 * i + 2, :ties] = part
    wide_ref[12:13, :ties] = jnp.where(lane < tally_ref[0, last], 1.0, 0.0)
    out_ref[0, height:] = wide_ref[...].astype(BF16)
    copies[0].wait()


def setup_kernel(cjac_ref, ajac_ref, *refs):
    far_refs, refs = refs[:9], refs[9:]
    (out_cjac_ref, out_ajac_ref, coef_ref, put1_ref, put2_ref, pick1_ref, pick2_ref, t1_ref, t2_ref, damp_ref) = refs[:10]
    live_ref, q1_ref, q2_ref, index_ref, sems = refs[10:15]
    near_refs, near_sems = refs[15:24], refs[24]
    near = fetch(list(zip(far_refs, near_refs)), near_sems)
    ce_ref, cres_ref, ae_ref, ares_ref, count_ref, own_ref, group_ref, other_ref, scale_ref = near_refs
    copies = []
    for ref, out_ref in ((cjac_ref, out_cjac_ref), (ajac_ref, out_ajac_ref)):
        for at in range(0, ref.shape[0], OCTET):
            part = pl.ds(at, OCTET)
            copies.append(pltpu.make_async_copy(ref.at[part], out_ref.at[part], sems.at[len(copies)]))
    for copy in copies[:2]:
        copy.start()
    links, scenes = cjac_ref.shape[0], ajac_ref.shape[0]
    blocks = links + scenes
    for copy in near:
        copy.wait()
    for copy in copies[2:]:
        copy.start()
    live_ref[0:links] = jnp.ones((links, live_ref.shape[1]), F32)
    live_rows(count_ref, live_ref.at[links:blocks])
    for i in range(scenes):
        damp_ref[i : i + 1, :] = jnp.full((1, damp_ref.shape[1]), scale_ref[0, i], F32)
    for rows, e_ref, res_ref in ((slice(0, links), ce_ref, cres_ref), (slice(links, blocks), ae_ref, ares_ref)):
        c = elimination(e_ref[:, 0, :], e_ref[:, 1, :], live_ref[rows])
        for i in range(3):
            coef_ref[i, rows] = c[i]
        q1_ref[rows], q2_ref[rows] = settled(*c, res_ref[:, 0, :], res_ref[:, 1, :])

    first = lax.axis_index("group") * scenes
    slots = put1_ref.shape[1]
    index_ref[...] = jnp.zeros_like(index_ref)
    index_ref[0:1, :links] = own_ref[...] + first
    index_ref[1:2, :links] = group_ref[...] * scenes + other_ref[...]
    lane = lax.broadcasted_iota(jnp.int32, (1, index_ref.shape[1]), 1)
    one = jnp.where(lane < links, index_ref[0:1, :], jnp.where(lane < blocks, first + lane - links, -1))
    two = jnp.where(lane < blocks - 1, first + lane - links + 1, jnp.where(lane == blocks, first, -1))
    two = jnp.where(lane < links, index_ref[1:2, :], two)
    for index, put_ref, pick_ref in ((one, put1_ref, pick1_ref), (two, put2_ref, pick2_ref)):
        shape = (put_ref.shape[0], index.shape[1])
        table = jnp.where(row_of(shape) == index, 1.0, 0.0)
        put_ref[...] = table[:, :slots].astype(BF16)
        pick_ref[...] = table.T[:slots].astype(BF16)

    octet = 0
    for ref in (out_cjac_ref, out_ajac_ref):
        for at in range(0, ref.shape[0], OCTET):
            copies[octet].wait()
            rows = pl.ds(octet * OCTET, OCTET)
            t1_ref[rows], t2_ref[rows] = terms(q1_ref[rows], q2_ref[rows], ref, at, OCTET)
            octet += 1


def rhs_kernel(coef_ref, t1_ref, t2_ref, edge_ref, put1_ref, put2_ref, out_ref, out_coef_ref, ejac_ref, all1_ref, all2_ref):
    blocks, ties = t1_ref.shape[0], coef_ref.shape[2]
    height = ejac_ref.shape[1]
    rows = pl.ds(blocks, OCTET)
    ejac_ref[...] = edge_ref[:, :height]
    parts = edge_ref[0, height:, :ties].astype(F32)
    e1, e2, r1, r2 = (parts[i : i + 1] + parts[i + 4 : i + 5] + parts[i + 8 : i + 9] for i in range(4))
    c = elimination(e1, e2, parts[12:13])
    fill = lambda x: jnp.where(row_of((OCTET, x.shape[1])) == 0, x, 0.0)
    for i in range(3):
        out_coef_ref[i, :blocks] = coef_ref[i]
        out_coef_ref[i, rows] = fill(c[i])
    q1, q2 = settled(*c, r1, r2)
    all1_ref[:blocks] = t1_ref[...]
    all2_ref[:blocks] = t2_ref[...]
    all1_ref[rows], all2_ref[rows] = terms(fill(q1), fill(q2), ejac_ref, 0, 1)
    out_ref[...] = scatter(all1_ref, all2_ref, put1_ref, put2_ref).astype(BF16)


def gather_kernel(scenes, start, parts, *refs):
    first = pl.multiple_of(lax.axis_index("group") * scenes, scenes)
    field = refs[0][...].astype(F32)
    for ref in refs[1:parts]:
        field = field + ref[...].astype(F32)
    refs = refs[parts:]
    if start:
        out_ref, packet_ref = refs
        field = -field
    else:
        res_ref, out_ref, packet_ref = refs
    out_ref[...] = field
    packet_ref[...] = jnp.zeros_like(packet_ref)
    if not start:
        res = res_ref[...]
        half = packet_ref.shape[1] // 2
        packet_ref[0:1, :half] = jnp.full((1, half), jnp.sum(res * res), F32)
        packet_ref[0:1, half:] = jnp.full((1, half), jnp.sum(res * field), F32)
    packet_ref[1:2, :] = out_ref[pl.ds(first, OCTET), :][0:1]
    packet_ref[2:3, :] = out_ref[pl.ds(pl.multiple_of(first + scenes - OCTET, OCTET), OCTET), :][OCTET - 1 :]


def outside(packet_refs, ajac_ref, ejac_ref, part_ref, slot):
    _, one, _, three = packet_refs
    ties = part_ref.shape[1] // 2
    last = ajac_ref.shape[0] - 1
    even = lax.axis_index("orbit") % 2 == 0
    after = jnp.where(even, one[1:2, :], three[1:2, :])
    ahead = jnp.where(even, three[2:3, :], one[2:3, :])
    sub = row_of((OCTET, after.shape[1]))
    both = jnp.where(sub == last % OCTET, after, jnp.where(sub == 0, ahead, 0.0))
    high = both.astype(BF16).astype(F32)
    left = jnp.concatenate([high, both - high]).astype(BF16)
    got = dot_t(left, ajac_ref[last])
    got = got[:OCTET] + got[OCTET:]
    tail = pl.ds(slot + last - last % OCTET, OCTET)
    keep = row_of((OCTET, ties)) == last % OCTET
    part_ref[tail, ties:] = part_ref[tail, ties:] + jnp.where(keep, got[:, ties:], 0.0)
    got = dot_t(left, ejac_ref[0])
    got = got[:OCTET] + got[OCTET:]
    tail = pl.ds(slot + last + 1, OCTET)
    keep = row_of((OCTET, ties)) == 0
    part_ref[tail, :ties] = part_ref[tail, :ties] + jnp.where(keep, got[:, :ties], 0.0)


def scalars(packet_refs, scal_ref, step):
    mine, one, two, three = (ref[0:1, :] for ref in packet_refs)
    sums = (mine + one) + (two + three)
    half = sums.shape[1] // 2
    now, along = sums[:, :half], sums[:, half:]
    if step == 0:
        beta = jnp.zeros_like(now)
        alpha = now / along
    else:
        before, last = scal_ref[0:1, :], scal_ref[1:2, :]
        beta = now / before
        alpha = now / (along - beta * now / last)
    return now, alpha, beta


def wide(x):
    return jnp.concatenate([x, x], axis=1)


def step_kernel(step, scenes, *refs):
    refs = list(refs)
    take = lambda n: [refs.pop(0) for _ in range(n)]
    (part_ref,) = take(1)
    packet_refs = take(4)
    coef_ref, put1_ref, put2_ref, damp_ref, cjac_ref, ajac_ref, ejac_ref = take(7)
    (res_ref,) = take(1)
    if step >= 1:
        field_ref, obs_ref, x_ref = take(3)
    if step >= 2:
        image_ref, shadow_ref, dir_ref, scal_ref = take(4)
    (sent_ref, out_obs_ref) = take(2)
    if step >= 1:
        out_res_ref, out_image_ref, out_shadow_ref, out_dir_ref, out_x_ref, out_scal_ref = take(6)
    part_scr, q1_ref, q2_ref, t1_ref, t2_ref, c_ref = take(6)
    ties = q1_ref.shape[1]
    first = pl.multiple_of(lax.axis_index("group") * scenes, scenes)
    own = pl.ds(first, scenes)

    part_scr[...] = part_ref[...]
    outside(packet_refs, ajac_ref, ejac_ref, part_scr, cjac_ref.shape[0])
    if step == 0:
        out_obs_ref[...] = part_scr[...]
        now_res_ref = res_ref
    else:
        now, alpha, beta = scalars(packet_refs, None if step == 1 else scal_ref, step - 1)
        out_scal_ref[...] = jnp.zeros_like(out_scal_ref)
        out_scal_ref[0:1, :] = now
        out_scal_ref[1:2, :] = alpha
        alpha, beta = wide(alpha), wide(beta)
        image, shadow, direction = field_ref[...], part_scr[...], res_ref[own]
        if step >= 2:
            image = image + beta * image_ref[...]
            shadow = shadow + beta * shadow_ref[...]
            direction = direction + beta * dir_ref[...]
            out_x_ref[...] = x_ref[...] + alpha * direction
        else:
            out_x_ref[...] = alpha * direction
        out_image_ref[...] = image
        out_shadow_ref[...] = shadow
        out_dir_ref[...] = direction
        out_res_ref[...] = res_ref[...] - alpha * image
        out_obs_ref[...] = obs_ref[...] - alpha * shadow
        now_res_ref = out_res_ref
    r1, r2 = out_obs_ref[:, :ties], out_obs_ref[:, ties:]
    q1_ref[...], q2_ref[...] = settled(coef_ref[0], coef_ref[1], coef_ref[2], r1, r2)
    c_ref[...] = backward(q1_ref, q2_ref, put1_ref, put2_ref, cjac_ref, ajac_ref, ejac_ref, t1_ref, t2_ref)
    c_ref[own] = c_ref[own] + damp_ref[...] * now_res_ref[own]
    sent_ref[...] = c_ref[...].astype(BF16)


def final_kernel(step, scenes, *refs):
    field_ref, m, a, b, c, res_ref, image_ref, dir_ref, x_ref, scal_ref, out_x_ref, out_res_ref = refs
    own = pl.ds(pl.multiple_of(lax.axis_index("group") * scenes, scenes), scenes)
    now, alpha, beta = scalars((m, a, b, c), scal_ref, step)
    alpha, beta = wide(alpha), wide(beta)
    res = res_ref[own]
    out_x_ref[...] = x_ref[...] + alpha * (res + beta * dir_ref[...])
    out_res_ref[...] = res - alpha * (field_ref[own] + beta * image_ref[own])


def call(kernel, outs, scratch, name, args, flops=0, spaces={}, limit=None):
    args = [
        pltpu.with_memory_space_constraint(a, pltpu.HBM) if spaces.get(i) == pltpu.HBM else a
        for i, a in enumerate(args)
    ]
    at = lambda i: pl.BlockSpec(memory_space=spaces.get(i, pltpu.VMEM))
    moved = sum(a.size * a.dtype.itemsize for a in args)
    return pl.pallas_call(
        kernel,
        out_shape=[jax.ShapeDtypeStruct(*o) for o in outs],
        in_specs=[at(i) for i in range(len(args))],
        out_specs=[pl.BlockSpec(memory_space=pltpu.VMEM)] * len(outs),
        scratch_shapes=[pltpu.VMEM(*s) if isinstance(s, tuple) else s for s in scratch],
        cost_estimate=pl.CostEstimate(flops=flops, bytes_accessed=moved, transcendentals=0),
        compiler_params=pltpu.CompilerParams(vmem_limit_bytes=limit or VMEM_LIMIT),
        name=name,
    )(*args)


VMEM_LIMIT = 16 << 20


def group_sum_but_last(sent, first=(), between=None):
    size = lax.axis_size("group")
    stride, pairs = 1, None
    while stride < size:
        masks = (1, 2, 3) if 4 * stride <= size else (1,)
        got = [swap(sent, "group", mask * stride) for mask in masks]
        stride *= len(masks) + 1
        pairs = [sent] + got
        if stride < size or len(pairs) > 2:
            low = [p.astype(F32) for p in pairs]
            total = low[0] + low[1]
            if len(low) > 2:
                total = total + (low[2] + low[3])
            if stride < size:
                sent, first = lax.optimization_barrier((total.astype(BF16), first))
                if between is not None:
                    between(sent, first)
                    first, between = (), None
            else:
                pairs = [total]
    return pairs


def swap(block, axis, mask):
    return lax.ppermute(block, axis, [(i, i ^ mask) for i in range(lax.axis_size(axis))])


def orbit_packets(packet):
    n = lax.axis_size("orbit")
    return [packet] + [lax.ppermute(packet, "orbit", [(i, i ^ mask) for i in range(n)]) for mask in range(1, n)]


def on_device(
    along_jac,
    along_res,
    along_e,
    along_count,
    damping,
    cross_jac,
    cross_res,
    cross_e,
    cross_own,
    cross_group,
    cross_other,
):
    scenes, _, ties, width = along_jac.shape[1:]
    links = cross_jac.shape[1]
    groups = lax.axis_size("group")
    rows = groups * scenes
    ajac = along_jac[0].reshape(scenes, 2 * ties, width)
    cjac = cross_jac[0].reshape(links, 2 * ties, width)
    slots = links + scenes + OCTET

    def pass_on(block):
        n = lax.axis_size("orbit")
        return lax.ppermute(block, "orbit", [(i, (i + 1) % n) for i in range(n)])

    work = 2 * (links + scenes + 1) * 32 * 2 * ties * width
    tie = (slots, ties)
    pair = (slots, 2 * ties)
    full = (rows, width)
    own = (scenes, width)
    lanes = -(-slots // 128) * 128
    term_space = [((slots, width), F32)] * 2
    sems = pltpu.SemaphoreType.DMA
    pack_args = (ajac, along_e[0], along_res[0], along_count)
    edge = call(
        pack_kernel,
        [((1, 2 * ties + 2 * OCTET, width), BF16)],
        [((2, 2, ties), F32), pltpu.SMEM((1, scenes), jnp.int32), ((2 * OCTET, width), F32), sems((4,))],
        "pack",
        pack_args,
        spaces={i: pltpu.HBM for i in range(4)},
    )
    edge = pass_on(edge[0])
    blocks = links + scenes
    part_tie = (blocks, ties)
    put = ((rows, slots), BF16)
    pick = ((slots, rows), BF16)
    cjac, ajac, coef, put1, put2, pick1, pick2, t1, t2, damp = call(
        setup_kernel,
        [
            (cjac.shape, BF16),
            (ajac.shape, BF16),
            ((3,) + part_tie, F32),
            put,
            put,
            pick,
            pick,
            ((blocks, width), F32),
            ((blocks, width), F32),
            (own, F32),
        ],
        [(part_tie, F32)] * 3
        + [((OCTET, lanes), jnp.int32), sems((blocks // OCTET,))]
        + [((links, 2, ties), F32)] * 2
        + [((scenes, 2, ties), F32)] * 2
        + [pltpu.SMEM((1, scenes), jnp.int32)]
        + [((1, links), jnp.int32)] * 3
        + [pltpu.SMEM((1, scenes), F32), sems((9,))],
        "setup",
        (cjac, ajac, cross_e[0], cross_res[0], along_e[0], along_res[0], along_count)
        + (cross_own, cross_group[:, :, 0], cross_other, damping),
        work,
        {i: pltpu.HBM for i in range(11)},
    )

    def turn(start, count, refs, after):
        outs = [((min(count, j.shape[0]),) + j.shape[1:], BF16) for j in refs]
        share = work * sum(o[0][0] for o in outs) // blocks
        return call(functools.partial(turn_kernel, start), outs, [], "turn", (after,) + refs, share)

    def project(field, turned, refs):
        scratch = [((2, slots, width), F32)] * 2
        kernel = functools.partial(project_kernel, turned)
        return call(kernel, [(pair, F32)], scratch, "project", (field, pick1, pick2) + tuple(refs), work)[0]

    def finish(sums, res=None):
        args = sums if res is None else sums + [res]
        kernel = functools.partial(gather_kernel, scenes, res is None, len(sums))
        field, packet = call(kernel, [(full, F32), ((OCTET, width), F32)], [], "finish", args)
        return field, orbit_packets(packet)

    sent, coef, ejac = call(
        rhs_kernel,
        [(full, BF16), ((3,) + tie, F32), ((1, 2 * ties, width), BF16)],
        term_space,
        "rhs",
        (coef, t1, t2, edge, put1, put2),
        work // blocks,
    )
    jacs = (cjac, ajac, ejac)
    half = links // 2
    turned = []

    def more(after, done):
        turned.extend([*done, *turn(half, links - half, (cjac,), after)])

    sums = group_sum_but_last(sent, turn(0, half, (cjac,), sent), more)
    res, packets = finish(sums)
    part = project(res, (True, True, False, False), turned + [ajac, ejac])
    fixed = (coef, put1, put2, damp) + jacs
    scratch = [(pair, F32), (tie, F32), (tie, F32)] + term_space + [(full, F32)]
    sent, obs = call(
        functools.partial(step_kernel, 0, scenes),
        [(full, BF16), (pair, F32)],
        scratch,
        "step",
        (part, *packets) + fixed + (res,),
        work,
    )
    turned += turn(0, scenes, (ajac, ejac), sent)
    state = ()
    x = jnp.zeros(own, F32)
    for step in range(1, ITERS):
        field, packets = finish(group_sum_but_last(sent), res)
        part = project(field, (True,) * 4, turned)
        sent, obs, res, image, shadow, direction, x, scal = call(
            functools.partial(step_kernel, step, scenes),
            [(full, BF16), (pair, F32), (full, F32), (full, F32), (pair, F32), (own, F32), (own, F32), ((OCTET, width // 2), F32)],
            scratch,
            "step",
            (part, *packets) + fixed + (res, field, obs, x) + state,
            work,
        )
        state = (image, shadow, direction, scal)
    field, packets = finish(group_sum_but_last(sent), res)
    x, res = call(
        functools.partial(final_kernel, ITERS - 1, scenes),
        [(own, F32), (own, F32)],
        [],
        "final",
        (field, *packets, res, image, direction, x, scal),
    )
    return x[None], res[None]


def solution(mesh):
    placed = (
        P("group", "orbit", None, None, None),
        P("group", "orbit", None, None),
        P("group", "orbit", None, None),
        P("group", "orbit"),
        P("group", "orbit"),
        P("group", "orbit", None, None, None),
        P("group", "orbit", None, None),
        P("group", "orbit", None, None),
        P("group", "orbit"),
        P("group", "orbit", None),
        P("group", "orbit"),
    )
    return jax.shard_map(
        on_device,
        mesh=mesh,
        in_specs=placed,
        out_specs=(P("group", "orbit", None), P("group", "orbit", None)),
        check_vma=False,
    )
```

```python
import functools

import jax
import jax.numpy as jnp
from jax import lax
from jax.experimental import pallas as pl
from jax.experimental.pallas import tpu as pltpu
from jax.sharding import PartitionSpec as P

ITERS = 4
F32, BF16 = jnp.float32, jnp.bfloat16
OCTET = 8


def dot(a, b):
    return lax.dot_general(a, b, (((1,), (0,)), ((), ())), preferred_element_type=F32)


def dot_t(a, b):
    return lax.dot_general(a, b, (((1,), (1,)), ((), ())), preferred_element_type=F32)


def halves(x):
    high = x.astype(BF16)
    return high, (x - high.astype(F32)).astype(BF16)


def row_of(shape):
    return lax.broadcasted_iota(jnp.int32, shape, 0)


def octets(refs, body):
    slot = 0
    for number, ref in enumerate(refs):
        blocks = ref.shape[0]
        for at in range(0, blocks, OCTET):
            body(number, ref, at, slot + at, min(OCTET, blocks - at))
        slot += padded(blocks)


def padded(blocks):
    return -(-blocks // OCTET) * OCTET


def project_kernel(turned, starts, field_ref, pick1_ref, pick2_ref, *refs):
    *jac_refs, out_ref, l1_ref, l2_ref = refs
    product = [dot if is_turned else dot_t for is_turned in turned]
    ties = out_ref.shape[1] // 2
    high, low = halves(field_ref[...])
    to = 0
    for ref, start in zip(jac_refs, starts):
        count = padded(ref.shape[0])
        for pick_ref, left_ref in ((pick1_ref, l1_ref), (pick2_ref, l2_ref)):
            pick = pick_ref[start : start + count]
            left_ref[0, to : to + count] = dot(pick, high)
            left_ref[1, to : to + count] = dot(pick, low)
        to += count

    def body(number, ref, at, slot, count):
        rows = pl.ds(slot, OCTET)
        left = jnp.concatenate([l1_ref[0, rows], l2_ref[0, rows], l1_ref[1, rows], l2_ref[1, rows]])
        left = left.astype(BF16)
        total = jnp.zeros((OCTET, 2 * ties), F32)
        for j in range(count):
            got = product[number](left, ref[at + j])
            one = got[0:8, :ties] + got[16:24, :ties]
            two = got[8:16, ties:] + got[24:32, ties:]
            got = jnp.concatenate([one, two], axis=1)
            total = jnp.where(row_of(total.shape) == j, got, total)
        out_ref[rows] = total

    octets(jac_refs, body)


def turn_kernel(start, after_ref, *refs):
    half = len(refs) // 2
    for ref, out_ref in zip(refs[:half], refs[half:]):

        @pl.loop(0, out_ref.shape[0])
        def _(i, ref=ref, out_ref=out_ref):
            out_ref[i] = ref[start + i].T


def terms(q1, q2, ref, at, count):
    zero = jnp.zeros_like(q1)
    total = jnp.zeros((2 * OCTET, ref.shape[2]), F32)
    for j in range(count):
        chosen = row_of(q1.shape) == j
        top = jnp.concatenate([jnp.where(chosen, q1, 0.0), zero], axis=1)
        low = jnp.concatenate([zero, jnp.where(chosen, q2, 0.0)], axis=1)
        total = total + dot(jnp.concatenate([top, low]).astype(BF16), ref[at + j])
    return total[:OCTET], total[OCTET:]


def scatter(t1_ref, t2_ref, put1_ref, put2_ref):
    out = None
    for t_ref, put_ref in ((t1_ref, put1_ref), (t2_ref, put2_ref)):
        for part in halves(t_ref[...]):
            term = dot(put_ref[...], part)
            out = term if out is None else out + term
    return out


def backward(q1_ref, q2_ref, put1_ref, put2_ref, cjac_ref, ajac_ref, ejac_ref, t1_ref, t2_ref):
    def body(number, ref, at, slot, count):
        rows = pl.ds(slot, OCTET)
        t1_ref[rows], t2_ref[rows] = terms(q1_ref[rows], q2_ref[rows], ref, at, count)

    octets((cjac_ref, ajac_ref, ejac_ref), body)
    return scatter(t1_ref, t2_ref, put1_ref, put2_ref)


def elimination(e1, e2, live):
    over = live / (1.0 + e1 * e1 + e2 * e2)
    return (1.0 + e2 * e2) * over, e1 * e2 * over, (1.0 + e1 * e1) * over


def settled(c11, c12, c22, r1, r2):
    return c11 * r1 - c12 * r2, c22 * r2 - c12 * r1


def live_rows(count_ref, out_ref):
    lane = lax.broadcasted_iota(jnp.int32, (1, out_ref.shape[1]), 1)
    for i in range(out_ref.shape[0]):
        out_ref[i : i + 1, :] = jnp.where(lane < count_ref[0, i], 1.0, 0.0)


def fetch(pairs, sems):
    copies = [pltpu.make_async_copy(a, b, sems.at[i]) for i, (a, b) in enumerate(pairs)]
    for copy in copies:
        copy.start()
    return copies


def pack_kernel(jac_ref, e_ref, res_ref, count_ref, out_ref, pair_ref, tally_ref, wide_ref, sems):
    last = jac_ref.shape[0] - 1
    block = pl.ds(last, 1)
    height = jac_ref.shape[1]
    copies = fetch(
        [
            (jac_ref.at[block], out_ref.at[:, :height]),
            (e_ref.at[block], pair_ref.at[0:1]),
            (res_ref.at[block], pair_ref.at[1:2]),
            (count_ref, tally_ref),
        ],
        sems,
    )
    for copy in copies[1:]:
        copy.wait()
    ties = pair_ref.shape[2]
    lane = lax.broadcasted_iota(jnp.int32, (1, ties), 1)
    wide_ref[...] = jnp.zeros_like(wide_ref)
    for i in range(2):
        rest = pair_ref[i]
        for j in range(3):
            part = rest.astype(BF16).astype(F32)
            rest = rest - part
            wide_ref[4 * j + 2 * i : 4 * j + 2 * i + 2, :ties] = part
    wide_ref[12:13, :ties] = jnp.where(lane < tally_ref[0, last], 1.0, 0.0)
    out_ref[0, height:] = wide_ref[...].astype(BF16)
    copies[0].wait()


def setup_kernel(cjac_ref, ajac_ref, *refs):
    far_refs, refs = refs[:9], refs[9:]
    (out_cjac_ref, out_ajac_ref, coef_ref, put1_ref, put2_ref, pick1_ref, pick2_ref, t1_ref, t2_ref, damp_ref) = refs[:10]
    live_ref, q1_ref, q2_ref, index_ref, sems = refs[10:15]
    near_refs, near_sems = refs[15:24], refs[24]
    near = fetch(list(zip(far_refs, near_refs)), near_sems)
    ce_ref, cres_ref, ae_ref, ares_ref, count_ref, own_ref, group_ref, other_ref, scale_ref = near_refs
    copies = []
    for ref, out_ref in ((cjac_ref, out_cjac_ref), (ajac_ref, out_ajac_ref)):
        for at in range(0, ref.shape[0], OCTET):
            part = pl.ds(at, OCTET)
            copies.append(pltpu.make_async_copy(ref.at[part], out_ref.at[part], sems.at[len(copies)]))
    for copy in copies[:2]:
        copy.start()
    links, scenes = cjac_ref.shape[0], ajac_ref.shape[0]
    blocks = links + scenes
    for copy in near:
        copy.wait()
    for copy in copies[2:]:
        copy.start()
    live_ref[0:links] = jnp.ones((links, live_ref.shape[1]), F32)
    live_rows(count_ref, live_ref.at[links:blocks])
    for i in range(scenes):
        damp_ref[i : i + 1, :] = jnp.full((1, damp_ref.shape[1]), scale_ref[0, i], F32)
    for rows, e_ref, res_ref in ((slice(0, links), ce_ref, cres_ref), (slice(links, blocks), ae_ref, ares_ref)):
        c = elimination(e_ref[:, 0, :], e_ref[:, 1, :], live_ref[rows])
        for i in range(3):
            coef_ref[i, rows] = c[i]
        q1_ref[rows], q2_ref[rows] = settled(*c, res_ref[:, 0, :], res_ref[:, 1, :])

    first = lax.axis_index("group") * scenes
    slots = put1_ref.shape[1]
    index_ref[...] = jnp.zeros_like(index_ref)
    index_ref[0:1, :links] = own_ref[...] + first
    index_ref[1:2, :links] = group_ref[...] * scenes + other_ref[...]
    lane = lax.broadcasted_iota(jnp.int32, (1, index_ref.shape[1]), 1)
    one = jnp.where(lane < links, index_ref[0:1, :], jnp.where(lane < blocks, first + lane - links, -1))
    two = jnp.where(lane < blocks - 1, first + lane - links + 1, jnp.where(lane == blocks, first, -1))
    two = jnp.where(lane < links, index_ref[1:2, :], two)
    for index, put_ref, pick_ref in ((one, put1_ref, pick1_ref), (two, put2_ref, pick2_ref)):
        shape = (put_ref.shape[0], index.shape[1])
        table = jnp.where(row_of(shape) == index, 1.0, 0.0)
        put_ref[...] = table[:, :slots].astype(BF16)
        pick_ref[...] = table.T[:slots].astype(BF16)

    octet = 0
    for ref in (out_cjac_ref, out_ajac_ref):
        for at in range(0, ref.shape[0], OCTET):
            copies[octet].wait()
            rows = pl.ds(octet * OCTET, OCTET)
            t1_ref[rows], t2_ref[rows] = terms(q1_ref[rows], q2_ref[rows], ref, at, OCTET)
            octet += 1


def rhs_kernel(coef_ref, t1_ref, t2_ref, edge_ref, put1_ref, put2_ref, out_ref, out_coef_ref, ejac_ref, all1_ref, all2_ref):
    blocks, ties = t1_ref.shape[0], coef_ref.shape[2]
    height = ejac_ref.shape[1]
    rows = pl.ds(blocks, OCTET)
    ejac_ref[...] = edge_ref[:, :height]
    parts = edge_ref[0, height:, :ties].astype(F32)
    e1, e2, r1, r2 = (parts[i : i + 1] + parts[i + 4 : i + 5] + parts[i + 8 : i + 9] for i in range(4))
    c = elimination(e1, e2, parts[12:13])
    fill = lambda x: jnp.where(row_of((OCTET, x.shape[1])) == 0, x, 0.0)
    for i in range(3):
        out_coef_ref[i, :blocks] = coef_ref[i]
        out_coef_ref[i, rows] = fill(c[i])
    q1, q2 = settled(*c, r1, r2)
    all1_ref[:blocks] = t1_ref[...]
    all2_ref[:blocks] = t2_ref[...]
    all1_ref[rows], all2_ref[rows] = terms(fill(q1), fill(q2), ejac_ref, 0, 1)
    out_ref[...] = scatter(all1_ref, all2_ref, put1_ref, put2_ref).astype(BF16)


def gather_kernel(scenes, start, parts, *refs):
    first = pl.multiple_of(lax.axis_index("group") * scenes, scenes)
    field = refs[0][...].astype(F32)
    for ref in refs[1:parts]:
        field = field + ref[...].astype(F32)
    refs = refs[parts:]
    if start:
        out_ref, packet_ref = refs
        field = -field
    else:
        res_ref, out_ref, packet_ref = refs
    out_ref[...] = field
    packet_ref[...] = jnp.zeros_like(packet_ref)
    if not start:
        res = res_ref[...]
        half = packet_ref.shape[1] // 2
        packet_ref[0:1, :half] = jnp.full((1, half), jnp.sum(res * res), F32)
        packet_ref[0:1, half:] = jnp.full((1, half), jnp.sum(res * field), F32)
    packet_ref[1:2, :] = out_ref[pl.ds(first, OCTET), :][0:1]
    packet_ref[2:3, :] = out_ref[pl.ds(pl.multiple_of(first + scenes - OCTET, OCTET), OCTET), :][OCTET - 1 :]


def outside(packet_refs, ajac_ref, ejac_ref, part_ref, slot):
    _, one, _, three = packet_refs
    ties = part_ref.shape[1] // 2
    last = ajac_ref.shape[0] - 1
    even = lax.axis_index("orbit") % 2 == 0
    after = jnp.where(even, one[1:2, :], three[1:2, :])
    ahead = jnp.where(even, three[2:3, :], one[2:3, :])
    sub = row_of((OCTET, after.shape[1]))
    both = jnp.where(sub == last % OCTET, after, jnp.where(sub == 0, ahead, 0.0))
    high = both.astype(BF16).astype(F32)
    left = jnp.concatenate([high, both - high]).astype(BF16)
    got = dot_t(left, ajac_ref[last])
    got = got[:OCTET] + got[OCTET:]
    tail = pl.ds(slot + last - last % OCTET, OCTET)
    keep = row_of((OCTET, ties)) == last % OCTET
    part_ref[tail, ties:] = part_ref[tail, ties:] + jnp.where(keep, got[:, ties:], 0.0)
    got = dot_t(left, ejac_ref[0])
    got = got[:OCTET] + got[OCTET:]
    tail = pl.ds(slot + last + 1, OCTET)
    keep = row_of((OCTET, ties)) == 0
    part_ref[tail, :ties] = part_ref[tail, :ties] + jnp.where(keep, got[:, :ties], 0.0)


def scalars(packet_refs, scal_ref, step):
    mine, one, two, three = (ref[0:1, :] for ref in packet_refs)
    sums = (mine + one) + (two + three)
    half = sums.shape[1] // 2
    now, along = sums[:, :half], sums[:, half:]
    if step == 0:
        beta = jnp.zeros_like(now)
        alpha = now / along
    else:
        before, last = scal_ref[0:1, :], scal_ref[1:2, :]
        beta = now / before
        alpha = now / (along - beta * now / last)
    return now, alpha, beta


def wide(x):
    return jnp.concatenate([x, x], axis=1)


def step_kernel(step, scenes, places, *refs):
    refs = list(refs)
    take = lambda n: [refs.pop(0) for _ in range(n)]
    part_refs = take(2)
    packet_refs = take(4)
    coef_ref, put1_ref, put2_ref, damp_ref, cjac_ref, ajac_ref, ejac_ref = take(7)
    (res_ref,) = take(1)
    if step >= 1:
        field_ref, obs_ref, x_ref = take(3)
    if step >= 2:
        image_ref, shadow_ref, dir_ref, scal_ref = take(4)
    (sent_ref, out_obs_ref) = take(2)
    if step >= 1:
        out_res_ref, out_image_ref, out_shadow_ref, out_dir_ref, out_x_ref, out_scal_ref = take(6)
    part_scr, q1_ref, q2_ref, t1_ref, t2_ref, c_ref = take(6)
    ties = q1_ref.shape[1]
    first = pl.multiple_of(lax.axis_index("group") * scenes, scenes)
    own = pl.ds(first, scenes)

    for part_ref, pieces in zip(part_refs, places):
        at = 0
        for start, count in pieces:
            part_scr[start : start + count] = part_ref[at : at + count]
            at += count
    outside(packet_refs, ajac_ref, ejac_ref, part_scr, cjac_ref.shape[0])
    if step == 0:
        out_obs_ref[...] = part_scr[...]
        now_res_ref = res_ref
    else:
        now, alpha, beta = scalars(packet_refs, None if step == 1 else scal_ref, step - 1)
        out_scal_ref[...] = jnp.zeros_like(out_scal_ref)
        out_scal_ref[0:1, :] = now
        out_scal_ref[1:2, :] = alpha
        alpha, beta = wide(alpha), wide(beta)
        image, shadow, direction = field_ref[...], part_scr[...], res_ref[own]
        if step >= 2:
            image = image + beta * image_ref[...]
            shadow = shadow + beta * shadow_ref[...]
            direction = direction + beta * dir_ref[...]
            out_x_ref[...] = x_ref[...] + alpha * direction
        else:
            out_x_ref[...] = alpha * direction
        out_image_ref[...] = image
        out_shadow_ref[...] = shadow
        out_dir_ref[...] = direction
        out_res_ref[...] = res_ref[...] - alpha * image
        out_obs_ref[...] = obs_ref[...] - alpha * shadow
        now_res_ref = out_res_ref
    r1, r2 = out_obs_ref[:, :ties], out_obs_ref[:, ties:]
    q1_ref[...], q2_ref[...] = settled(coef_ref[0], coef_ref[1], coef_ref[2], r1, r2)
    c_ref[...] = backward(q1_ref, q2_ref, put1_ref, put2_ref, cjac_ref, ajac_ref, ejac_ref, t1_ref, t2_ref)
    c_ref[own] = c_ref[own] + damp_ref[...] * now_res_ref[own]
    sent_ref[...] = c_ref[...].astype(BF16)


def final_kernel(step, scenes, *refs):
    field_ref, m, a, b, c, res_ref, image_ref, dir_ref, x_ref, scal_ref, out_x_ref, out_res_ref = refs
    own = pl.ds(pl.multiple_of(lax.axis_index("group") * scenes, scenes), scenes)
    now, alpha, beta = scalars((m, a, b, c), scal_ref, step)
    alpha, beta = wide(alpha), wide(beta)
    res = res_ref[own]
    out_x_ref[...] = x_ref[...] + alpha * (res + beta * dir_ref[...])
    out_res_ref[...] = res - alpha * (field_ref[own] + beta * image_ref[own])


def call(kernel, outs, scratch, name, args, flops=0, spaces={}, limit=None):
    args = [
        pltpu.with_memory_space_constraint(a, pltpu.HBM) if spaces.get(i) == pltpu.HBM else a
        for i, a in enumerate(args)
    ]
    at = lambda i: pl.BlockSpec(memory_space=spaces.get(i, pltpu.VMEM))
    moved = sum(a.size * a.dtype.itemsize for a in args)
    return pl.pallas_call(
        kernel,
        out_shape=[jax.ShapeDtypeStruct(*o) for o in outs],
        in_specs=[at(i) for i in range(len(args))],
        out_specs=[pl.BlockSpec(memory_space=pltpu.VMEM)] * len(outs),
        scratch_shapes=[pltpu.VMEM(*s) if isinstance(s, tuple) else s for s in scratch],
        cost_estimate=pl.CostEstimate(flops=flops, bytes_accessed=moved, transcendentals=0),
        compiler_params=pltpu.CompilerParams(vmem_limit_bytes=limit or VMEM_LIMIT),
        name=name,
    )(*args)


VMEM_LIMIT = 16 << 20


def group_sum_but_last(sent, first=(), between=None):
    size = lax.axis_size("group")
    stride, pairs = 1, None
    while stride < size:
        masks = (1, 2, 3) if 4 * stride <= size else (1,)
        got = [swap(sent, "group", mask * stride) for mask in masks]
        stride *= len(masks) + 1
        pairs = [sent] + got
        if stride < size or len(pairs) > 2:
            low = [p.astype(F32) for p in pairs]
            total = low[0] + low[1]
            if len(low) > 2:
                total = total + (low[2] + low[3])
            if stride < size:
                sent, first = lax.optimization_barrier((total.astype(BF16), first))
                if between is not None:
                    between(sent, first)
                    first, between = (), None
            else:
                pairs = [total]
    return pairs


def swap(block, axis, mask):
    return lax.ppermute(block, axis, [(i, i ^ mask) for i in range(lax.axis_size(axis))])


def far_packets(packet):
    return swap(packet, "orbit", 1), swap(packet, "orbit", 3)


def on_device(
    along_jac,
    along_res,
    along_e,
    along_count,
    damping,
    cross_jac,
    cross_res,
    cross_e,
    cross_own,
    cross_group,
    cross_other,
):
    scenes, _, ties, width = along_jac.shape[1:]
    links = cross_jac.shape[1]
    groups = lax.axis_size("group")
    rows = groups * scenes
    ajac = along_jac[0].reshape(scenes, 2 * ties, width)
    cjac = cross_jac[0].reshape(links, 2 * ties, width)
    slots = links + scenes + OCTET

    def pass_on(block):
        n = lax.axis_size("orbit")
        return lax.ppermute(block, "orbit", [(i, (i + 1) % n) for i in range(n)])

    work = 2 * (links + scenes + 1) * 32 * 2 * ties * width
    tie = (slots, ties)
    pair = (slots, 2 * ties)
    full = (rows, width)
    own = (scenes, width)
    lanes = -(-slots // 128) * 128
    term_space = [((slots, width), F32)] * 2
    sems = pltpu.SemaphoreType.DMA
    pack_args = (ajac, along_e[0], along_res[0], along_count)
    edge = call(
        pack_kernel,
        [((1, 2 * ties + 2 * OCTET, width), BF16)],
        [((2, 2, ties), F32), pltpu.SMEM((1, scenes), jnp.int32), ((2 * OCTET, width), F32), sems((4,))],
        "pack",
        pack_args,
        spaces={i: pltpu.HBM for i in range(4)},
    )
    edge = pass_on(edge[0])
    blocks = links + scenes
    part_tie = (blocks, ties)
    put = ((rows, slots), BF16)
    pick = ((slots, rows), BF16)
    cjac, ajac, coef, put1, put2, pick1, pick2, t1, t2, damp = call(
        setup_kernel,
        [
            (cjac.shape, BF16),
            (ajac.shape, BF16),
            ((3,) + part_tie, F32),
            put,
            put,
            pick,
            pick,
            ((blocks, width), F32),
            ((blocks, width), F32),
            (own, F32),
        ],
        [(part_tie, F32)] * 3
        + [((OCTET, lanes), jnp.int32), sems((blocks // OCTET,))]
        + [((links, 2, ties), F32)] * 2
        + [((scenes, 2, ties), F32)] * 2
        + [pltpu.SMEM((1, scenes), jnp.int32)]
        + [((1, links), jnp.int32)] * 3
        + [pltpu.SMEM((1, scenes), F32), sems((9,))],
        "setup",
        (cjac, ajac, cross_e[0], cross_res[0], along_e[0], along_res[0], along_count)
        + (cross_own, cross_group[:, :, 0], cross_other, damping),
        work,
        {i: pltpu.HBM for i in range(11)},
    )

    def turn(start, count, refs, after):
        outs = [((min(count, j.shape[0]),) + j.shape[1:], BF16) for j in refs]
        share = work * sum(o[0][0] for o in outs) // blocks
        return call(functools.partial(turn_kernel, start), outs, [], "turn", (after,) + refs, share)

    half = links // 2
    places = (((0, half), (links, scenes)), ((half, links - half), (blocks, OCTET)))

    def project(field, pieces, turned, refs):
        count = sum(n for _, n in pieces)
        kernel = functools.partial(project_kernel, turned, [at for at, _ in pieces])
        return call(
            kernel,
            [((count, 2 * ties), F32)],
            [((2, count, width), F32)] * 2,
            "project",
            (field, pick1, pick2) + tuple(refs),
            work * count // blocks,
        )[0]

    def meet(field, packet, turned, refs):
        near, far = far_packets(packet)
        parts = []
        if refs is not None:
            parts.append(project(field, places[0], turned[0::2], refs[0::2]))
            far, parts[0] = lax.optimization_barrier((far, parts[0]))
        opposite = swap(far, "orbit", 1)
        if refs is not None:
            parts.append(project(field, places[1], turned[1::2], refs[1::2]))
        return parts, (packet, near, opposite, far)

    def finish(sums, res=None):
        args = sums if res is None else sums + [res]
        kernel = functools.partial(gather_kernel, scenes, res is None, len(sums))
        return call(kernel, [(full, F32), ((OCTET, width), F32)], [], "finish", args)

    sent, coef, ejac = call(
        rhs_kernel,
        [(full, BF16), ((3,) + tie, F32), ((1, 2 * ties, width), BF16)],
        term_space,
        "rhs",
        (coef, t1, t2, edge, put1, put2),
        work // blocks,
    )
    jacs = (cjac, ajac, ejac)
    turned = []

    def more(after, done):
        turned.extend([*done, *turn(half, links - half, (cjac,), after)])

    sums = group_sum_but_last(sent, turn(0, half, (cjac,), sent), more)
    res, packet = finish(sums)
    parts, packets = meet(res, packet, (True, True, False, False), turned + [ajac, ejac])
    fixed = (coef, put1, put2, damp) + jacs
    scratch = [(pair, F32), (tie, F32), (tie, F32)] + term_space + [(full, F32)]
    sent, obs = call(
        functools.partial(step_kernel, 0, scenes, places),
        [(full, BF16), (pair, F32)],
        scratch,
        "step",
        (*parts, *packets) + fixed + (res,),
        work,
    )
    turned += turn(0, scenes, (ajac, ejac), sent)
    state = ()
    x = jnp.zeros(own, F32)
    for step in range(1, ITERS):
        field, packet = finish(group_sum_but_last(sent), res)
        parts, packets = meet(field, packet, (True,) * 4, turned)
        sent, obs, res, image, shadow, direction, x, scal = call(
            functools.partial(step_kernel, step, scenes, places),
            [(full, BF16), (pair, F32), (full, F32), (full, F32), (pair, F32), (own, F32), (own, F32), ((OCTET, width // 2), F32)],
            scratch,
            "step",
            (*parts, *packets) + fixed + (res, field, obs, x) + state,
            work,
        )
        state = (image, shadow, direction, scal)
    field, packet = finish(group_sum_but_last(sent), res)
    _, packets = meet(field, packet, None, None)
    x, res = call(
        functools.partial(final_kernel, ITERS - 1, scenes),
        [(own, F32), (own, F32)],
        [],
        "final",
        (field, *packets, res, image, direction, x, scal),
    )
    return x[None], res[None]


def solution(mesh):
    placed = (
        P("group", "orbit", None, None, None),
        P("group", "orbit", None, None),
        P("group", "orbit", None, None),
        P("group", "orbit"),
        P("group", "orbit"),
        P("group", "orbit", None, None, None),
        P("group", "orbit", None, None),
        P("group", "orbit", None, None),
        P("group", "orbit"),
        P("group", "orbit", None),
        P("group", "orbit"),
    )
    return jax.shard_map(
        on_device,
        mesh=mesh,
        in_specs=placed,
        out_specs=(P("group", "orbit", None), P("group", "orbit", None)),
        check_vma=False,
    )
```

```python
import functools

import jax
import jax.numpy as jnp
from jax import lax
from jax.experimental import pallas as pl
from jax.experimental.pallas import tpu as pltpu
from jax.sharding import PartitionSpec as P

ITERS = 4
F32, BF16 = jnp.float32, jnp.bfloat16
OCTET = 8


def dot(a, b):
    return lax.dot_general(a, b, (((1,), (0,)), ((), ())), preferred_element_type=F32)


def dot_t(a, b):
    return lax.dot_general(a, b, (((1,), (1,)), ((), ())), preferred_element_type=F32)


def halves(x):
    high = x.astype(BF16)
    return high, (x - high.astype(F32)).astype(BF16)


def row_of(shape):
    return lax.broadcasted_iota(jnp.int32, shape, 0)


def octets(refs, body):
    slot = 0
    for number, ref in enumerate(refs):
        blocks = ref.shape[0]
        for at in range(0, blocks, OCTET):
            body(number, ref, at, slot + at, min(OCTET, blocks - at))
        slot += -(-blocks // OCTET) * OCTET


def project_kernel(turned, field_ref, pick1_ref, pick2_ref, *refs):
    *jac_refs, out_ref, l1_ref, l2_ref = refs
    product = [dot if is_turned else dot_t for is_turned in turned]
    ties = out_ref.shape[1] // 2
    high, low = halves(field_ref[...])
    for pick_ref, left_ref in ((pick1_ref, l1_ref), (pick2_ref, l2_ref)):
        left_ref[0] = dot(pick_ref[...], high)
        left_ref[1] = dot(pick_ref[...], low)

    def body(number, ref, at, slot, count):
        rows = pl.ds(slot, OCTET)
        left = jnp.concatenate([l1_ref[0, rows], l2_ref[0, rows], l1_ref[1, rows], l2_ref[1, rows]])
        left = left.astype(BF16)
        total = jnp.zeros((OCTET, 2 * ties), F32)
        for j in range(count):
            got = product[number](left, ref[at + j])
            one = got[0:8, :ties] + got[16:24, :ties]
            two = got[8:16, ties:] + got[24:32, ties:]
            got = jnp.concatenate([one, two], axis=1)
            total = jnp.where(row_of(total.shape) == j, got, total)
        out_ref[rows] = total

    octets(jac_refs, body)


def turn_kernel(start, after_ref, *refs):
    half = len(refs) // 2
    for ref, out_ref in zip(refs[:half], refs[half:]):

        @pl.loop(0, out_ref.shape[0])
        def _(i, ref=ref, out_ref=out_ref):
            out_ref[i] = ref[start + i].T


def terms(q1, q2, ref, at, count):
    zero = jnp.zeros_like(q1)
    total = jnp.zeros((2 * OCTET, ref.shape[2]), F32)
    for j in range(count):
        chosen = row_of(q1.shape) == j
        top = jnp.concatenate([jnp.where(chosen, q1, 0.0), zero], axis=1)
        low = jnp.concatenate([zero, jnp.where(chosen, q2, 0.0)], axis=1)
        total = total + dot(jnp.concatenate([top, low]).astype(BF16), ref[at + j])
    return total[:OCTET], total[OCTET:]


def scatter(t1_ref, t2_ref, put1_ref, put2_ref):
    out = None
    for t_ref, put_ref in ((t1_ref, put1_ref), (t2_ref, put2_ref)):
        for part in halves(t_ref[...]):
            term = dot(put_ref[...], part)
            out = term if out is None else out + term
    return out


def backward(q1_ref, q2_ref, put1_ref, put2_ref, cjac_ref, ajac_ref, ejac_ref, t1_ref, t2_ref):
    def body(number, ref, at, slot, count):
        rows = pl.ds(slot, OCTET)
        t1_ref[rows], t2_ref[rows] = terms(q1_ref[rows], q2_ref[rows], ref, at, count)

    octets((cjac_ref, ajac_ref, ejac_ref), body)
    return scatter(t1_ref, t2_ref, put1_ref, put2_ref)


def elimination(e1, e2, live):
    over = live / (1.0 + e1 * e1 + e2 * e2)
    return (1.0 + e2 * e2) * over, e1 * e2 * over, (1.0 + e1 * e1) * over


def settled(c11, c12, c22, r1, r2):
    return c11 * r1 - c12 * r2, c22 * r2 - c12 * r1


def live_rows(count_ref, out_ref):
    lane = lax.broadcasted_iota(jnp.int32, (1, out_ref.shape[1]), 1)
    for i in range(out_ref.shape[0]):
        out_ref[i : i + 1, :] = jnp.where(lane < count_ref[0, i], 1.0, 0.0)


def fetch(pairs, sems):
    copies = [pltpu.make_async_copy(a, b, sems.at[i]) for i, (a, b) in enumerate(pairs)]
    for copy in copies:
        copy.start()
    return copies


def pack_kernel(*refs):
    far_refs, count_ref, scale_ref, refs = refs[:8], refs[8], refs[9], refs[10:]
    near_refs, out_ref, live_ref, damp_ref = refs[:8], refs[8], refs[9], refs[10]
    tally_ref, factor_ref, wide_ref, sems = refs[11:]
    jac_ref, near_jac_ref, e_ref, res_ref = far_refs[0], near_refs[0], near_refs[1], near_refs[2]
    last, height, ties = jac_ref.shape[0] - 1, jac_ref.shape[1], e_ref.shape[2]
    pairs = list(zip(far_refs[1:], near_refs[1:])) + [(count_ref, tally_ref), (scale_ref, factor_ref)]
    copies = fetch(pairs + [(jac_ref.at[pl.ds(last, 1)], out_ref.at[:, :height]), (jac_ref, near_jac_ref)], sems)
    for copy in copies[: len(pairs)]:
        copy.wait()
    wide_ref[...] = jnp.zeros_like(wide_ref)
    for i, ref in enumerate((e_ref, res_ref)):
        rest = ref[last]
        for j in range(3):
            part = rest.astype(BF16).astype(F32)
            rest = rest - part
            wide_ref[4 * j + 2 * i : 4 * j + 2 * i + 2, :ties] = part
    live_rows(tally_ref, live_ref)
    wide_ref[12:13, :ties] = live_ref[last : last + 1, :]
    out_ref[0, height:] = wide_ref[...].astype(BF16)
    for i in range(damp_ref.shape[0]):
        damp_ref[i : i + 1, :] = jnp.full((1, damp_ref.shape[1]), factor_ref[0, i], F32)
    for copy in copies[len(pairs) :]:
        copy.wait()


def setup_kernel(cjac_ref, ajac_ref, *refs):
    ae_ref, ares_ref, ce_ref, cres_ref, own_ref, group_ref, other_ref, lived_ref = refs[:8]
    out_cjac_ref, coef_ref, put1_ref, put2_ref, pick1_ref, pick2_ref, t1_ref, t2_ref = refs[8:16]
    live_ref, q1_ref, q2_ref, index_ref, sems = refs[16:]
    parts = [pl.ds(at, OCTET) for at in range(0, cjac_ref.shape[0], OCTET)]
    copies = fetch([(cjac_ref.at[part], out_cjac_ref.at[part]) for part in parts], sems)
    links, scenes = cjac_ref.shape[0], ajac_ref.shape[0]
    blocks = links + scenes
    live_ref[0:links] = jnp.ones((links, live_ref.shape[1]), F32)
    live_ref[links:blocks] = lived_ref[...]
    for rows, e_ref, res_ref in ((slice(0, links), ce_ref, cres_ref), (slice(links, blocks), ae_ref, ares_ref)):
        c = elimination(e_ref[:, 0, :], e_ref[:, 1, :], live_ref[rows])
        for i in range(3):
            coef_ref[i, rows] = c[i]
        q1_ref[rows], q2_ref[rows] = settled(*c, res_ref[:, 0, :], res_ref[:, 1, :])

    first = lax.axis_index("group") * scenes
    slots = put1_ref.shape[1]
    index_ref[...] = jnp.zeros_like(index_ref)
    index_ref[0:1, :links] = own_ref[...] + first
    index_ref[1:2, :links] = group_ref[...] * scenes + other_ref[...]
    lane = lax.broadcasted_iota(jnp.int32, (1, index_ref.shape[1]), 1)
    one = jnp.where(lane < links, index_ref[0:1, :], jnp.where(lane < blocks, first + lane - links, -1))
    two = jnp.where(lane < blocks - 1, first + lane - links + 1, jnp.where(lane == blocks, first, -1))
    two = jnp.where(lane < links, index_ref[1:2, :], two)
    for index, put_ref, pick_ref in ((one, put1_ref, pick1_ref), (two, put2_ref, pick2_ref)):
        shape = (put_ref.shape[0], index.shape[1])
        table = jnp.where(row_of(shape) == index, 1.0, 0.0)
        put_ref[...] = table[:, :slots].astype(BF16)
        pick_ref[...] = table.T[:slots].astype(BF16)

    for ref, slot in ((ajac_ref, links), (out_cjac_ref, 0)):
        for at in range(0, ref.shape[0], OCTET):
            if ref is out_cjac_ref:
                copies[at // OCTET].wait()
            rows = pl.ds(slot + at, OCTET)
            t1_ref[rows], t2_ref[rows] = terms(q1_ref[rows], q2_ref[rows], ref, at, OCTET)


def rhs_kernel(coef_ref, t1_ref, t2_ref, edge_ref, put1_ref, put2_ref, out_ref, out_coef_ref, ejac_ref, all1_ref, all2_ref):
    blocks, ties = t1_ref.shape[0], coef_ref.shape[2]
    height = ejac_ref.shape[1]
    rows = pl.ds(blocks, OCTET)
    ejac_ref[...] = edge_ref[:, :height]
    parts = edge_ref[0, height:, :ties].astype(F32)
    e1, e2, r1, r2 = (parts[i : i + 1] + parts[i + 4 : i + 5] + parts[i + 8 : i + 9] for i in range(4))
    c = elimination(e1, e2, parts[12:13])
    fill = lambda x: jnp.where(row_of((OCTET, x.shape[1])) == 0, x, 0.0)
    for i in range(3):
        out_coef_ref[i, :blocks] = coef_ref[i]
        out_coef_ref[i, rows] = fill(c[i])
    q1, q2 = settled(*c, r1, r2)
    all1_ref[:blocks] = t1_ref[...]
    all2_ref[:blocks] = t2_ref[...]
    all1_ref[rows], all2_ref[rows] = terms(fill(q1), fill(q2), ejac_ref, 0, 1)
    out_ref[...] = scatter(all1_ref, all2_ref, put1_ref, put2_ref).astype(BF16)


def gather_kernel(scenes, start, parts, *refs):
    first = pl.multiple_of(lax.axis_index("group") * scenes, scenes)
    field = refs[0][...].astype(F32)
    for ref in refs[1:parts]:
        field = field + ref[...].astype(F32)
    refs = refs[parts:]
    if start:
        out_ref, packet_ref = refs
        field = -field
    else:
        res_ref, out_ref, packet_ref = refs
    out_ref[...] = field
    packet_ref[...] = jnp.zeros_like(packet_ref)
    if not start:
        res = res_ref[...]
        half = packet_ref.shape[1] // 2
        packet_ref[0:1, :half] = jnp.full((1, half), jnp.sum(res * res), F32)
        packet_ref[0:1, half:] = jnp.full((1, half), jnp.sum(res * field), F32)
    packet_ref[1:2, :] = out_ref[pl.ds(first, OCTET), :][0:1]
    packet_ref[2:3, :] = out_ref[pl.ds(pl.multiple_of(first + scenes - OCTET, OCTET), OCTET), :][OCTET - 1 :]


def outside(packet_refs, ajac_ref, ejac_ref, part_ref, slot):
    _, one, _, three = packet_refs
    ties = part_ref.shape[1] // 2
    last = ajac_ref.shape[0] - 1
    even = lax.axis_index("orbit") % 2 == 0
    after = jnp.where(even, one[1:2, :], three[1:2, :])
    ahead = jnp.where(even, three[2:3, :], one[2:3, :])
    sub = row_of((OCTET, after.shape[1]))
    both = jnp.where(sub == last % OCTET, after, jnp.where(sub == 0, ahead, 0.0))
    high = both.astype(BF16).astype(F32)
    left = jnp.concatenate([high, both - high]).astype(BF16)
    got = dot_t(left, ajac_ref[last])
    got = got[:OCTET] + got[OCTET:]
    tail = pl.ds(slot + last - last % OCTET, OCTET)
    keep = row_of((OCTET, ties)) == last % OCTET
    part_ref[tail, ties:] = part_ref[tail, ties:] + jnp.where(keep, got[:, ties:], 0.0)
    got = dot_t(left, ejac_ref[0])
    got = got[:OCTET] + got[OCTET:]
    tail = pl.ds(slot + last + 1, OCTET)
    keep = row_of((OCTET, ties)) == 0
    part_ref[tail, :ties] = part_ref[tail, :ties] + jnp.where(keep, got[:, :ties], 0.0)


def scalars(packet_refs, scal_ref, step):
    mine, one, two, three = (ref[0:1, :] for ref in packet_refs)
    sums = (mine + one) + (two + three)
    half = sums.shape[1] // 2
    now, along = sums[:, :half], sums[:, half:]
    if step == 0:
        beta = jnp.zeros_like(now)
        alpha = now / along
    else:
        before, last = scal_ref[0:1, :], scal_ref[1:2, :]
        beta = now / before
        alpha = now / (along - beta * now / last)
    return now, alpha, beta


def wide(x):
    return jnp.concatenate([x, x], axis=1)


def step_kernel(step, scenes, *refs):
    refs = list(refs)
    take = lambda n: [refs.pop(0) for _ in range(n)]
    (part_ref,) = take(1)
    packet_refs = take(4)
    coef_ref, put1_ref, put2_ref, damp_ref, cjac_ref, ajac_ref, ejac_ref = take(7)
    (res_ref,) = take(1)
    if step >= 1:
        field_ref, obs_ref, x_ref = take(3)
    if step >= 2:
        image_ref, shadow_ref, dir_ref, scal_ref = take(4)
    (sent_ref, out_obs_ref) = take(2)
    if step >= 1:
        out_res_ref, out_image_ref, out_shadow_ref, out_dir_ref, out_x_ref, out_scal_ref = take(6)
    part_scr, q1_ref, q2_ref, t1_ref, t2_ref, c_ref = take(6)
    ties = q1_ref.shape[1]
    first = pl.multiple_of(lax.axis_index("group") * scenes, scenes)
    own = pl.ds(first, scenes)

    part_scr[...] = part_ref[...]
    outside(packet_refs, ajac_ref, ejac_ref, part_scr, cjac_ref.shape[0])
    if step == 0:
        out_obs_ref[...] = part_scr[...]
        now_res_ref = res_ref
    else:
        now, alpha, beta = scalars(packet_refs, None if step == 1 else scal_ref, step - 1)
        out_scal_ref[...] = jnp.zeros_like(out_scal_ref)
        out_scal_ref[0:1, :] = now
        out_scal_ref[1:2, :] = alpha
        alpha, beta = wide(alpha), wide(beta)
        image, shadow, direction = field_ref[...], part_scr[...], res_ref[own]
        if step >= 2:
            image = image + beta * image_ref[...]
            shadow = shadow + beta * shadow_ref[...]
            direction = direction + beta * dir_ref[...]
            out_x_ref[...] = x_ref[...] + alpha * direction
        else:
            out_x_ref[...] = alpha * direction
        out_image_ref[...] = image
        out_shadow_ref[...] = shadow
        out_dir_ref[...] = direction
        out_res_ref[...] = res_ref[...] - alpha * image
        out_obs_ref[...] = obs_ref[...] - alpha * shadow
        now_res_ref = out_res_ref
    r1, r2 = out_obs_ref[:, :ties], out_obs_ref[:, ties:]
    q1_ref[...], q2_ref[...] = settled(coef_ref[0], coef_ref[1], coef_ref[2], r1, r2)
    c_ref[...] = backward(q1_ref, q2_ref, put1_ref, put2_ref, cjac_ref, ajac_ref, ejac_ref, t1_ref, t2_ref)
    c_ref[own] = c_ref[own] + damp_ref[...] * now_res_ref[own]
    sent_ref[...] = c_ref[...].astype(BF16)


def final_kernel(step, scenes, *refs):
    field_ref, m, a, b, c, res_ref, image_ref, dir_ref, x_ref, scal_ref, out_x_ref, out_res_ref = refs
    own = pl.ds(pl.multiple_of(lax.axis_index("group") * scenes, scenes), scenes)
    now, alpha, beta = scalars((m, a, b, c), scal_ref, step)
    alpha, beta = wide(alpha), wide(beta)
    res = res_ref[own]
    out_x_ref[...] = x_ref[...] + alpha * (res + beta * dir_ref[...])
    out_res_ref[...] = res - alpha * (field_ref[own] + beta * image_ref[own])


def call(kernel, outs, scratch, name, args, flops=0, spaces={}, limit=None):
    args = [
        pltpu.with_memory_space_constraint(a, pltpu.HBM) if spaces.get(i) == pltpu.HBM else a
        for i, a in enumerate(args)
    ]
    at = lambda i: pl.BlockSpec(memory_space=spaces.get(i, pltpu.VMEM))
    moved = sum(a.size * a.dtype.itemsize for a in args)
    return pl.pallas_call(
        kernel,
        out_shape=[jax.ShapeDtypeStruct(*o) for o in outs],
        in_specs=[at(i) for i in range(len(args))],
        out_specs=[pl.BlockSpec(memory_space=pltpu.VMEM)] * len(outs),
        scratch_shapes=[pltpu.VMEM(*s) if isinstance(s, tuple) else s for s in scratch],
        cost_estimate=pl.CostEstimate(flops=flops, bytes_accessed=moved, transcendentals=0),
        compiler_params=pltpu.CompilerParams(vmem_limit_bytes=limit or VMEM_LIMIT),
        name=name,
    )(*args)


VMEM_LIMIT = 16 << 20


def group_sum_but_last(sent, first=(), between=None):
    size = lax.axis_size("group")
    stride, pairs = 1, None
    while stride < size:
        masks = (1, 2, 3) if 4 * stride <= size else (1,)
        got = [swap(sent, "group", mask * stride) for mask in masks]
        stride *= len(masks) + 1
        pairs = [sent] + got
        if stride < size or len(pairs) > 2:
            low = [p.astype(F32) for p in pairs]
            total = low[0] + low[1]
            if len(low) > 2:
                total = total + (low[2] + low[3])
            if stride < size:
                sent, first = lax.optimization_barrier((total.astype(BF16), first))
                if between is not None:
                    between(sent, first)
                    first, between = (), None
            else:
                pairs = [total]
    return pairs


def swap(block, axis, mask):
    return lax.ppermute(block, axis, [(i, i ^ mask) for i in range(lax.axis_size(axis))])


def orbit_packets(packet):
    n = lax.axis_size("orbit")
    return [packet] + [lax.ppermute(packet, "orbit", [(i, i ^ mask) for i in range(n)]) for mask in range(1, n)]


def on_device(
    along_jac,
    along_res,
    along_e,
    along_count,
    damping,
    cross_jac,
    cross_res,
    cross_e,
    cross_own,
    cross_group,
    cross_other,
):
    scenes, _, ties, width = along_jac.shape[1:]
    links = cross_jac.shape[1]
    groups = lax.axis_size("group")
    rows = groups * scenes
    ajac = along_jac[0].reshape(scenes, 2 * ties, width)
    cjac = cross_jac[0].reshape(links, 2 * ties, width)
    slots = links + scenes + OCTET

    def pass_on(block):
        n = lax.axis_size("orbit")
        return lax.ppermute(block, "orbit", [(i, (i + 1) % n) for i in range(n)])

    work = 2 * (links + scenes + 1) * 32 * 2 * ties * width
    tie = (slots, ties)
    pair = (slots, 2 * ties)
    full = (rows, width)
    own = (scenes, width)
    lanes = -(-slots // 128) * 128
    term_space = [((slots, width), F32)] * 2
    sems = pltpu.SemaphoreType.DMA
    blocks = links + scenes
    small = [ajac, along_e[0], along_res[0], cross_e[0], cross_res[0], cross_own, cross_group[:, :, 0], cross_other]
    near = call(
        pack_kernel,
        [(a.shape, a.dtype) for a in small]
        + [((1, 2 * ties + 2 * OCTET, width), BF16), ((scenes, ties), F32), (own, F32)],
        [pltpu.SMEM((1, scenes), jnp.int32), pltpu.SMEM((1, scenes), F32)]
        + [((2 * OCTET, width), F32), sems((len(small) + 3,))],
        "pack",
        small + [along_count, damping],
        spaces={i: pltpu.HBM for i in range(len(small) + 2)},
    )
    ajac, edge, live, damp = near[0], pass_on(near[8]), near[9], near[10]
    part_tie = (blocks, ties)
    put = ((rows, slots), BF16)
    pick = ((slots, rows), BF16)
    term = ((blocks, width), F32)
    cjac, coef, put1, put2, pick1, pick2, t1, t2 = call(
        setup_kernel,
        [(cjac.shape, BF16), ((3,) + part_tie, F32), put, put, pick, pick, term, term],
        [(part_tie, F32)] * 3 + [((OCTET, lanes), jnp.int32), sems((links // OCTET,))],
        "setup",
        [cjac, *near[:8], live],
        work,
        {0: pltpu.HBM},
    )

    def turn(start, count, refs, after):
        outs = [((min(count, j.shape[0]),) + j.shape[1:], BF16) for j in refs]
        share = work * sum(o[0][0] for o in outs) // blocks
        return call(functools.partial(turn_kernel, start), outs, [], "turn", (after,) + refs, share)

    def project(field, turned, refs):
        scratch = [((2, slots, width), F32)] * 2
        kernel = functools.partial(project_kernel, turned)
        return call(kernel, [(pair, F32)], scratch, "project", (field, pick1, pick2) + tuple(refs), work)[0]

    def finish(sums, res=None):
        args = sums if res is None else sums + [res]
        kernel = functools.partial(gather_kernel, scenes, res is None, len(sums))
        field, packet = call(kernel, [(full, F32), ((OCTET, width), F32)], [], "finish", args)
        return field, orbit_packets(packet)

    sent, coef, ejac = call(
        rhs_kernel,
        [(full, BF16), ((3,) + tie, F32), ((1, 2 * ties, width), BF16)],
        term_space,
        "rhs",
        (coef, t1, t2, edge, put1, put2),
        work // blocks,
    )
    jacs = (cjac, ajac, ejac)
    half = links // 2
    turned = []

    def more(after, done):
        turned.extend([*done, *turn(half, links - half, (cjac,), after)])

    sums = group_sum_but_last(sent, turn(0, half, (cjac,), sent), more)
    res, packets = finish(sums)
    part = project(res, (True, True, False, False), turned + [ajac, ejac])
    fixed = (coef, put1, put2, damp) + jacs
    scratch = [(pair, F32), (tie, F32), (tie, F32)] + term_space + [(full, F32)]
    sent, obs = call(
        functools.partial(step_kernel, 0, scenes),
        [(full, BF16), (pair, F32)],
        scratch,
        "step",
        (part, *packets) + fixed + (res,),
        work,
    )
    turned += turn(0, scenes, (ajac, ejac), sent)
    state = ()
    x = jnp.zeros(own, F32)
    for step in range(1, ITERS):
        field, packets = finish(group_sum_but_last(sent), res)
        part = project(field, (True,) * 4, turned)
        sent, obs, res, image, shadow, direction, x, scal = call(
            functools.partial(step_kernel, step, scenes),
            [(full, BF16), (pair, F32), (full, F32), (full, F32), (pair, F32), (own, F32), (own, F32), ((OCTET, width // 2), F32)],
            scratch,
            "step",
            (part, *packets) + fixed + (res, field, obs, x) + state,
            work,
        )
        state = (image, shadow, direction, scal)
    field, packets = finish(group_sum_but_last(sent), res)
    x, res = call(
        functools.partial(final_kernel, ITERS - 1, scenes),
        [(own, F32), (own, F32)],
        [],
        "final",
        (field, *packets, res, image, direction, x, scal),
    )
    return x[None], res[None]


def solution(mesh):
    placed = (
        P("group", "orbit", None, None, None),
        P("group", "orbit", None, None),
        P("group", "orbit", None, None),
        P("group", "orbit"),
        P("group", "orbit"),
        P("group", "orbit", None, None, None),
        P("group", "orbit", None, None),
        P("group", "orbit", None, None),
        P("group", "orbit"),
        P("group", "orbit", None),
        P("group", "orbit"),
    )
    return jax.shard_map(
        on_device,
        mesh=mesh,
        in_specs=placed,
        out_specs=(P("group", "orbit", None), P("group", "orbit", None)),
        check_vma=False,
    )
```

```python
import functools

import jax
import jax.numpy as jnp
from jax import lax
from jax.experimental import pallas as pl
from jax.experimental.pallas import tpu as pltpu
from jax.sharding import PartitionSpec as P

ITERS = 4
F32, BF16 = jnp.float32, jnp.bfloat16
OCTET = 8


def dot(a, b):
    return lax.dot_general(a, b, (((1,), (0,)), ((), ())), preferred_element_type=F32)


def dot_t(a, b):
    return lax.dot_general(a, b, (((1,), (1,)), ((), ())), preferred_element_type=F32)


def halves(x):
    high = x.astype(BF16)
    return high, (x - high.astype(F32)).astype(BF16)


def row_of(shape):
    return lax.broadcasted_iota(jnp.int32, shape, 0)


def octets(refs, body):
    slot = 0
    for number, ref in enumerate(refs):
        blocks = ref.shape[0]
        for at in range(0, blocks, OCTET):
            body(number, ref, at, slot + at, min(OCTET, blocks - at))
        slot += -(-blocks // OCTET) * OCTET


def project_kernel(turned, field_ref, pick1_ref, pick2_ref, *refs):
    *jac_refs, out_ref, l1_ref, l2_ref = refs
    product = [dot if is_turned else dot_t for is_turned in turned]
    ties = out_ref.shape[1] // 2
    high, low = halves(field_ref[...])
    for pick_ref, left_ref in ((pick1_ref, l1_ref), (pick2_ref, l2_ref)):
        left_ref[0] = dot(pick_ref[...], high)
        left_ref[1] = dot(pick_ref[...], low)

    def body(number, ref, at, slot, count):
        rows = pl.ds(slot, OCTET)
        left = jnp.concatenate([l1_ref[0, rows], l2_ref[0, rows], l1_ref[1, rows], l2_ref[1, rows]])
        left = left.astype(BF16)
        total = jnp.zeros((OCTET, 2 * ties), F32)
        for j in range(count):
            got = product[number](left, ref[at + j])
            one = got[0:8, :ties] + got[16:24, :ties]
            two = got[8:16, ties:] + got[24:32, ties:]
            got = jnp.concatenate([one, two], axis=1)
            total = jnp.where(row_of(total.shape) == j, got, total)
        out_ref[rows] = total

    octets(jac_refs, body)


def turn_kernel(start, after_ref, *refs):
    half = len(refs) // 2
    for ref, out_ref in zip(refs[:half], refs[half:]):

        @pl.loop(0, out_ref.shape[0])
        def _(i, ref=ref, out_ref=out_ref):
            out_ref[i] = ref[start + i].T


def terms(q1, q2, ref, at, count):
    zero = jnp.zeros_like(q1)
    total = jnp.zeros((2 * OCTET, ref.shape[2]), F32)
    for j in range(count):
        chosen = row_of(q1.shape) == j
        top = jnp.concatenate([jnp.where(chosen, q1, 0.0), zero], axis=1)
        low = jnp.concatenate([zero, jnp.where(chosen, q2, 0.0)], axis=1)
        total = total + dot(jnp.concatenate([top, low]).astype(BF16), ref[at + j])
    return total[:OCTET], total[OCTET:]


def scatter(t1_ref, t2_ref, put1_ref, put2_ref):
    out = None
    for t_ref, put_ref in ((t1_ref, put1_ref), (t2_ref, put2_ref)):
        for part in halves(t_ref[...]):
            term = dot(put_ref[...], part)
            out = term if out is None else out + term
    return out


def backward(q1_ref, q2_ref, put1_ref, put2_ref, cjac_ref, ajac_ref, ejac_ref, t1_ref, t2_ref):
    def body(number, ref, at, slot, count):
        rows = pl.ds(slot, OCTET)
        t1_ref[rows], t2_ref[rows] = terms(q1_ref[rows], q2_ref[rows], ref, at, count)

    octets((cjac_ref, ajac_ref, ejac_ref), body)
    return scatter(t1_ref, t2_ref, put1_ref, put2_ref)


def elimination(e1, e2, live):
    over = live / (1.0 + e1 * e1 + e2 * e2)
    return (1.0 + e2 * e2) * over, e1 * e2 * over, (1.0 + e1 * e1) * over


def settled(c11, c12, c22, r1, r2):
    return c11 * r1 - c12 * r2, c22 * r2 - c12 * r1


def live_rows(count_ref, out_ref):
    lane = lax.broadcasted_iota(jnp.int32, (1, out_ref.shape[1]), 1)
    for i in range(out_ref.shape[0]):
        out_ref[i : i + 1, :] = jnp.where(lane < count_ref[0, i], 1.0, 0.0)


def fetch(pairs, sems):
    copies = [pltpu.make_async_copy(a, b, sems.at[i]) for i, (a, b) in enumerate(pairs)]
    for copy in copies:
        copy.start()
    return copies


def pack_kernel(*refs):
    jac_ref, far_refs, count_ref, scale_ref, refs = refs[0], refs[1:8], refs[8], refs[9], refs[10:]
    near_refs, out_ref, live_ref, damp_ref = refs[:7], refs[7], refs[8], refs[9]
    tally_ref, factor_ref, wide_ref, sems = refs[10:]
    e_ref, res_ref = near_refs[:2]
    last, height, ties = jac_ref.shape[0] - 1, jac_ref.shape[1], e_ref.shape[2]
    pairs = list(zip(far_refs, near_refs)) + [(count_ref, tally_ref), (scale_ref, factor_ref)]
    copies = fetch(pairs + [(jac_ref.at[pl.ds(last, 1)], out_ref.at[:, :height])], sems)
    for copy in copies[: len(pairs)]:
        copy.wait()
    wide_ref[...] = jnp.zeros_like(wide_ref)
    for i, ref in enumerate((e_ref, res_ref)):
        rest = ref[last]
        for j in range(3):
            part = rest.astype(BF16).astype(F32)
            rest = rest - part
            wide_ref[4 * j + 2 * i : 4 * j + 2 * i + 2, :ties] = part
    live_rows(tally_ref, live_ref)
    wide_ref[12:13, :ties] = live_ref[last : last + 1, :]
    out_ref[0, height:] = wide_ref[...].astype(BF16)
    for i in range(damp_ref.shape[0]):
        damp_ref[i : i + 1, :] = jnp.full((1, damp_ref.shape[1]), factor_ref[0, i], F32)
    for copy in copies[len(pairs) :]:
        copy.wait()


def setup_kernel(cjac_ref, ajac_ref, *refs):
    ae_ref, ares_ref, ce_ref, cres_ref, own_ref, group_ref, other_ref, lived_ref = refs[:8]
    out_cjac_ref, out_ajac_ref, coef_ref, put1_ref, put2_ref, pick1_ref, pick2_ref, t1_ref, t2_ref = refs[8:17]
    live_ref, q1_ref, q2_ref, index_ref, sems = refs[17:]
    copies = []
    for ref, out_ref in ((cjac_ref, out_cjac_ref), (ajac_ref, out_ajac_ref)):
        for at in range(0, ref.shape[0], OCTET):
            part = pl.ds(at, OCTET)
            copies.append(pltpu.make_async_copy(ref.at[part], out_ref.at[part], sems.at[len(copies)]))
    for copy in copies:
        copy.start()
    links, scenes = cjac_ref.shape[0], ajac_ref.shape[0]
    blocks = links + scenes
    live_ref[0:links] = jnp.ones((links, live_ref.shape[1]), F32)
    live_ref[links:blocks] = lived_ref[...]
    for rows, e_ref, res_ref in ((slice(0, links), ce_ref, cres_ref), (slice(links, blocks), ae_ref, ares_ref)):
        c = elimination(e_ref[:, 0, :], e_ref[:, 1, :], live_ref[rows])
        for i in range(3):
            coef_ref[i, rows] = c[i]
        q1_ref[rows], q2_ref[rows] = settled(*c, res_ref[:, 0, :], res_ref[:, 1, :])

    first = lax.axis_index("group") * scenes
    slots = put1_ref.shape[1]
    index_ref[...] = jnp.zeros_like(index_ref)
    index_ref[0:1, :links] = own_ref[...] + first
    index_ref[1:2, :links] = group_ref[...] * scenes + other_ref[...]
    lane = lax.broadcasted_iota(jnp.int32, (1, index_ref.shape[1]), 1)
    one = jnp.where(lane < links, index_ref[0:1, :], jnp.where(lane < blocks, first + lane - links, -1))
    two = jnp.where(lane < blocks - 1, first + lane - links + 1, jnp.where(lane == blocks, first, -1))
    two = jnp.where(lane < links, index_ref[1:2, :], two)
    for index, put_ref, pick_ref in ((one, put1_ref, pick1_ref), (two, put2_ref, pick2_ref)):
        shape = (put_ref.shape[0], index.shape[1])
        table = jnp.where(row_of(shape) == index, 1.0, 0.0)
        put_ref[...] = table[:, :slots].astype(BF16)
        pick_ref[...] = table.T[:slots].astype(BF16)

    count = len(copies)
    cuts = [0, 2 * count // 5, 4 * count // 5, count]
    for number in range(count):
        if number in cuts:
            for copy in copies[number : cuts[cuts.index(number) + 1]]:
                copy.wait()
        at = number * OCTET
        ref, at = (out_cjac_ref, at) if at < links else (out_ajac_ref, at - links)
        rows = pl.ds(number * OCTET, OCTET)
        t1_ref[rows], t2_ref[rows] = terms(q1_ref[rows], q2_ref[rows], ref, at, OCTET)


def rhs_kernel(coef_ref, t1_ref, t2_ref, edge_ref, put1_ref, put2_ref, out_ref, out_coef_ref, ejac_ref, all1_ref, all2_ref):
    blocks, ties = t1_ref.shape[0], coef_ref.shape[2]
    height = ejac_ref.shape[1]
    rows = pl.ds(blocks, OCTET)
    ejac_ref[...] = edge_ref[:, :height]
    parts = edge_ref[0, height:, :ties].astype(F32)
    e1, e2, r1, r2 = (parts[i : i + 1] + parts[i + 4 : i + 5] + parts[i + 8 : i + 9] for i in range(4))
    c = elimination(e1, e2, parts[12:13])
    fill = lambda x: jnp.where(row_of((OCTET, x.shape[1])) == 0, x, 0.0)
    for i in range(3):
        out_coef_ref[i, :blocks] = coef_ref[i]
        out_coef_ref[i, rows] = fill(c[i])
    q1, q2 = settled(*c, r1, r2)
    all1_ref[:blocks] = t1_ref[...]
    all2_ref[:blocks] = t2_ref[...]
    all1_ref[rows], all2_ref[rows] = terms(fill(q1), fill(q2), ejac_ref, 0, 1)
    out_ref[...] = scatter(all1_ref, all2_ref, put1_ref, put2_ref).astype(BF16)


def gather_kernel(scenes, start, parts, *refs):
    first = pl.multiple_of(lax.axis_index("group") * scenes, scenes)
    field = refs[0][...].astype(F32)
    for ref in refs[1:parts]:
        field = field + ref[...].astype(F32)
    refs = refs[parts:]
    if start:
        out_ref, packet_ref = refs
        field = -field
    else:
        res_ref, out_ref, packet_ref = refs
    out_ref[...] = field
    packet_ref[...] = jnp.zeros_like(packet_ref)
    if not start:
        res = res_ref[...]
        half = packet_ref.shape[1] // 2
        packet_ref[0:1, :half] = jnp.full((1, half), jnp.sum(res * res), F32)
        packet_ref[0:1, half:] = jnp.full((1, half), jnp.sum(res * field), F32)
    packet_ref[1:2, :] = out_ref[pl.ds(first, OCTET), :][0:1]
    packet_ref[2:3, :] = out_ref[pl.ds(pl.multiple_of(first + scenes - OCTET, OCTET), OCTET), :][OCTET - 1 :]


def outside(packet_refs, ajac_ref, ejac_ref, part_ref, slot):
    _, one, _, three = packet_refs
    ties = part_ref.shape[1] // 2
    last = ajac_ref.shape[0] - 1
    even = lax.axis_index("orbit") % 2 == 0
    after = jnp.where(even, one[1:2, :], three[1:2, :])
    ahead = jnp.where(even, three[2:3, :], one[2:3, :])
    sub = row_of((OCTET, after.shape[1]))
    both = jnp.where(sub == last % OCTET, after, jnp.where(sub == 0, ahead, 0.0))
    high = both.astype(BF16).astype(F32)
    left = jnp.concatenate([high, both - high]).astype(BF16)
    got = dot_t(left, ajac_ref[last])
    got = got[:OCTET] + got[OCTET:]
    tail = pl.ds(slot + last - last % OCTET, OCTET)
    keep = row_of((OCTET, ties)) == last % OCTET
    part_ref[tail, ties:] = part_ref[tail, ties:] + jnp.where(keep, got[:, ties:], 0.0)
    got = dot_t(left, ejac_ref[0])
    got = got[:OCTET] + got[OCTET:]
    tail = pl.ds(slot + last + 1, OCTET)
    keep = row_of((OCTET, ties)) == 0
    part_ref[tail, :ties] = part_ref[tail, :ties] + jnp.where(keep, got[:, :ties], 0.0)


def scalars(packet_refs, scal_ref, step):
    mine, one, two, three = (ref[0:1, :] for ref in packet_refs)
    sums = (mine + one) + (two + three)
    half = sums.shape[1] // 2
    now, along = sums[:, :half], sums[:, half:]
    if step == 0:
        beta = jnp.zeros_like(now)
        alpha = now / along
    else:
        before, last = scal_ref[0:1, :], scal_ref[1:2, :]
        beta = now / before
        alpha = now / (along - beta * now / last)
    return now, alpha, beta


def wide(x):
    return jnp.concatenate([x, x], axis=1)


def step_kernel(step, scenes, *refs):
    refs = list(refs)
    take = lambda n: [refs.pop(0) for _ in range(n)]
    (part_ref,) = take(1)
    packet_refs = take(4)
    coef_ref, put1_ref, put2_ref, damp_ref, cjac_ref, ajac_ref, ejac_ref = take(7)
    (res_ref,) = take(1)
    if step >= 1:
        field_ref, obs_ref, x_ref = take(3)
    if step >= 2:
        image_ref, shadow_ref, dir_ref, scal_ref = take(4)
    (sent_ref, out_obs_ref) = take(2)
    if step >= 1:
        out_res_ref, out_image_ref, out_shadow_ref, out_dir_ref, out_x_ref, out_scal_ref = take(6)
    part_scr, q1_ref, q2_ref, t1_ref, t2_ref, c_ref = take(6)
    ties = q1_ref.shape[1]
    first = pl.multiple_of(lax.axis_index("group") * scenes, scenes)
    own = pl.ds(first, scenes)

    part_scr[...] = part_ref[...]
    outside(packet_refs, ajac_ref, ejac_ref, part_scr, cjac_ref.shape[0])
    if step == 0:
        out_obs_ref[...] = part_scr[...]
        now_res_ref = res_ref
    else:
        now, alpha, beta = scalars(packet_refs, None if step == 1 else scal_ref, step - 1)
        out_scal_ref[...] = jnp.zeros_like(out_scal_ref)
        out_scal_ref[0:1, :] = now
        out_scal_ref[1:2, :] = alpha
        alpha, beta = wide(alpha), wide(beta)
        image, shadow, direction = field_ref[...], part_scr[...], res_ref[own]
        if step >= 2:
            image = image + beta * image_ref[...]
            shadow = shadow + beta * shadow_ref[...]
            direction = direction + beta * dir_ref[...]
            out_x_ref[...] = x_ref[...] + alpha * direction
        else:
            out_x_ref[...] = alpha * direction
        out_image_ref[...] = image
        out_shadow_ref[...] = shadow
        out_dir_ref[...] = direction
        out_res_ref[...] = res_ref[...] - alpha * image
        out_obs_ref[...] = obs_ref[...] - alpha * shadow
        now_res_ref = out_res_ref
    r1, r2 = out_obs_ref[:, :ties], out_obs_ref[:, ties:]
    q1_ref[...], q2_ref[...] = settled(coef_ref[0], coef_ref[1], coef_ref[2], r1, r2)
    c_ref[...] = backward(q1_ref, q2_ref, put1_ref, put2_ref, cjac_ref, ajac_ref, ejac_ref, t1_ref, t2_ref)
    c_ref[own] = c_ref[own] + damp_ref[...] * now_res_ref[own]
    sent_ref[...] = c_ref[...].astype(BF16)


def final_kernel(step, scenes, *refs):
    field_ref, m, a, b, c, res_ref, image_ref, dir_ref, x_ref, scal_ref, out_x_ref, out_res_ref = refs
    own = pl.ds(pl.multiple_of(lax.axis_index("group") * scenes, scenes), scenes)
    now, alpha, beta = scalars((m, a, b, c), scal_ref, step)
    alpha, beta = wide(alpha), wide(beta)
    res = res_ref[own]
    out_x_ref[...] = x_ref[...] + alpha * (res + beta * dir_ref[...])
    out_res_ref[...] = res - alpha * (field_ref[own] + beta * image_ref[own])


def call(kernel, outs, scratch, name, args, flops=0, spaces={}, limit=None):
    args = [
        pltpu.with_memory_space_constraint(a, pltpu.HBM) if spaces.get(i) == pltpu.HBM else a
        for i, a in enumerate(args)
    ]
    at = lambda i: pl.BlockSpec(memory_space=spaces.get(i, pltpu.VMEM))
    moved = sum(a.size * a.dtype.itemsize for a in args)
    return pl.pallas_call(
        kernel,
        out_shape=[jax.ShapeDtypeStruct(*o) for o in outs],
        in_specs=[at(i) for i in range(len(args))],
        out_specs=[pl.BlockSpec(memory_space=pltpu.VMEM)] * len(outs),
        scratch_shapes=[pltpu.VMEM(*s) if isinstance(s, tuple) else s for s in scratch],
        cost_estimate=pl.CostEstimate(flops=flops, bytes_accessed=moved, transcendentals=0),
        compiler_params=pltpu.CompilerParams(vmem_limit_bytes=limit or VMEM_LIMIT),
        name=name,
    )(*args)


VMEM_LIMIT = 16 << 20


def group_sum_but_last(sent, first=(), between=None):
    size = lax.axis_size("group")
    stride, pairs = 1, None
    while stride < size:
        masks = (1, 2, 3) if 4 * stride <= size else (1,)
        got = [swap(sent, "group", mask * stride) for mask in masks]
        stride *= len(masks) + 1
        pairs = [sent] + got
        if stride < size or len(pairs) > 2:
            low = [p.astype(F32) for p in pairs]
            total = low[0] + low[1]
            if len(low) > 2:
                total = total + (low[2] + low[3])
            if stride < size:
                sent, first = lax.optimization_barrier((total.astype(BF16), first))
                if between is not None:
                    between(sent, first)
                    first, between = (), None
            else:
                pairs = [total]
    return pairs


def swap(block, axis, mask):
    return lax.ppermute(block, axis, [(i, i ^ mask) for i in range(lax.axis_size(axis))])


def orbit_packets(packet):
    n = lax.axis_size("orbit")
    return [packet] + [lax.ppermute(packet, "orbit", [(i, i ^ mask) for i in range(n)]) for mask in range(1, n)]


def on_device(
    along_jac,
    along_res,
    along_e,
    along_count,
    damping,
    cross_jac,
    cross_res,
    cross_e,
    cross_own,
    cross_group,
    cross_other,
):
    scenes, _, ties, width = along_jac.shape[1:]
    links = cross_jac.shape[1]
    groups = lax.axis_size("group")
    rows = groups * scenes
    ajac = along_jac[0].reshape(scenes, 2 * ties, width)
    cjac = cross_jac[0].reshape(links, 2 * ties, width)
    slots = links + scenes + OCTET

    def pass_on(block):
        n = lax.axis_size("orbit")
        return lax.ppermute(block, "orbit", [(i, (i + 1) % n) for i in range(n)])

    work = 2 * (links + scenes + 1) * 32 * 2 * ties * width
    tie = (slots, ties)
    pair = (slots, 2 * ties)
    full = (rows, width)
    own = (scenes, width)
    lanes = -(-slots // 128) * 128
    term_space = [((slots, width), F32)] * 2
    sems = pltpu.SemaphoreType.DMA
    blocks = links + scenes
    small = [ajac, along_e[0], along_res[0], cross_e[0], cross_res[0], cross_own, cross_group[:, :, 0], cross_other]
    near = call(
        pack_kernel,
        [(a.shape, a.dtype) for a in small[1:]]
        + [((1, 2 * ties + 2 * OCTET, width), BF16), ((scenes, ties), F32), (own, F32)],
        [pltpu.SMEM((1, scenes), jnp.int32), pltpu.SMEM((1, scenes), F32)]
        + [((2 * OCTET, width), F32), sems((len(small) + 2,))],
        "pack",
        small + [along_count, damping],
        spaces={i: pltpu.HBM for i in range(len(small) + 2)},
    )
    edge, live, damp = pass_on(near[7]), near[8], near[9]
    part_tie = (blocks, ties)
    put = ((rows, slots), BF16)
    pick = ((slots, rows), BF16)
    term = ((blocks, width), F32)
    cjac, ajac, coef, put1, put2, pick1, pick2, t1, t2 = call(
        setup_kernel,
        [(cjac.shape, BF16), (ajac.shape, BF16), ((3,) + part_tie, F32), put, put, pick, pick, term, term],
        [(part_tie, F32)] * 3 + [((OCTET, lanes), jnp.int32), sems((blocks // OCTET,))],
        "setup",
        [cjac, ajac, *near[:7], live],
        work,
        {0: pltpu.HBM, 1: pltpu.HBM},
    )

    def turn(start, count, refs, after):
        outs = [((min(count, j.shape[0]),) + j.shape[1:], BF16) for j in refs]
        share = work * sum(o[0][0] for o in outs) // blocks
        return call(functools.partial(turn_kernel, start), outs, [], "turn", (after,) + refs, share)

    def project(field, turned, refs):
        scratch = [((2, slots, width), F32)] * 2
        kernel = functools.partial(project_kernel, turned)
        return call(kernel, [(pair, F32)], scratch, "project", (field, pick1, pick2) + tuple(refs), work)[0]

    def finish(sums, res=None):
        args = sums if res is None else sums + [res]
        kernel = functools.partial(gather_kernel, scenes, res is None, len(sums))
        field, packet = call(kernel, [(full, F32), ((OCTET, width), F32)], [], "finish", args)
        return field, orbit_packets(packet)

    sent, coef, ejac = call(
        rhs_kernel,
        [(full, BF16), ((3,) + tie, F32), ((1, 2 * ties, width), BF16)],
        term_space,
        "rhs",
        (coef, t1, t2, edge, put1, put2),
        work // blocks,
    )
    jacs = (cjac, ajac, ejac)
    half = links // 2
    turned = []

    def more(after, done):
        turned.extend([*done, *turn(half, links - half, (cjac,), after)])

    sums = group_sum_but_last(sent, turn(0, half, (cjac,), sent), more)
    res, packets = finish(sums)
    part = project(res, (True, True, False, False), turned + [ajac, ejac])
    fixed = (coef, put1, put2, damp) + jacs
    scratch = [(pair, F32), (tie, F32), (tie, F32)] + term_space + [(full, F32)]
    sent, obs = call(
        functools.partial(step_kernel, 0, scenes),
        [(full, BF16), (pair, F32)],
        scratch,
        "step",
        (part, *packets) + fixed + (res,),
        work,
    )
    turned += turn(0, scenes, (ajac, ejac), sent)
    state = ()
    x = jnp.zeros(own, F32)
    for step in range(1, ITERS):
        field, packets = finish(group_sum_but_last(sent), res)
        part = project(field, (True,) * 4, turned)
        sent, obs, res, image, shadow, direction, x, scal = call(
            functools.partial(step_kernel, step, scenes),
            [(full, BF16), (pair, F32), (full, F32), (full, F32), (pair, F32), (own, F32), (own, F32), ((OCTET, width // 2), F32)],
            scratch,
            "step",
            (part, *packets) + fixed + (res, field, obs, x) + state,
            work,
        )
        state = (image, shadow, direction, scal)
    field, packets = finish(group_sum_but_last(sent), res)
    x, res = call(
        functools.partial(final_kernel, ITERS - 1, scenes),
        [(own, F32), (own, F32)],
        [],
        "final",
        (field, *packets, res, image, direction, x, scal),
    )
    return x[None], res[None]


def solution(mesh):
    placed = (
        P("group", "orbit", None, None, None),
        P("group", "orbit", None, None),
        P("group", "orbit", None, None),
        P("group", "orbit"),
        P("group", "orbit"),
        P("group", "orbit", None, None, None),
        P("group", "orbit", None, None),
        P("group", "orbit", None, None),
        P("group", "orbit"),
        P("group", "orbit", None),
        P("group", "orbit"),
    )
    return jax.shard_map(
        on_device,
        mesh=mesh,
        in_specs=placed,
        out_specs=(P("group", "orbit", None), P("group", "orbit", None)),
        check_vma=False,
    )
```

```python
import functools

import jax
import jax.numpy as jnp
from jax import lax
from jax.experimental import pallas as pl
from jax.experimental.pallas import tpu as pltpu
from jax.sharding import PartitionSpec as P

ITERS = 4
F32, BF16 = jnp.float32, jnp.bfloat16
OCTET = 8


def dot(a, b):
    return lax.dot_general(a, b, (((1,), (0,)), ((), ())), preferred_element_type=F32)


def dot_t(a, b):
    return lax.dot_general(a, b, (((1,), (1,)), ((), ())), preferred_element_type=F32)


def halves(x):
    high = x.astype(BF16)
    return high, (x - high.astype(F32)).astype(BF16)


def row_of(shape):
    return lax.broadcasted_iota(jnp.int32, shape, 0)


def octets(refs, body):
    slot = 0
    for number, ref in enumerate(refs):
        blocks = ref.shape[0]
        for at in range(0, blocks, OCTET):
            body(number, ref, at, slot + at, min(OCTET, blocks - at))
        slot += -(-blocks // OCTET) * OCTET


def project_kernel(turned, field_ref, pick1_ref, pick2_ref, *refs):
    *jac_refs, out_ref, l1_ref, l2_ref = refs
    product = [dot if is_turned else dot_t for is_turned in turned]
    ties = out_ref.shape[1] // 2
    high, low = halves(field_ref[...])
    for pick_ref, left_ref in ((pick1_ref, l1_ref), (pick2_ref, l2_ref)):
        left_ref[0] = dot(pick_ref[...], high)
        left_ref[1] = dot(pick_ref[...], low)

    def body(number, ref, at, slot, count):
        rows = pl.ds(slot, OCTET)
        left = jnp.concatenate([l1_ref[0, rows], l2_ref[0, rows], l1_ref[1, rows], l2_ref[1, rows]])
        left = left.astype(BF16)
        total = jnp.zeros((OCTET, 2 * ties), F32)
        for j in range(count):
            got = product[number](left, ref[at + j])
            one = got[0:8, :ties] + got[16:24, :ties]
            two = got[8:16, ties:] + got[24:32, ties:]
            got = jnp.concatenate([one, two], axis=1)
            total = jnp.where(row_of(total.shape) == j, got, total)
        out_ref[rows] = total

    octets(jac_refs, body)


def turn_kernel(start, after_ref, *refs):
    half = len(refs) // 2
    for ref, out_ref in zip(refs[:half], refs[half:]):

        @pl.loop(0, out_ref.shape[0])
        def _(i, ref=ref, out_ref=out_ref):
            out_ref[i] = ref[start + i].T


def terms(q1, q2, ref, at, count):
    zero = jnp.zeros_like(q1)
    total = jnp.zeros((2 * OCTET, ref.shape[2]), F32)
    for j in range(count):
        chosen = row_of(q1.shape) == j
        top = jnp.concatenate([jnp.where(chosen, q1, 0.0), zero], axis=1)
        low = jnp.concatenate([zero, jnp.where(chosen, q2, 0.0)], axis=1)
        total = total + dot(jnp.concatenate([top, low]).astype(BF16), ref[at + j])
    return total[:OCTET], total[OCTET:]


def scatter(t1_ref, t2_ref, put1_ref, put2_ref):
    out = None
    for t_ref, put_ref in ((t1_ref, put1_ref), (t2_ref, put2_ref)):
        for part in halves(t_ref[...]):
            term = dot(put_ref[...], part)
            out = term if out is None else out + term
    return out


def backward(q1_ref, q2_ref, put1_ref, put2_ref, cjac_ref, ajac_ref, ejac_ref, t1_ref, t2_ref):
    def body(number, ref, at, slot, count):
        rows = pl.ds(slot, OCTET)
        t1_ref[rows], t2_ref[rows] = terms(q1_ref[rows], q2_ref[rows], ref, at, count)

    octets((cjac_ref, ajac_ref, ejac_ref), body)
    return scatter(t1_ref, t2_ref, put1_ref, put2_ref)


def elimination(e1, e2, live):
    over = live / (1.0 + e1 * e1 + e2 * e2)
    return (1.0 + e2 * e2) * over, e1 * e2 * over, (1.0 + e1 * e1) * over


def settled(c11, c12, c22, r1, r2):
    return c11 * r1 - c12 * r2, c22 * r2 - c12 * r1


def live_rows(count_ref, out_ref):
    lane = lax.broadcasted_iota(jnp.int32, (1, out_ref.shape[1]), 1)
    for i in range(out_ref.shape[0]):
        out_ref[i : i + 1, :] = jnp.where(lane < count_ref[0, i], 1.0, 0.0)


def fetch(pairs, sems):
    copies = [pltpu.make_async_copy(a, b, sems.at[i]) for i, (a, b) in enumerate(pairs)]
    for copy in copies:
        copy.start()
    return copies


def pack_kernel(*refs):
    jac_ref, far_refs, count_ref, scale_ref, refs = refs[0], refs[1:8], refs[8], refs[9], refs[10:]
    near_refs, out_ref, live_ref, damp_ref = refs[:7], refs[7], refs[8], refs[9]
    tally_ref, factor_ref, wide_ref, sems = refs[10:]
    e_ref, res_ref = near_refs[:2]
    last, height, ties = jac_ref.shape[0] - 1, jac_ref.shape[1], e_ref.shape[2]
    pairs = list(zip(far_refs, near_refs)) + [(count_ref, tally_ref), (scale_ref, factor_ref)]
    copies = fetch(pairs + [(jac_ref.at[pl.ds(last, 1)], out_ref.at[:, :height])], sems)
    for copy in copies[: len(pairs)]:
        copy.wait()
    wide_ref[...] = jnp.zeros_like(wide_ref)
    for i, ref in enumerate((e_ref, res_ref)):
        rest = ref[last]
        for j in range(3):
            part = rest.astype(BF16).astype(F32)
            rest = rest - part
            wide_ref[4 * j + 2 * i : 4 * j + 2 * i + 2, :ties] = part
    live_rows(tally_ref, live_ref)
    wide_ref[12:13, :ties] = live_ref[last : last + 1, :]
    out_ref[0, height:] = wide_ref[...].astype(BF16)
    for i in range(damp_ref.shape[0]):
        damp_ref[i : i + 1, :] = jnp.full((1, damp_ref.shape[1]), factor_ref[0, i], F32)
    for copy in copies[len(pairs) :]:
        copy.wait()


def setup_kernel(cjac_ref, ajac_ref, *refs):
    ae_ref, ares_ref, ce_ref, cres_ref, own_ref, group_ref, other_ref, lived_ref = refs[:8]
    out_cjac_ref, out_ajac_ref, coef_ref, put1_ref, put2_ref, pick1_ref, pick2_ref, t1_ref, t2_ref = refs[8:17]
    live_ref, q1_ref, q2_ref, index_ref, sems = refs[17:]
    copies = []
    for ref, out_ref in ((cjac_ref, out_cjac_ref), (ajac_ref, out_ajac_ref)):
        for at in range(0, ref.shape[0], OCTET):
            part = pl.ds(at, OCTET)
            copies.append(pltpu.make_async_copy(ref.at[part], out_ref.at[part], sems.at[len(copies)]))
    for copy in copies:
        copy.start()
    links, scenes = cjac_ref.shape[0], ajac_ref.shape[0]
    blocks = links + scenes
    live_ref[0:links] = jnp.ones((links, live_ref.shape[1]), F32)
    live_ref[links:blocks] = lived_ref[...]
    for rows, e_ref, res_ref in ((slice(0, links), ce_ref, cres_ref), (slice(links, blocks), ae_ref, ares_ref)):
        c = elimination(e_ref[:, 0, :], e_ref[:, 1, :], live_ref[rows])
        for i in range(3):
            coef_ref[i, rows] = c[i]
        q1_ref[rows], q2_ref[rows] = settled(*c, res_ref[:, 0, :], res_ref[:, 1, :])

    first = lax.axis_index("group") * scenes
    slots = put1_ref.shape[1]
    index_ref[...] = jnp.zeros_like(index_ref)
    index_ref[0:1, :links] = own_ref[...] + first
    index_ref[1:2, :links] = group_ref[...] * scenes + other_ref[...]
    lane = lax.broadcasted_iota(jnp.int32, (1, index_ref.shape[1]), 1)
    one = jnp.where(lane < links, index_ref[0:1, :], jnp.where(lane < blocks, first + lane - links, -1))
    two = jnp.where(lane < blocks - 1, first + lane - links + 1, jnp.where(lane == blocks, first, -1))
    two = jnp.where(lane < links, index_ref[1:2, :], two)
    for index, put_ref, pick_ref in ((one, put1_ref, pick1_ref), (two, put2_ref, pick2_ref)):
        shape = (put_ref.shape[0], index.shape[1])
        table = jnp.where(row_of(shape) == index, 1.0, 0.0)
        put_ref[...] = table[:, :slots].astype(BF16)
        pick_ref[...] = table.T[:slots].astype(BF16)

    count = len(copies)
    cuts = [0, 2 * count // 5, 4 * count // 5, count]
    for number in range(count):
        if number in cuts:
            for copy in copies[number : cuts[cuts.index(number) + 1]]:
                copy.wait()
        at = number * OCTET
        ref, at = (out_cjac_ref, at) if at < links else (out_ajac_ref, at - links)
        rows = pl.ds(number * OCTET, OCTET)
        t1_ref[rows], t2_ref[rows] = terms(q1_ref[rows], q2_ref[rows], ref, at, OCTET)


def rhs_kernel(coef_ref, t1_ref, t2_ref, edge_ref, put1_ref, put2_ref, out_ref, out_coef_ref, ejac_ref, all1_ref, all2_ref):
    blocks, ties = t1_ref.shape[0], coef_ref.shape[2]
    height = ejac_ref.shape[1]
    rows = pl.ds(blocks, OCTET)
    ejac_ref[...] = edge_ref[:, :height]
    parts = edge_ref[0, height:, :ties].astype(F32)
    e1, e2, r1, r2 = (parts[i : i + 1] + parts[i + 4 : i + 5] + parts[i + 8 : i + 9] for i in range(4))
    c = elimination(e1, e2, parts[12:13])
    fill = lambda x: jnp.where(row_of((OCTET, x.shape[1])) == 0, x, 0.0)
    for i in range(3):
        out_coef_ref[i, :blocks] = coef_ref[i]
        out_coef_ref[i, rows] = fill(c[i])
    q1, q2 = settled(*c, r1, r2)
    all1_ref[:blocks] = t1_ref[...]
    all2_ref[:blocks] = t2_ref[...]
    all1_ref[rows], all2_ref[rows] = terms(fill(q1), fill(q2), ejac_ref, 0, 1)
    out_ref[...] = scatter(all1_ref, all2_ref, put1_ref, put2_ref).astype(BF16)


def gather_kernel(scenes, start, parts, *refs):
    first = pl.multiple_of(lax.axis_index("group") * scenes, scenes)
    field = refs[0][...].astype(F32)
    for ref in refs[1:parts]:
        field = field + ref[...].astype(F32)
    refs = refs[parts:]
    if start:
        out_ref, packet_ref = refs
        field = -field
    else:
        res_ref, out_ref, packet_ref = refs
    out_ref[...] = field
    packet_ref[...] = jnp.zeros_like(packet_ref)
    if not start:
        res = res_ref[...]
        half = packet_ref.shape[1] // 2
        packet_ref[0:1, :half] = jnp.full((1, half), jnp.sum(res * res), F32)
        packet_ref[0:1, half:] = jnp.full((1, half), jnp.sum(res * field), F32)
    packet_ref[1:2, :] = out_ref[pl.ds(first, OCTET), :][0:1]
    packet_ref[2:3, :] = out_ref[pl.ds(pl.multiple_of(first + scenes - OCTET, OCTET), OCTET), :][OCTET - 1 :]


def outside(packet_refs, ajac_ref, ejac_ref, part_ref, slot):
    _, one, _, three = packet_refs
    ties = part_ref.shape[1] // 2
    last = ajac_ref.shape[0] - 1
    even = lax.axis_index("orbit") % 2 == 0
    after = jnp.where(even, one[1:2, :], three[1:2, :])
    ahead = jnp.where(even, three[2:3, :], one[2:3, :])
    sub = row_of((OCTET, after.shape[1]))
    both = jnp.where(sub == last % OCTET, after, jnp.where(sub == 0, ahead, 0.0))
    high = both.astype(BF16).astype(F32)
    left = jnp.concatenate([high, both - high]).astype(BF16)
    got = dot_t(left, ajac_ref[last])
    got = got[:OCTET] + got[OCTET:]
    tail = pl.ds(slot + last - last % OCTET, OCTET)
    keep = row_of((OCTET, ties)) == last % OCTET
    part_ref[tail, ties:] = part_ref[tail, ties:] + jnp.where(keep, got[:, ties:], 0.0)
    got = dot_t(left, ejac_ref[0])
    got = got[:OCTET] + got[OCTET:]
    tail = pl.ds(slot + last + 1, OCTET)
    keep = row_of((OCTET, ties)) == 0
    part_ref[tail, :ties] = part_ref[tail, :ties] + jnp.where(keep, got[:, :ties], 0.0)


def scalars(packet_refs, scal_ref, step):
    mine, one, two, three = (ref[0:1, :] for ref in packet_refs)
    sums = (mine + one) + (two + three)
    half = sums.shape[1] // 2
    now, along = sums[:, :half], sums[:, half:]
    if step == 0:
        beta = jnp.zeros_like(now)
        alpha = now / along
    else:
        before, last = scal_ref[0:1, :], scal_ref[1:2, :]
        beta = now / before
        alpha = now / (along - beta * now / last)
    return now, alpha, beta


def wide(x):
    return jnp.concatenate([x, x], axis=1)


def step_kernel(step, scenes, *refs):
    refs = list(refs)
    take = lambda n: [refs.pop(0) for _ in range(n)]
    (part_ref,) = take(1)
    packet_refs = take(4)
    coef_ref, put1_ref, put2_ref, damp_ref, cjac_ref, ajac_ref, ejac_ref = take(7)
    (res_ref,) = take(1)
    if step >= 1:
        field_ref, obs_ref, x_ref = take(3)
    if step >= 2:
        image_ref, shadow_ref, dir_ref, scal_ref = take(4)
    (sent_ref, out_obs_ref) = take(2)
    if step >= 1:
        out_res_ref, out_image_ref, out_shadow_ref, out_dir_ref, out_x_ref, out_scal_ref = take(6)
    part_scr, q1_ref, q2_ref, t1_ref, t2_ref, c_ref = take(6)
    ties = q1_ref.shape[1]
    first = pl.multiple_of(lax.axis_index("group") * scenes, scenes)
    own = pl.ds(first, scenes)

    part_scr[...] = part_ref[...]
    outside(packet_refs, ajac_ref, ejac_ref, part_scr, cjac_ref.shape[0])
    if step == 0:
        out_obs_ref[...] = part_scr[...]
        now_res_ref = res_ref
    else:
        now, alpha, beta = scalars(packet_refs, None if step == 1 else scal_ref, step - 1)
        out_scal_ref[...] = jnp.zeros_like(out_scal_ref)
        out_scal_ref[0:1, :] = now
        out_scal_ref[1:2, :] = alpha
        alpha, beta = wide(alpha), wide(beta)
        image, shadow, direction = field_ref[...], part_scr[...], res_ref[own]
        if step >= 2:
            image = image + beta * image_ref[...]
            shadow = shadow + beta * shadow_ref[...]
            direction = direction + beta * dir_ref[...]
            out_x_ref[...] = x_ref[...] + alpha * direction
        else:
            out_x_ref[...] = alpha * direction
        out_image_ref[...] = image
        out_shadow_ref[...] = shadow
        out_dir_ref[...] = direction
        out_res_ref[...] = res_ref[...] - alpha * image
        out_obs_ref[...] = obs_ref[...] - alpha * shadow
        now_res_ref = out_res_ref
    r1, r2 = out_obs_ref[:, :ties], out_obs_ref[:, ties:]
    q1_ref[...], q2_ref[...] = settled(coef_ref[0], coef_ref[1], coef_ref[2], r1, r2)
    c_ref[...] = backward(q1_ref, q2_ref, put1_ref, put2_ref, cjac_ref, ajac_ref, ejac_ref, t1_ref, t2_ref)
    c_ref[own] = c_ref[own] + damp_ref[...] * now_res_ref[own]
    sent_ref[...] = c_ref[...].astype(BF16)


def final_kernel(step, scenes, *refs):
    field_ref, m, a, b, c, res_ref, image_ref, dir_ref, x_ref, scal_ref, out_x_ref, out_res_ref = refs
    own = pl.ds(pl.multiple_of(lax.axis_index("group") * scenes, scenes), scenes)
    now, alpha, beta = scalars((m, a, b, c), scal_ref, step)
    alpha, beta = wide(alpha), wide(beta)
    res = res_ref[own]
    out_x_ref[...] = x_ref[...] + alpha * (res + beta * dir_ref[...])
    out_res_ref[...] = res - alpha * (field_ref[own] + beta * image_ref[own])


def call(kernel, outs, scratch, name, args, flops=0, spaces={}, limit=None):
    args = [
        pltpu.with_memory_space_constraint(a, pltpu.HBM) if spaces.get(i) == pltpu.HBM else a
        for i, a in enumerate(args)
    ]
    at = lambda i: pl.BlockSpec(memory_space=spaces.get(i, pltpu.VMEM))
    moved = sum(a.size * a.dtype.itemsize for a in args)
    return pl.pallas_call(
        kernel,
        out_shape=[jax.ShapeDtypeStruct(*o) for o in outs],
        in_specs=[at(i) for i in range(len(args))],
        out_specs=[pl.BlockSpec(memory_space=pltpu.VMEM)] * len(outs),
        scratch_shapes=[pltpu.VMEM(*s) if isinstance(s, tuple) else s for s in scratch],
        cost_estimate=pl.CostEstimate(flops=flops, bytes_accessed=moved, transcendentals=0),
        compiler_params=pltpu.CompilerParams(vmem_limit_bytes=limit or VMEM_LIMIT),
        name=name,
    )(*args)


VMEM_LIMIT = 16 << 20


def group_sum_but_last(sent, first=(), between=None):
    size = lax.axis_size("group")
    stride, pairs = 1, None
    while stride < size:
        masks = (1, 2, 3) if 4 * stride <= size else (1,)
        got = [swap(sent, "group", mask * stride) for mask in masks]
        stride *= len(masks) + 1
        pairs = [sent] + got
        if stride < size or len(pairs) > 2:
            low = [p.astype(F32) for p in pairs]
            total = low[0] + low[1]
            if len(low) > 2:
                total = total + (low[2] + low[3])
            if stride < size:
                sent, first = lax.optimization_barrier((total.astype(BF16), first))
                if between is not None:
                    between(sent, first)
                    first, between = (), None
            else:
                pairs = [total]
    return pairs


def swap(block, axis, mask):
    return lax.ppermute(block, axis, [(i, i ^ mask) for i in range(lax.axis_size(axis))])


def orbit_packets(packet, scenes_only):
    near, far = swap(packet, "orbit", 1), swap(packet, "orbit", 3)
    opposite = packet if scenes_only else swap(packet, "orbit", 2)
    return [packet, near, opposite, far]


def on_device(
    along_jac,
    along_res,
    along_e,
    along_count,
    damping,
    cross_jac,
    cross_res,
    cross_e,
    cross_own,
    cross_group,
    cross_other,
):
    scenes, _, ties, width = along_jac.shape[1:]
    links = cross_jac.shape[1]
    groups = lax.axis_size("group")
    rows = groups * scenes
    ajac = along_jac[0].reshape(scenes, 2 * ties, width)
    cjac = cross_jac[0].reshape(links, 2 * ties, width)
    slots = links + scenes + OCTET

    def pass_on(block):
        n = lax.axis_size("orbit")
        return lax.ppermute(block, "orbit", [(i, (i + 1) % n) for i in range(n)])

    work = 2 * (links + scenes + 1) * 32 * 2 * ties * width
    tie = (slots, ties)
    pair = (slots, 2 * ties)
    full = (rows, width)
    own = (scenes, width)
    lanes = -(-slots // 128) * 128
    term_space = [((slots, width), F32)] * 2
    sems = pltpu.SemaphoreType.DMA
    blocks = links + scenes
    small = [ajac, along_e[0], along_res[0], cross_e[0], cross_res[0], cross_own, cross_group[:, :, 0], cross_other]
    near = call(
        pack_kernel,
        [(a.shape, a.dtype) for a in small[1:]]
        + [((1, 2 * ties + 2 * OCTET, width), BF16), ((scenes, ties), F32), (own, F32)],
        [pltpu.SMEM((1, scenes), jnp.int32), pltpu.SMEM((1, scenes), F32)]
        + [((2 * OCTET, width), F32), sems((len(small) + 2,))],
        "pack",
        small + [along_count, damping],
        spaces={i: pltpu.HBM for i in range(len(small) + 2)},
    )
    edge, live, damp = pass_on(near[7]), near[8], near[9]
    part_tie = (blocks, ties)
    put = ((rows, slots), BF16)
    pick = ((slots, rows), BF16)
    term = ((blocks, width), F32)
    cjac, ajac, coef, put1, put2, pick1, pick2, t1, t2 = call(
        setup_kernel,
        [(cjac.shape, BF16), (ajac.shape, BF16), ((3,) + part_tie, F32), put, put, pick, pick, term, term],
        [(part_tie, F32)] * 3 + [((OCTET, lanes), jnp.int32), sems((blocks // OCTET,))],
        "setup",
        [cjac, ajac, *near[:7], live],
        work,
        {0: pltpu.HBM, 1: pltpu.HBM},
    )

    def turn(start, count, refs, after):
        outs = [((min(count, j.shape[0]),) + j.shape[1:], BF16) for j in refs]
        share = work * sum(o[0][0] for o in outs) // blocks
        return call(functools.partial(turn_kernel, start), outs, [], "turn", (after,) + refs, share)

    def project(field, turned, refs):
        scratch = [((2, slots, width), F32)] * 2
        kernel = functools.partial(project_kernel, turned)
        return call(kernel, [(pair, F32)], scratch, "project", (field, pick1, pick2) + tuple(refs), work)[0]

    def finish(sums, res=None):
        args = sums if res is None else sums + [res]
        kernel = functools.partial(gather_kernel, scenes, res is None, len(sums))
        field, packet = call(kernel, [(full, F32), ((OCTET, width), F32)], [], "finish", args)
        return field, orbit_packets(packet, res is None)

    sent, coef, ejac = call(
        rhs_kernel,
        [(full, BF16), ((3,) + tie, F32), ((1, 2 * ties, width), BF16)],
        term_space,
        "rhs",
        (coef, t1, t2, edge, put1, put2),
        work // blocks,
    )
    jacs = (cjac, ajac, ejac)
    half = links // 2
    turned = []

    def more(after, done):
        turned.extend([*done, *turn(half, links - half, (cjac,), after)])

    sums = group_sum_but_last(sent, turn(0, half, (cjac,), sent), more)
    res, packets = finish(sums)
    part = project(res, (True, True, False, False), turned + [ajac, ejac])
    fixed = (coef, put1, put2, damp) + jacs
    scratch = [(pair, F32), (tie, F32), (tie, F32)] + term_space + [(full, F32)]
    sent, obs = call(
        functools.partial(step_kernel, 0, scenes),
        [(full, BF16), (pair, F32)],
        scratch,
        "step",
        (part, *packets) + fixed + (res,),
        work,
    )
    turned += turn(0, scenes, (ajac, ejac), sent)
    state = ()
    x = jnp.zeros(own, F32)
    for step in range(1, ITERS):
        field, packets = finish(group_sum_but_last(sent), res)
        part = project(field, (True,) * 4, turned)
        sent, obs, res, image, shadow, direction, x, scal = call(
            functools.partial(step_kernel, step, scenes),
            [(full, BF16), (pair, F32), (full, F32), (full, F32), (pair, F32), (own, F32), (own, F32), ((OCTET, width // 2), F32)],
            scratch,
            "step",
            (part, *packets) + fixed + (res, field, obs, x) + state,
            work,
        )
        state = (image, shadow, direction, scal)
    field, packets = finish(group_sum_but_last(sent), res)
    x, res = call(
        functools.partial(final_kernel, ITERS - 1, scenes),
        [(own, F32), (own, F32)],
        [],
        "final",
        (field, *packets, res, image, direction, x, scal),
    )
    return x[None], res[None]


def solution(mesh):
    placed = (
        P("group", "orbit", None, None, None),
        P("group", "orbit", None, None),
        P("group", "orbit", None, None),
        P("group", "orbit"),
        P("group", "orbit"),
        P("group", "orbit", None, None, None),
        P("group", "orbit", None, None),
        P("group", "orbit", None, None),
        P("group", "orbit"),
        P("group", "orbit", None),
        P("group", "orbit"),
    )
    return jax.shard_map(
        on_device,
        mesh=mesh,
        in_specs=placed,
        out_specs=(P("group", "orbit", None), P("group", "orbit", None)),
        check_vma=False,
    )
```
